128 devices in a mesh: expert: 32 (over x, y, core), tensor: 4 (over z).
Axes of the slice: x: 4, y: 4, z: 4, core: 2. Of those that a mesh axis runs over, the one named last changes fastest.
Arguments:
- tokens: bfloat16 [65536, 512], P(('expert', 'tensor')), may hold values from -6 to 6
- first_gain: float32 [512], replicated, may hold values from 0.5 to 1.5
- second_gain: float32 [512], replicated, may hold values from 0.5 to 1.5
- query_weight: bfloat16 [512, 512], P(None, 'tensor'), may hold values from -0.25 to 0.25
- key_weight: bfloat16 [512, 512], P(None, 'tensor'), may hold values from -0.25 to 0.25
- value_weight: bfloat16 [512, 512], P(None, 'tensor'), may hold values from -0.25 to 0.25
- output_weight: bfloat16 [512, 512], P('tensor'), may hold values from -2 to 2
- router_weight: bfloat16 [512, 32], replicated, may hold values from -0.125 to 0.125
- expert_in: bfloat16 [32, 512, 2048], P('expert', None, 'tensor'), may hold values from -0.5 to 0.5
- expert_out: bfloat16 [32, 2048, 512], P('expert', 'tensor'), may hold values from -0.5 to 0.5
- cotangent: float32 [65536, 512], P(('expert', 'tensor')), may hold values from -6 to 6
- routes: int32 [65536, 4], P(('expert', 'tensor')), may hold values from 0 to 31, all different within a row
- priority: int32 [2048, 32], P(('expert', 'tensor')), may hold values from 0 to 31, each once within a row
- prefix_len: int32 [32], P('expert'), may hold values from 204 to 1024
Outputs:
- layer_output: bfloat16 [65536, 512], P(('expert', 'tensor'))
- tokens_grad: float32 [65536, 512], P(('expert', 'tensor'))
- first_gain_grad: float32 [512], replicated
- second_gain_grad: float32 [512], replicated
- query_grad: float32 [512, 512], P(None, 'tensor')
- key_grad: float32 [512, 512], P(None, 'tensor')
- value_grad: float32 [512, 512], P(None, 'tensor')
- output_grad: float32 [512, 512], P('tensor')
- router_grad: float32 [512, 32], replicated
- expert_in_grad: float32 [32, 512, 2048], P('expert', None, 'tensor')
- expert_out_grad: float32 [32, 2048, 512], P('expert', 'tensor')
The draws below stay inside these ranges and needn't reach their ends.
Inputs may be any that keep to these rules, and one draw needn't show every extreme that they name: `routes`: each row names 4 different experts, and every expert is named by some row. `priority`: each row holds every number of 0 to 31 once.
All inputs are finite; a program needn't handle non-finite values.
Results may differ from the reference program's by a relative error of at most 0.028.
Values may be sent and summed in bfloat16 or wider, within the bound.
A program may use at most 128 MiB of HBM per device.

```python
import jax
import jax.numpy as jnp
from jax import lax

D = 512
HEADS = 8
HEAD_DIM = 64
FF = 2048
GROUP = 32
TOP = 4
TOK_DEV = 512
EXPERTS = 32
SEQ_LEN = 2048
SEQS = 32
TOKENS = 65536
CAP = 5
N_TENSOR = 4


def set_ends(entries, own_key, smallest, largest):
    shape = entries.shape
    place = [jax.random.randint(jax.random.fold_in(own_key, axis), (), 0, shape[axis]) for axis in range(len(shape))]
    entries = entries.at[tuple(place)].set(smallest)
    longest = shape.index(max(shape))
    place[longest] = (place[longest] + 1) % shape[longest]
    return entries.at[tuple(place)].set(largest)


def block_scale(key, extent, pieces, least, largest):
    def one(position, parts):
        draws = jax.random.uniform(jax.random.fold_in(jax.random.fold_in(key, 6), position), (parts,), jnp.float32, least / len(pieces), largest / len(pieces))
        return jnp.repeat(jnp.exp(draws), extent[position] // parts).reshape((-1,) + (1,) * (len(extent) - position - 1))

    gain = one(*pieces[0])
    for cut in pieces[1:]:
        gain = gain * one(*cut)
    return gain


def picks_of(stream_key, rows, number_of, top, lift):
    order = jax.random.permutation(jax.random.fold_in(stream_key, 1), number_of)
    favour = order
    for power in range(3):
        favour = favour * favour // number_of
    favour = favour * lift // number_of
    tickets = jax.random.randint(jax.random.fold_in(stream_key, 2), (rows, number_of), 0, 4096) + favour
    fixed_rows = jax.random.permutation(jax.random.fold_in(stream_key, 3), rows)[jnp.arange(number_of) % rows]
    tickets = jnp.where(jnp.arange(rows)[:, None] == fixed_rows[None, :], 1 << 14, tickets)
    merit = tickets * number_of + jnp.arange(number_of)
    return lax.top_k(merit.astype(jnp.int32), top)[1].astype(jnp.int32)


def normal_values(own_key, shape, spread, limit, pieces=(), kind=jnp.bfloat16):
    entries = spread * jax.random.normal(own_key, shape, jnp.float32)
    if pieces:
        entries = entries * block_scale(own_key, shape, pieces, -0.22, 0.18)
    return jnp.clip(entries, -limit, limit).astype(kind)


def setup_inputs(seed: int = 0) -> dict:
    streams_of = jax.random.split(jax.random.key(seed), 15)
    return {
        "tokens": normal_values(streams_of[0], (TOKENS, D), 1.0, 6.0, ((0, 128),)),
        "first_gain": jnp.clip(1.0 + 0.1 * jax.random.normal(streams_of[1], (D,), jnp.float32), 0.5, 1.5),
        "second_gain": jnp.clip(1.0 + 0.1 * jax.random.normal(streams_of[2], (D,), jnp.float32), 0.5, 1.5),
        "query_weight": normal_values(streams_of[3], (D, D), D ** -0.5, 0.25, ((1, 4),)),
        "key_weight": normal_values(streams_of[4], (D, D), D ** -0.5, 0.25, ((1, 4),)),
        "value_weight": normal_values(streams_of[5], (D, D), D ** -0.5, 0.25, ((1, 4),)),
        "output_weight": normal_values(streams_of[6], (D, D), (D // 64) ** -0.5, 2.0, ((0, 4),)),
        "router_weight": normal_values(streams_of[7], (D, EXPERTS), (4 * D) ** -0.5, 0.125),
        "expert_in": normal_values(streams_of[8], (EXPERTS, D, FF), (D // 4) ** -0.5, 0.5, ((0, 32), (2, 4))),
        "expert_out": normal_values(streams_of[9], (EXPERTS, FF, D), (FF // 16) ** -0.5, 0.5, ((0, 32), (1, 4))),
        "cotangent": normal_values(streams_of[10], (TOKENS, D), 1.0, 6.0, ((0, 128),), jnp.float32),
        "routes": picks_of(streams_of[11], TOKENS, EXPERTS, TOP, 1024),
        "priority": jax.vmap(lambda own: jax.random.permutation(own, GROUP))(jax.random.split(streams_of[12], (TOKENS // GROUP))).reshape((TOKENS // GROUP, GROUP)).astype(jnp.int32),
        "prefix_len": set_ends(jax.random.randint(streams_of[13], (SEQS,), SEQ_LEN // 10, SEQ_LEN // 2 + 1), jax.random.fold_in(streams_of[13], 1), SEQ_LEN // 10, (SEQ_LEN // 2 + 1) - 1).astype(jnp.int32),
    }


@jax.custom_vjp
def low(v):
    return lax.optimization_barrier(v.astype(jnp.bfloat16)).astype(jnp.float32)

@jax.custom_vjp
def low_back(v):
    return v

def low_keep(v):
    return (low(v), None)

def low_pass(kept, grad):
    return (grad,)

def back_keep(v):
    return (v, None)

def back_low(kept, grad):
    return (low(grad),)
low.defvjp(low_keep, low_pass)
low_back.defvjp(back_keep, back_low)
EPS = 1e-05
NEG = -1e+30
HIGHEST = lax.Precision.HIGHEST

def norm_rows(values, gain_vec):
    center = values - lax.optimization_barrier(jnp.mean(values, axis=-1, keepdims=True))
    return center * lax.rsqrt(lax.optimization_barrier(jnp.mean(center * center, axis=-1, keepdims=True)) + EPS) * gain_vec

def attend_block(query_blk, start_row, key_rows, value_rows, prefix):
    block_rows = query_blk.shape[0]
    length = key_rows.shape[0]
    scores = low_back(jnp.einsum('qhd,khd->hqk', query_blk, key_rows, precision=HIGHEST) * HEAD_DIM ** (-0.5))
    row_ids = start_row + jnp.arange(block_rows, dtype=jnp.int32)
    col_ids = jnp.arange(length, dtype=jnp.int32)
    allowed = (col_ids[None, :] <= row_ids[:, None]) | (col_ids[None, :] < prefix)
    scores = jnp.where(allowed[None], scores, NEG)
    soft_rows = low(jax.nn.softmax(scores, axis=-1))
    return jnp.einsum('hqk,khd->qhd', soft_rows, value_rows, precision=HIGHEST)

def sequence_layer(stream, prefix, route_rows, order_rows, first_gain, second_gain, query_weight, key_weight, value_weight, output_weight, router_weight, expert_in, expert_out):
    length = stream.shape[0]
    block_rows = min(512, length)
    normed = low(norm_rows(stream, first_gain))

    def project(weight_mat):
        return low_back(low(jnp.dot(normed, weight_mat, precision=HIGHEST))).reshape(length, HEADS, HEAD_DIM)
    queries = project(query_weight)
    key_rows = project(key_weight)
    value_rows = project(value_weight)
    starts = jnp.arange(length // block_rows, dtype=jnp.int32) * block_rows
    blocks = queries.reshape(length // block_rows, block_rows, HEADS, HEAD_DIM)
    checked = jax.checkpoint(attend_block)

    def run_block(items):
        return checked(items[0], items[1], key_rows, value_rows, prefix)
    context = lax.map(run_block, (blocks, starts)).reshape(length, D)
    context = low_back(low(context))
    attended = low_back(jnp.dot(context, output_weight, precision=HIGHEST))
    residual = stream + attended
    mixer_in = low(norm_rows(residual, second_gain))
    logits = low_back(jnp.dot(mixer_in, router_weight, precision=HIGHEST))
    groups = length // GROUP
    member = lax.optimization_barrier(jnp.sum((route_rows[:, :, None] == jnp.arange(EXPERTS, dtype=jnp.int32)).astype(jnp.float32), axis=1))
    member = member.reshape(groups, GROUP, EXPERTS)
    earlier = (order_rows[:, :, None] < order_rows[:, None, :]).astype(jnp.float32)
    order_rank = jnp.einsum('gst,gse->gte', earlier, member, precision=HIGHEST)
    kept_pairs = member * (order_rank < CAP).astype(jnp.float32)
    exp_terms = kept_pairs * jnp.exp(logits.reshape(groups, GROUP, EXPERTS))
    exp_total = lax.optimization_barrier(jnp.sum(exp_terms, axis=1, keepdims=True))
    kept_count = lax.optimization_barrier(jnp.sum(kept_pairs, axis=1, keepdims=True))
    weights = low(exp_terms / jnp.where(kept_count > 0, exp_total, 1.0))
    grouped = mixer_in.reshape(groups, GROUP, D)
    mixed_rows = low_back(low(jnp.einsum('gte,gtd->egd', weights, grouped, precision=HIGHEST)))
    hidden_pre = low_back(jnp.einsum('egd,edf->egf', mixed_rows, expert_in, precision=HIGHEST))
    hidden = low(jax.nn.silu(hidden_pre))
    returned = low_back(low(jnp.einsum('egf,efd->egd', hidden, expert_out, precision=HIGHEST)))
    mixed_back = low_back(jnp.einsum('gte,egd->gtd', weights, returned, precision=HIGHEST)).reshape(length, D)
    return residual + mixed_back

def reference(tokens, first_gain, second_gain, query_weight, key_weight, value_weight, output_weight, router_weight, expert_in, expert_out, cotangent, routes, priority, prefix_len):
    length = TOK_DEV * N_TENSOR
    streams = tokens.astype(jnp.float32).reshape(SEQS, length, D)
    route_all = routes.reshape(SEQS, length, TOP)
    order_all = priority.reshape(SEQS, length // GROUP, GROUP)
    checked = jax.checkpoint(sequence_layer)

    def whole(stream_all, gain_one, gain_two, query_mat, key_mat, value_mat, output_mat, router_mat, first_mat, second_mat):

        def one_sequence(items):
            return checked(items[0], items[1], items[2], items[3], gain_one, gain_two, query_mat, key_mat, value_mat, output_mat, router_mat, first_mat, second_mat)
        return lax.map(one_sequence, (stream_all, prefix_len, route_all, order_all))
    output, pull = jax.vjp(whole, streams, first_gain.astype(jnp.float32), second_gain.astype(jnp.float32), query_weight.astype(jnp.float32), key_weight.astype(jnp.float32), value_weight.astype(jnp.float32), output_weight.astype(jnp.float32), router_weight.astype(jnp.float32), expert_in.astype(jnp.float32), expert_out.astype(jnp.float32))
    grads = pull(cotangent.astype(jnp.float32).reshape(SEQS, length, D))
    return (output.reshape(TOKENS, D).astype(jnp.bfloat16), grads[0].reshape(TOKENS, D), grads[1], grads[2], grads[3], grads[4], grads[5], grads[6], grads[7], grads[8], grads[9])
```

```python
import functools
import math

import jax
import jax.numpy as jnp
from jax import lax
from jax.experimental import pallas as pl
from jax.experimental.pallas import tpu as pltpu
from jax.sharding import PartitionSpec as P

HEAD_DIM = 64
GROUP = 32
TOP = 4
EPS = 1e-05
NEG = -1e30
SCORE_SCALE = HEAD_DIM**-0.5
SCORE_LOG2 = SCORE_SCALE * math.log2(math.e)
MESH = pl.DeviceIdType.MESH
VM = pl.BlockSpec(memory_space=pltpu.VMEM)
SM = pl.BlockSpec(memory_space=pltpu.SMEM)
TENSOR = 4
VMEM_BYTES = 48 << 20
BF16 = jnp.bfloat16
F32 = jnp.float32


def dotf(left, right, dims=((1,), (0,)), precision=None):
    return lax.dot_general(
        left, right, (dims, ((), ())), preferred_element_type=F32, precision=precision
    )


def iota(shape, axis):
    return lax.broadcasted_iota(jnp.int32, shape, axis)


def norm_parts(values):
    center = values - jnp.mean(values, axis=1, keepdims=True)
    spread = lax.rsqrt(jnp.mean(center * center, axis=1, keepdims=True) + EPS)
    return center * spread, spread


def remote(src, dst, send_sem, recv_sem, axis, to):
    return pltpu.make_async_remote_copy(
        src_ref=src,
        dst_ref=dst,
        send_sem=send_sem,
        recv_sem=recv_sem,
        device_id={axis: to},
        device_id_type=MESH,
    )


def greet(axis, size):
    barrier = pltpu.get_barrier_semaphore()
    me = lax.axis_index(axis)

    def one(off, _):
        pl.semaphore_signal(
            barrier, inc=1, device_id={axis: lax.rem(me + off, size)}, device_id_type=MESH
        )
        return 0

    lax.fori_loop(1, size, one, 0)


def project_kernel(
    tok_ref,
    gain_ref,
    wq_ref,
    wk_ref,
    wv_ref,
    routes_ref,
    prio_ref,
    seq_ref,
    q_ref,
    k_ref,
    v_ref,
    kept_ref,
    w_s,
    send_sem,
    recv_sem,
    *,
    experts,
    capacity,
):
    place = lax.axis_index("tensor")
    right, left = lax.rem(place + 1, TENSOR), lax.rem(place + TENSOR - 1, TENSOR)
    far = lax.rem(place + 2, TENSOR)
    barrier = pltpu.get_barrier_semaphore()
    for neighbour in (right, left):
        pl.semaphore_signal(
            barrier, inc=1, device_id={"tensor": neighbour}, device_id_type=MESH
        )
    rows, width = tok_ref.shape
    half = rows // 2

    def start_of(owner, part):
        return pl.multiple_of(owner * rows + part * half, half)

    def send(slot, owner, part, to):
        block = seq_ref.at[pl.ds(start_of(owner, part), half), :]
        return remote(block, block, send_sem.at[slot], recv_sem.at[slot], "tensor", to)

    for part in range(2):
        scaled, _ = norm_parts(tok_ref[part * half : (part + 1) * half, :].astype(F32))
        seq_ref[pl.ds(start_of(place, part), half), :] = (scaled * gain_ref[...]).astype(BF16)
    pl.semaphore_wait(barrier, 2)
    right_low, left_high = send(0, place, 0, right), send(1, place, 1, left)
    right_high, left_low = send(2, place, 1, right), send(3, place, 0, left)
    for copy in (right_low, left_high, right_high, left_low):
        copy.start()
    head_cols = wq_ref.shape[1]
    w_s[:, 0:head_cols] = wq_ref[...]
    w_s[:, head_cols : 2 * head_cols] = wk_ref[...]
    w_s[:, 2 * head_cols : 3 * head_cols] = wv_ref[...]

    def project(owner, part):
        start = start_of(owner, part)
        out = dotf(seq_ref[pl.ds(start, half), :], w_s[...]).astype(BF16)
        q_ref[pl.ds(start, half), :] = out[:, 0:head_cols]
        k_ref[pl.ds(start, half), :] = out[:, head_cols : 2 * head_cols]
        v_ref[pl.ds(start, half), :] = out[:, 2 * head_cols : 3 * head_cols]

    project(place, 0)
    project(place, 1)
    right_low.wait_recv()
    right_on = send(4, left, 0, right)
    right_on.start()
    left_high.wait_recv()
    left_on = send(5, right, 1, left)
    left_on.start()

    groups, size = prio_ref.shape
    wide = experts * groups
    prio = prio_ref[...].astype(F32).astype(BF16)
    tok_group = (iota((rows, groups), 0) // size) == iota((rows, groups), 1)
    spread_rows = dotf(jnp.where(tok_group, 1.0, 0.0).astype(BF16), prio)
    at_col = (iota((rows, size), 0) % size) == iota((rows, size), 1)
    prio_col = jnp.sum(jnp.where(at_col, spread_rows, 0.0), axis=1, keepdims=True)
    group_tok = (iota((groups, rows), 1) // size) == iota((groups, rows), 0)
    spread_cols = dotf(prio, jnp.where(group_tok, 1.0, 0.0).astype(BF16), ((0,), (0,)))
    at_row = (iota((size, rows), 1) % size) == iota((size, rows), 0)
    prio_row = jnp.sum(jnp.where(at_row, spread_cols, 0.0), axis=0, keepdims=True)
    col = iota((rows, wide), 1)
    own_group = (iota((rows, wide), 0) // size) == (col % groups)
    col_expert = col // groups
    named = routes_ref[:, 0:1] == col_expert
    for pick in range(1, TOP):
        named = named | (routes_ref[:, pick : pick + 1] == col_expert)
    member = jnp.where(named & own_group, 1.0, 0.0)
    earlier = jnp.where(prio_row < prio_col, 1.0, 0.0).astype(BF16)
    rank = dotf(earlier, member.astype(BF16))
    kept_ref[...] = jnp.where(rank < capacity, member, 0.0).astype(BF16)

    right_high.wait_recv()
    project(left, 0)
    project(left, 1)
    left_low.wait_recv()
    project(right, 0)
    project(right, 1)
    right_on.wait_recv()
    project(far, 0)
    left_on.wait_recv()
    project(far, 1)
    for copy in (right_low, left_high, right_high, left_low, right_on, left_on):
        copy.wait_send()


def project_rows(tokens, gain, wq, wk, wv, routes, priority, experts, capacity):
    rows, width = tokens.shape
    head_cols = wq.shape[1]
    heads = jax.ShapeDtypeStruct((TENSOR * rows, head_cols), BF16)
    return pl.pallas_call(
        functools.partial(project_kernel, experts=experts, capacity=float(capacity)),
        out_shape=(
            jax.ShapeDtypeStruct((TENSOR * rows, width), BF16),
            heads,
            heads,
            heads,
            jax.ShapeDtypeStruct((rows, experts * priority.shape[0]), BF16),
        ),
        in_specs=[VM] * 7,
        out_specs=(VM,) * 5,
        scratch_shapes=[
            pltpu.VMEM((width, 3 * head_cols), BF16),
            pltpu.SemaphoreType.DMA((6,)),
            pltpu.SemaphoreType.DMA((6,)),
        ],
        compiler_params=pltpu.CompilerParams(
            collective_id=0, has_side_effects=True, vmem_limit_bytes=VMEM_BYTES
        ),
        name="project",
    )(tokens, gain, wq, wk, wv, routes, priority)


def pick_head(values, head):
    lane = iota(values.shape, 1)
    inside = (lane >= head * HEAD_DIM) & (lane < (head + 1) * HEAD_DIM)
    return jnp.where(inside, values, jnp.zeros_like(values))


def attend_kernel(bq, bk, prefix_ref, q_ref, k_ref, v_ref, ctx_ref, lse_ref):
    length, cols = q_ref.shape
    heads = cols // HEAD_DIM
    prefix = prefix_ref[0]

    @pl.loop(0, length // bq)
    def _(blk):
        row0 = pl.multiple_of(blk * bq, bq)
        q = q_ref[pl.ds(row0, bq), :]
        q_heads = [pick_head(q, head) for head in range(heads)]
        n_full = jnp.maximum(prefix // bk, (row0 + 1) // bk)
        n_seen = jnp.maximum((prefix + bk - 1) // bk, (row0 + bq + bk - 1) // bk)

        def step(kb, carry, masked):
            col0 = pl.multiple_of(kb * bk, bk)
            keys = k_ref[pl.ds(col0, bk), :]
            vals = v_ref[pl.ds(col0, bk), :]
            out = []
            if masked:
                row_ids = iota((bq, bk), 0) + row0
                col_ids = iota((bq, bk), 1) + col0
                seen = (col_ids <= row_ids) | (col_ids < prefix)
            for head in range(heads):
                peak, total, acc = carry[3 * head : 3 * head + 3]
                scores = dotf(q_heads[head], keys, ((1,), (1,)))
                if masked:
                    scores = jnp.where(seen, scores, NEG)
                new_peak = jnp.maximum(peak, jnp.max(scores, axis=1, keepdims=True))
                soft = jnp.exp2((scores - new_peak) * SCORE_LOG2)
                shrink = jnp.exp2((peak - new_peak) * SCORE_LOG2)
                total = shrink * total + jnp.sum(soft, axis=1, keepdims=True)
                acc = shrink * acc + dotf(soft.astype(BF16), vals)
                out += [new_peak, total, acc]
            return tuple(out)

        init = (
            jnp.full((bq, 1), NEG, F32),
            jnp.zeros((bq, 1), F32),
            jnp.zeros((bq, cols), F32),
        ) * heads
        carry = lax.fori_loop(0, n_full, functools.partial(step, masked=False), init)
        carry = lax.fori_loop(n_full, n_seen, functools.partial(step, masked=True), carry)
        merged = jnp.zeros((bq, cols), F32)
        for head in range(heads):
            peak, total, acc = carry[3 * head : 3 * head + 3]
            merged = merged + pick_head(acc * (1.0 / total), head)
            lse = peak * SCORE_LOG2 + jnp.log2(total)
            lse_ref[pl.ds(8 * head, 8), pl.ds(row0, bq)] = jnp.transpose(
                jnp.broadcast_to(lse, (bq, 128))
            )[:8]
        ctx_ref[pl.ds(row0, bq), :] = merged.astype(BF16)


def attend(q, k, v, prefix):
    length, cols = q.shape
    heads = cols // HEAD_DIM
    block = min(512, length)
    return pl.pallas_call(
        functools.partial(attend_kernel, block, block),
        out_shape=(
            jax.ShapeDtypeStruct((length, cols), BF16),
            jax.ShapeDtypeStruct((8 * heads, length), F32),
        ),
        in_specs=[SM, VM, VM, VM],
        out_specs=(VM, VM),
        compiler_params=pltpu.CompilerParams(vmem_limit_bytes=VMEM_BYTES),
        name="attend",
    )(prefix, q, k, v)


def attend_back_kernel(
    bq,
    bk,
    prefix_ref,
    q_ref,
    k_ref,
    v_ref,
    grad_ref,
    ctx_ref,
    lse_ref,
    dq_ref,
    dk_ref,
    dv_ref,
    dq_acc,
    dk_acc,
    dv_acc,
    inner,
):
    length, cols = q_ref.shape
    heads = cols // HEAD_DIM
    prefix = prefix_ref[0]
    dq_acc[...] = jnp.zeros_like(dq_acc)
    ones = [pick_head(jnp.ones((8, cols), F32), head) for head in range(heads)]

    @pl.loop(0, length // bq)
    def _(blk):
        rows = pl.ds(pl.multiple_of(blk * bq, bq), bq)
        product = grad_ref[rows, :].astype(F32) * ctx_ref[rows, :].astype(F32)
        for head in range(heads):
            inner[pl.ds(8 * head, 8), rows] = dotf(
                ones[head], product, ((1,), (1,)), lax.Precision.HIGHEST
            )

    @pl.loop(0, length // bk)
    def _(kb):
        col0 = pl.multiple_of(kb * bk, bk)
        keys = k_ref[pl.ds(col0, bk), :]
        vals = v_ref[pl.ds(col0, bk), :]
        key_heads = [pick_head(keys, head) for head in range(heads)]
        dk_acc[...] = jnp.zeros_like(dk_acc)
        dv_acc[...] = jnp.zeros_like(dv_acc)
        first = jnp.where(col0 < prefix, 0, col0 // bq)
        full = jnp.where(col0 + bk <= prefix, 0, (col0 + bk + bq - 2) // bq)
        full = jnp.maximum(first, full)

        def step(blk, _, masked):
            row0 = pl.multiple_of(blk * bq, bq)
            rows = pl.ds(row0, bq)
            q = q_ref[rows, :]
            grad = grad_ref[rows, :]
            if masked:
                key_ids = iota((bk, bq), 0) + col0
                row_ids = iota((bk, bq), 1) + row0
                seen = (key_ids <= row_ids) | (key_ids < prefix)
            dq = dq_acc[rows, :]
            dk = dk_acc[...]
            dv = dv_acc[...]
            for head in range(heads):
                q_head = pick_head(q, head)
                grad_head = pick_head(grad, head)
                soft = jnp.exp2(
                    dotf(keys, q_head, ((1,), (1,))) * SCORE_LOG2 - lse_ref[pl.ds(8 * head, 1), rows]
                )
                if masked:
                    soft = jnp.where(seen, soft, 0.0)
                grad_soft = dotf(vals, grad_head, ((1,), (1,)))
                grad_scores = (soft * (grad_soft - inner[pl.ds(8 * head, 1), rows])).astype(BF16)
                dv += dotf(soft.astype(BF16), grad_head)
                dk += dotf(grad_scores, q_head)
                dq += dotf(grad_scores, key_heads[head], ((0,), (0,)))
            dq_acc[rows, :] = dq
            dk_acc[...] = dk
            dv_acc[...] = dv
            return 0

        lax.fori_loop(first, full, functools.partial(step, masked=True), 0)
        lax.fori_loop(full, length // bq, functools.partial(step, masked=False), 0)
        dk_ref[pl.ds(col0, bk), :] = (dk_acc[...] * SCORE_SCALE).astype(BF16)
        dv_ref[pl.ds(col0, bk), :] = dv_acc[...].astype(BF16)

    dq_ref[...] = (dq_acc[...] * SCORE_SCALE).astype(BF16)


def attend_back(q, k, v, grad, ctx, lse, prefix):
    length, cols = q.shape
    block = min(512, length)
    out = jax.ShapeDtypeStruct((length, cols), BF16)
    return pl.pallas_call(
        functools.partial(attend_back_kernel, block, block),
        out_shape=(out, out, out),
        in_specs=[SM] + [VM] * 6,
        out_specs=(VM, VM, VM),
        scratch_shapes=[
            pltpu.VMEM((length, cols), F32),
            pltpu.VMEM((block, cols), F32),
            pltpu.VMEM((block, cols), F32),
            pltpu.VMEM(lse.shape, F32),
        ],
        compiler_params=pltpu.CompilerParams(vmem_limit_bytes=VMEM_BYTES),
        name="attend_back",
    )(prefix, q, k, v, grad, ctx, lse)


def middle_kernel(
    ctx_ref,
    tok_ref,
    gain_ref,
    wo_ref,
    router_ref,
    kept_ref,
    cot_ref,
    win_ref,
    wout_ref,
    out_ref,
    gres_ref,
    gctx_ref,
    dwin_ref,
    dwout_ref,
    dwo_ref,
    drouter_ref,
    dgain_ref,
    ctx_s,
    wide_router,
    res_s,
    scaled_s,
    spread_s,
    mixer_s,
    gmix_s,
    weight_s,
    low_s,
    out_s,
    in_s,
    done_s,
    ret_s,
    hidden_s,
    gpre_s,
    gctx_s,
    glog_s,
    gatt_s,
    ctx_sems,
    mix_sems,
    ret_sems,
    back_sems,
    *,
    experts,
):
    rows, width = tok_ref.shape
    place = lax.axis_index("tensor")
    me = lax.axis_index("expert")
    groups = rows // GROUP
    wide = experts * groups
    hcols = ctx_ref.shape[1]
    step_rows = 128
    steps = rows // step_rows
    peers = experts
    barrier = pltpu.get_barrier_semaphore()
    greet("tensor", TENSOR)
    greet("expert", peers)
    pl.semaphore_wait(barrier, TENSOR - 1 + peers - 1)

    def ctx_copy(off):
        to = lax.rem(place + off, TENSOR)
        block = ctx_ref.at[pl.ds(pl.multiple_of(to * rows, rows), rows), :]
        return remote(
            block, ctx_s.at[place], ctx_sems.at[0, off], ctx_sems.at[1, off], "tensor", to
        )

    ctx_copies = [ctx_copy(off) for off in (2, 1, 3)]
    for copy in ctx_copies:
        copy.start()
    ctx_s[place] = ctx_ref[pl.ds(pl.multiple_of(place * rows, rows), rows), :]
    to_wide = jnp.where(iota((experts, wide), 0) == iota((experts, wide), 1) // groups, 1.0, 0.0)
    to_wide = to_wide.astype(BF16)
    wide_router[...] = dotf(router_ref[...], to_wide).astype(BF16)
    gmix_s[...] = cot_ref[...].astype(BF16)
    for copy in ctx_copies:
        copy.wait_recv()

    @pl.loop(0, steps)
    def _(step):
        part = pl.ds(pl.multiple_of(step * step_rows, step_rows), step_rows)
        ctx = jnp.concatenate([ctx_s[at, part, :] for at in range(TENSOR)], axis=1)
        residual = tok_ref[part, :].astype(F32) + dotf(ctx, wo_ref[...])
        res_s[part, :] = residual
        scaled, spread = norm_parts(residual)
        scaled_s[part, :] = scaled
        spread_s[part, :] = jnp.broadcast_to(spread, (step_rows, 128))
        mixer = (scaled * gain_ref[...]).astype(BF16)
        mixer_s[part, :] = mixer
        logits = dotf(mixer, wide_router[...])
        kept = kept_ref[part, :].astype(F32)
        terms = jnp.where(kept > 0.0, jnp.exp(logits), 0.0)
        total = jnp.sum(terms, axis=0, keepdims=True)
        count = jnp.sum(kept, axis=0, keepdims=True)
        weight = terms / jnp.where(count > 0.0, total, 1.0)
        weight_s[part, :] = weight
        low_s[part, :] = weight.astype(BF16)

    def mix_to(src_ref, kind):
        @pl.loop(0, wide // 128)
        def _(blk):
            cols = pl.ds(pl.multiple_of(blk * 128, 128), 128)
            mixed = dotf(low_s[:, cols], src_ref[...], ((0,), (0,))).astype(BF16)
            count = 128 // groups
            out_s[pl.ds(blk * count, count), kind] = mixed.reshape(count, groups, width)

    mix_to(mixer_s, 0)
    mix_to(gmix_s, 1)

    def mix_copy(off):
        to = lax.rem(me + off, peers)
        return remote(
            out_s.at[to], in_s.at[off], mix_sems.at[0, off], mix_sems.at[1, off], "expert", to
        )

    def start_mix(off, _):
        mix_copy(off).start()
        return 0

    lax.fori_loop(1, peers, start_mix, 0)
    in_s[0] = out_s[me]

    def ret_copy(off):
        to = lax.rem(me + peers - off, peers)
        return remote(
            done_s.at[off], ret_s.at[me], ret_sems.at[0, off], ret_sems.at[1, off], "expert", to
        )

    batch = 128 // groups
    slices, _, fcols = win_ref.shape

    @pl.loop(0, peers // batch)
    def _(chunk):
        def wait_mix(off, _):
            mix_copy(off).wait_recv()
            return 0

        begin = chunk * batch
        lax.fori_loop(jnp.maximum(begin, 1), begin + batch, wait_mix, 0)
        slots = pl.ds(begin, batch)
        part = pl.ds(pl.multiple_of(chunk * 128, 128), 128)
        mixed = in_s[slots, 0].reshape(128, width)
        grad = in_s[slots, 1].reshape(128, width)

        def one_slice(at, carry):
            returned, grad_mixed = carry
            pre = dotf(mixed, win_ref[at])
            sigma = 1.0 / (1.0 + jnp.exp(-pre))
            hidden = (pre * sigma).astype(BF16)
            grad_hidden = dotf(grad, wout_ref[at], ((1,), (1,)))
            grad_pre = (grad_hidden * (sigma * (1.0 + pre * (1.0 - sigma)))).astype(BF16)
            hidden_s[at, part, :] = hidden
            gpre_s[at, part, :] = grad_pre
            returned = returned + dotf(hidden, wout_ref[at])
            grad_mixed = grad_mixed + dotf(grad_pre, win_ref[at], ((1,), (1,)))
            return returned, grad_mixed

        zero = jnp.zeros((128, width), F32)
        returned, grad_mixed = lax.fori_loop(0, slices, one_slice, (zero, zero))
        done_s[slots, 0] = returned.astype(BF16).reshape(batch, groups, width)
        done_s[slots, 1] = grad_mixed.astype(BF16).reshape(batch, groups, width)

        def start_ret(off, _):
            ret_copy(off).start()
            return 0

        lax.fori_loop(jnp.maximum(begin, 1), begin + batch, start_ret, 0)

    ret_s[me] = done_s[0]

    @pl.loop(0, slices)
    def _(at):
        mixed = in_s[:, 0].reshape(wide, width)
        grad = in_s[:, 1].reshape(wide, width)
        dwin_ref[at] = dotf(mixed, gpre_s[at], ((0,), (0,))).astype(BF16)
        dwout_ref[at] = dotf(hidden_s[at], grad, ((0,), (0,))).astype(BF16)

    def wait_ret(off, _):
        ret_copy(off).wait_recv()
        return 0

    lax.fori_loop(1, peers, wait_ret, 0)

    dgain_ref[...] = jnp.zeros_like(dgain_ref)
    from_wide = jnp.where(iota((wide, experts), 0) // groups == iota((wide, experts), 1), 1.0, 0.0)
    from_wide = from_wide.astype(BF16)

    @pl.loop(0, steps)
    def _(step):
        part = pl.ds(pl.multiple_of(step * step_rows, step_rows), step_rows)
        returned = ret_s[:, 0].reshape(wide, width)
        grad_mixed = ret_s[:, 1].reshape(wide, width)
        low = low_s[part, :]
        weight = weight_s[part, :]
        mixer = mixer_s[part, :]
        out_ref[part, :] = (res_s[part, :] + dotf(low, returned)).astype(BF16)
        grad_weight = dotf(gmix_s[part, :], returned, ((1,), (1,)))
        grad_weight = grad_weight + dotf(mixer, grad_mixed, ((1,), (1,)))
        inner = jnp.sum(weight * grad_weight, axis=0, keepdims=True)
        grad_logits = (weight * (grad_weight - inner)).astype(BF16)
        glog_s[part, :] = dotf(grad_logits, from_wide).astype(BF16)
        grad_mixer = dotf(low, grad_mixed) + dotf(grad_logits, wide_router[...], ((1,), (1,)))
        scaled = scaled_s[part, :]
        dgain_ref[...] += jnp.sum(grad_mixer * scaled, axis=0, keepdims=True)
        grad_scaled = grad_mixer * gain_ref[...]
        centered = grad_scaled - jnp.mean(grad_scaled, axis=1, keepdims=True)
        along = jnp.mean(grad_scaled * scaled, axis=1, keepdims=True)
        grad_res = cot_ref[part, :] + spread_s[part, 0:1] * (centered - scaled * along)
        gres_ref[part, :] = grad_res
        grad_att = grad_res.astype(BF16)
        gatt_s[part, :] = grad_att
        grad_ctx = dotf(grad_att, wo_ref[...], ((1,), (1,))).astype(BF16)
        for at in range(TENSOR):
            gctx_s[at, part, :] = grad_ctx[:, at * hcols : (at + 1) * hcols]

    def back_copy(off):
        to = lax.rem(place + off, TENSOR)
        block = gctx_ref.at[pl.ds(pl.multiple_of(place * rows, rows), rows), :]
        return remote(
            gctx_s.at[to], block, back_sems.at[0, off], back_sems.at[1, off], "tensor", to
        )

    back_copies = [back_copy(off) for off in (2, 1, 3)]
    for copy in back_copies:
        copy.start()
    gctx_ref[pl.ds(pl.multiple_of(place * rows, rows), rows), :] = gctx_s[place]
    for at in range(TENSOR):
        dwo_ref[at] = dotf(ctx_s[at], gatt_s[...], ((0,), (0,))).astype(BF16)
    drouter_ref[...] = dotf(glog_s[...], mixer_s[...], ((0,), (0,)))

    def wait_sent(off, _):
        mix_copy(off).wait_send()
        ret_copy(off).wait_send()
        return 0

    lax.fori_loop(1, peers, wait_sent, 0)
    for copy in back_copies:
        copy.wait_recv()
    for copy in ctx_copies + back_copies:
        copy.wait_send()


def middle(ctx, tokens, gain, wo, router, kept, cot, win, wout):
    rows, width = tokens.shape
    experts = router.shape[1]
    groups = rows // GROUP
    wide = experts * groups
    slices, _, fcols = win.shape
    hcols = ctx.shape[1]

    def dev(shape, kind):
        return jax.ShapeDtypeStruct(shape, kind)

    return pl.pallas_call(
        functools.partial(middle_kernel, experts=experts),
        out_shape=(
            dev((rows, width), BF16),
            dev((rows, width), F32),
            dev(ctx.shape, BF16),
            dev((slices, width, fcols), BF16),
            dev((slices, fcols, width), BF16),
            dev((TENSOR, hcols, width), BF16),
            dev((experts, width), F32),
            dev((1, width), F32),
        ),
        in_specs=[VM] * 9,
        out_specs=(VM,) * 8,
        scratch_shapes=[
            pltpu.VMEM((TENSOR, rows, hcols), BF16),
            pltpu.VMEM((width, wide), BF16),
            pltpu.VMEM((rows, width), F32),
            pltpu.VMEM((rows, width), F32),
            pltpu.VMEM((rows, 128), F32),
            pltpu.VMEM((rows, width), BF16),
            pltpu.VMEM((rows, width), BF16),
            pltpu.VMEM((rows, wide), F32),
            pltpu.VMEM((rows, wide), BF16),
            pltpu.VMEM((experts, 2, groups, width), BF16),
            pltpu.VMEM((experts, 2, groups, width), BF16),
            pltpu.VMEM((experts, 2, groups, width), BF16),
            pltpu.VMEM((experts, 2, groups, width), BF16),
            pltpu.VMEM((slices, wide, fcols), BF16),
            pltpu.VMEM((slices, wide, fcols), BF16),
            pltpu.VMEM((TENSOR, rows, hcols), BF16),
            pltpu.VMEM((rows, experts), BF16),
            pltpu.VMEM((rows, width), BF16),
            pltpu.SemaphoreType.DMA((2, TENSOR)),
            pltpu.SemaphoreType.DMA((2, experts)),
            pltpu.SemaphoreType.DMA((2, experts)),
            pltpu.SemaphoreType.DMA((2, TENSOR)),
        ],
        compiler_params=pltpu.CompilerParams(
            collective_id=1, has_side_effects=True, vmem_limit_bytes=VMEM_BYTES
        ),
        name="middle",
    )(ctx, tokens, gain, wo, router, kept, cot, win, wout)


def last_kernel(
    seq_ref,
    dq_ref,
    dk_ref,
    dv_ref,
    wq_ref,
    wk_ref,
    wv_ref,
    tok_ref,
    gain_ref,
    gres_ref,
    dwo_ref,
    drouter_ref,
    dgain_ref,
    gtok_ref,
    gq_ref,
    gk_ref,
    gv_ref,
    go_ref,
    small_ref,
    w_s,
    part_s,
    land_s,
    low_s,
    piece_s,
    gather_s,
    sum_s,
    all_s,
    small_s,
    row_sems,
    piece_sems,
    sum_sems,
    small_sems,
):
    rows, width = tok_ref.shape
    half = rows // 2
    hcols = wq_ref.shape[1]
    place = lax.axis_index("tensor")
    me = lax.axis_index("expert")
    peers = gather_s.shape[0]
    right, left = lax.rem(place + 1, TENSOR), lax.rem(place + TENSOR - 1, TENSOR)
    far = lax.rem(place + 2, TENSOR)
    barrier = pltpu.get_barrier_semaphore()
    greet("tensor", TENSOR)
    greet("expert", peers)
    w_s[:, 0:hcols] = wq_ref[...]
    w_s[:, hcols : 2 * hcols] = wk_ref[...]
    w_s[:, 2 * hcols : 3 * hcols] = wv_ref[...]

    def heads_grad(start, count):
        part = pl.ds(pl.multiple_of(start, count), count)
        return jnp.concatenate([dq_ref[part, :], dk_ref[part, :], dv_ref[part, :]], axis=1)

    def partial_rows(owner, piece):
        return dotf(heads_grad(owner * rows + piece * half, half), w_s[...], ((1,), (1,)))

    low, high = pl.ds(0, half), pl.ds(half, half)
    low_s[0, low, :] = partial_rows(far, 0).astype(BF16)
    low_s[1, high, :] = partial_rows(far, 1).astype(BF16)
    pl.semaphore_wait(barrier, TENSOR - 1 + peers - 1)

    def row_copy(slot, src, part, to):
        return remote(
            low_s.at[src, part, :],
            land_s.at[slot // 2, part, :],
            row_sems.at[0, slot],
            row_sems.at[1, slot],
            "tensor",
            to,
        )

    far_low = row_copy(0, 0, low, right)
    far_high = row_copy(1, 1, high, left)
    far_low.start()
    far_high.start()
    low_s[2, high, :] = partial_rows(right, 1).astype(BF16)
    right_high = row_copy(2, 2, high, right)
    right_high.start()
    low_s[3, low, :] = partial_rows(left, 0).astype(BF16)
    left_low = row_copy(4, 3, low, left)
    left_low.start()
    part_s[low, :] = partial_rows(right, 0)
    part_s[high, :] = partial_rows(left, 1)

    def grads_of(at, acc):
        part = pl.ds(pl.multiple_of(at * rows, rows), rows)
        return acc + dotf(seq_ref[part, :], heads_grad(at * rows, rows), ((0,), (0,)))

    grads = lax.fori_loop(0, TENSOR, grads_of, jnp.zeros((width, 3 * hcols), F32))
    for at in range(3):
        piece_s[:, at] = (
            grads[:, at * hcols : (at + 1) * hcols].astype(BF16).reshape(peers, width // peers, hcols)
        )
    blocks = width // hcols
    dwo = dwo_ref[...]
    piece_s[:, 3] = jnp.concatenate(
        [dwo[:, at * hcols : (at + 1) * hcols] for at in range(blocks)], axis=0
    ).reshape(peers, width // peers, hcols)
    ones = jnp.ones((8, 3 * hcols), F32)
    dfirst = dotf(ones, grads * w_s[...].astype(F32), ((1,), (1,)), lax.Precision.HIGHEST)
    dfirst = dfirst[0:1] / gain_ref[...]
    experts = drouter_ref.shape[0]
    small_rows = jnp.concatenate(
        [drouter_ref[...], dfirst, dgain_ref[...], jnp.zeros((width // blocks - experts - 2, width), F32)],
        axis=0,
    ).astype(BF16)
    piece_s[:, 4] = jnp.concatenate(
        [small_rows[:, at * hcols : (at + 1) * hcols] for at in range(blocks)], axis=0
    ).reshape(peers, width // peers, hcols)

    def piece_copy(off):
        to = lax.rem(me + off, peers)
        return remote(
            piece_s.at[to], gather_s.at[off], piece_sems.at[0, off], piece_sems.at[1, off], "expert", to
        )

    def start_piece(off, _):
        piece_copy(off).start()
        return 0

    lax.fori_loop(1, peers, start_piece, 0)
    gather_s[0] = piece_s[me]

    far_low.wait_recv()
    low_s[2, low, :] = (part_s[low, :] + land_s[0, low, :].astype(F32)).astype(BF16)
    right_low = row_copy(3, 2, low, right)
    right_low.start()
    far_high.wait_recv()
    low_s[3, high, :] = (part_s[high, :] + land_s[0, high, :].astype(F32)).astype(BF16)
    left_high = row_copy(5, 3, high, left)
    left_high.start()
    part_s[low, :] = partial_rows(place, 0)
    part_s[high, :] = partial_rows(place, 1)

    def wait_piece(off, _):
        piece_copy(off).wait_recv()
        return 0

    lax.fori_loop(1, peers, wait_piece, 0)

    def add_up(off, acc):
        return acc + gather_s[off].astype(F32)

    sum_s[...] = lax.fori_loop(0, peers, add_up, jnp.zeros(sum_s.shape, F32)).astype(BF16)

    def sum_copy(off):
        to = lax.rem(me + off, peers)
        return remote(sum_s, all_s.at[me], sum_sems.at[0, off], sum_sems.at[1, off], "expert", to)

    def start_sum(off, _):
        sum_copy(off).start()
        return 0

    lax.fori_loop(1, peers, start_sum, 0)
    all_s[me] = sum_s[...]

    for copy in (right_high, right_low, left_low, left_high):
        copy.wait_recv()
    for part in (low, high):
        grad_normed = part_s[part, :] + land_s[1, part, :].astype(F32) + land_s[2, part, :].astype(F32)
        scaled, spread = norm_parts(tok_ref[part, :].astype(F32))
        grad_scaled = grad_normed * gain_ref[...]
        centered = grad_scaled - jnp.mean(grad_scaled, axis=1, keepdims=True)
        along = jnp.mean(grad_scaled * scaled, axis=1, keepdims=True)
        gtok_ref[part, :] = gres_ref[part, :] + spread * (centered - scaled * along)

    def wait_sum(off, _):
        sum_copy(off).wait_recv()
        return 0

    lax.fori_loop(1, peers, wait_sum, 0)
    small = all_s[:, 4].reshape(width, hcols)
    each = width // blocks
    small_s[place] = jnp.concatenate(
        [small[at * each : at * each + small_s.shape[1]] for at in range(blocks)], axis=1
    ).astype(F32)

    def small_copy(off):
        to = lax.rem(place + off, TENSOR)
        return remote(
            small_s.at[place], small_s.at[place], small_sems.at[0, off], small_sems.at[1, off], "tensor", to
        )

    small_copies = [small_copy(off) for off in (2, 1, 3)]
    for copy in small_copies:
        copy.start()
    for at, out_ref in enumerate((gq_ref, gk_ref, gv_ref)):
        out_ref[...] = all_s[:, at].reshape(width, hcols).astype(F32)
    out_grad = all_s[:, 3].reshape(width, hcols).astype(F32)
    for at in range(blocks):
        go_ref[:, at * hcols : (at + 1) * hcols] = out_grad[at * each : (at + 1) * each]
    for copy in (far_low, far_high, right_high, right_low, left_low, left_high):
        copy.wait_send()

    def wait_sent(off, _):
        piece_copy(off).wait_send()
        sum_copy(off).wait_send()
        return 0

    lax.fori_loop(1, peers, wait_sent, 0)
    for copy in small_copies:
        copy.wait_recv()
    small_ref[...] = small_s[0] + small_s[1] + small_s[2] + small_s[3]
    for copy in small_copies:
        copy.wait_send()


def last(seq, dq, dk, dv, wq, wk, wv, tokens, gain, gres, dwo, drouter, dgain, peers):
    rows, width = tokens.shape
    hcols = wq.shape[1]
    experts = drouter.shape[0]
    small_rows = (experts + 2 + 15) // 16 * 16

    def dev(shape, kind):
        return jax.ShapeDtypeStruct(shape, kind)

    piece = (5, width // peers, hcols)
    return pl.pallas_call(
        last_kernel,
        out_shape=(
            dev((rows, width), F32),
            dev(wq.shape, F32),
            dev(wq.shape, F32),
            dev(wq.shape, F32),
            dev((hcols, width), F32),
            dev((small_rows, width), F32),
        ),
        in_specs=[VM] * 13,
        out_specs=(VM,) * 6,
        scratch_shapes=[
            pltpu.VMEM((width, 3 * hcols), BF16),
            pltpu.VMEM((rows, width), F32),
            pltpu.VMEM((3, rows, width), BF16),
            pltpu.VMEM((4, rows, width), BF16),
            pltpu.VMEM((peers,) + piece, BF16),
            pltpu.VMEM((peers,) + piece, BF16),
            pltpu.VMEM(piece, BF16),
            pltpu.VMEM((peers,) + piece, BF16),
            pltpu.VMEM((TENSOR, small_rows, width), F32),
            pltpu.SemaphoreType.DMA((2, 6)),
            pltpu.SemaphoreType.DMA((2, peers)),
            pltpu.SemaphoreType.DMA((2, peers)),
            pltpu.SemaphoreType.DMA((2, TENSOR)),
        ],
        compiler_params=pltpu.CompilerParams(
            collective_id=2, has_side_effects=True, vmem_limit_bytes=VMEM_BYTES
        ),
        name="last",
    )(seq, dq, dk, dv, wq, wk, wv, tokens, gain, gres, dwo, drouter, dgain)


def body(
    tokens,
    first_gain,
    second_gain,
    query_weight,
    key_weight,
    value_weight,
    output_weight,
    router_weight,
    expert_in,
    expert_out,
    cotangent,
    routes,
    priority,
    prefix_len,
):
    rows, width = tokens.shape
    experts = router_weight.shape[1]
    peers = lax.axis_size("expert")
    capacity = (5 * GROUP * TOP + 4 * experts - 1) // (4 * experts)
    gain_one = first_gain.reshape(1, width)
    gain_two = second_gain.reshape(1, width)
    seq, q, k, v, kept = project_rows(
        tokens, gain_one, query_weight, key_weight, value_weight, routes, priority, experts, capacity
    )
    wo = lax.all_gather(output_weight, "tensor", axis=0, tiled=True)
    win = lax.all_gather(expert_in, "tensor", axis=0, tiled=True)
    wout = lax.all_gather(expert_out, "tensor", axis=0, tiled=True)
    ctx, lse = attend(q, k, v, prefix_len)
    out, gres, gctx, dwin, dwout, dwo, drouter, dgain = middle(
        ctx, tokens, gain_two, wo, router_weight, kept, cotangent, win, wout
    )
    dwo = lax.psum_scatter(dwo, "tensor", scatter_dimension=0, tiled=True)
    dwin = lax.psum_scatter(dwin, "tensor", scatter_dimension=0, tiled=True)
    dwout = lax.psum_scatter(dwout, "tensor", scatter_dimension=0, tiled=True)
    dq, dk, dv = attend_back(q, k, v, gctx, ctx, lse, prefix_len)
    gtok, gq, gk, gv, go, small = last(
        seq,
        dq,
        dk,
        dv,
        query_weight,
        key_weight,
        value_weight,
        tokens,
        gain_one,
        gres,
        dwo[0],
        drouter,
        dgain,
        peers,
    )
    return (
        out,
        gtok,
        small[experts],
        small[experts + 1],
        gq,
        gk,
        gv,
        go,
        small[:experts].T,
        dwin.astype(F32),
        dwout.astype(F32),
    )


def solution(mesh):
    in_specs = (
        P(("expert", "tensor"), None),
        P(),
        P(),
        P(None, "tensor"),
        P(None, "tensor"),
        P(None, "tensor"),
        P("tensor", None),
        P(),
        P("expert", None, "tensor"),
        P("expert", "tensor", None),
        P(("expert", "tensor"), None),
        P(("expert", "tensor"), None),
        P(("expert", "tensor"), None),
        P("expert"),
    )
    out_specs = (
        P(("expert", "tensor"), None),
        P(("expert", "tensor"), None),
        P(),
        P(),
        P(None, "tensor"),
        P(None, "tensor"),
        P(None, "tensor"),
        P("tensor", None),
        P(),
        P("expert", None, "tensor"),
        P("expert", "tensor", None),
    )
    return jax.shard_map(body, mesh=mesh, in_specs=in_specs, out_specs=out_specs, check_vma=False)
```

```python
import functools

import jax
import jax.numpy as jnp
from jax import lax
from jax.experimental import pallas as pl
from jax.experimental.pallas import tpu as pltpu
from jax.sharding import PartitionSpec as P

HEAD_DIM = 64
GROUP = 32
TOP = 4
EPS = 1e-05
NEG = -1e30
SCORE_SCALE = HEAD_DIM**-0.5
PREFIX_MOST = 1024
MESH = pl.DeviceIdType.MESH
VM = pl.BlockSpec(memory_space=pltpu.VMEM)
SM = pl.BlockSpec(memory_space=pltpu.SMEM)
HB = pl.BlockSpec(memory_space=pltpu.HBM)
TENSOR = 4
VMEM_BYTES = 58 << 20
BF16 = jnp.bfloat16
F32 = jnp.float32


def dotf(left, right, dims=((1,), (0,)), precision=None):
    return lax.dot_general(
        left, right, (dims, ((), ())), preferred_element_type=F32, precision=precision
    )


def iota(shape, axis):
    return lax.broadcasted_iota(jnp.int32, shape, axis)


def one_hot(test):
    return jnp.where(test, 1.0, 0.0).astype(BF16)


def norm_parts(values):
    center = values - jnp.mean(values, axis=1, keepdims=True)
    spread = lax.rsqrt(jnp.mean(center * center, axis=1, keepdims=True) + EPS)
    return center * spread, spread


def remote(src, dst, sems, slot, axis, to):
    return pltpu.make_async_remote_copy(
        src_ref=src,
        dst_ref=dst,
        send_sem=sems.at[0, slot],
        recv_sem=sems.at[1, slot],
        device_id={axis: to},
        device_id_type=MESH,
    )


def greet(axis, size):
    barrier = pltpu.get_barrier_semaphore()
    me = lax.axis_index(axis)

    def one(off, _):
        pl.semaphore_signal(
            barrier, inc=1, device_id={axis: lax.rem(me + off, size)}, device_id_type=MESH
        )
        return 0

    lax.fori_loop(1, size, one, 0)


def each(first, last, act):
    def one(at, _):
        act(at)
        return 0

    lax.fori_loop(first, last, one, 0)


def block_of(start, size):
    return pl.ds(pl.multiple_of(start, size), size)


def pick_head(values, head, other=0.0):
    lane = iota(values.shape, 1)
    inside = (lane >= head * HEAD_DIM) & (lane < (head + 1) * HEAD_DIM)
    return jnp.where(inside, values, jnp.full_like(values, other))


class Gather:
    def __init__(self, buf, sems, place):
        self.buf, self.sems, self.place = buf, sems, place
        self.right, self.left = lax.rem(place + 1, TENSOR), lax.rem(place + TENSOR - 1, TENSOR)
        half = buf.shape[1] // 2
        self.low, self.high = pl.ds(0, half), pl.ds(half, half)

    def copy(self, slot):
        owner, part, to = (
            (self.place, self.low, self.right),
            (self.place, self.high, self.left),
            (self.place, self.high, self.right),
            (self.place, self.low, self.left),
            (self.left, self.low, self.right),
            (self.right, self.high, self.left),
        )[slot]
        block = self.buf.at[owner, part]
        return remote(block, block, self.sems, slot, "tensor", to)

    def start(self):
        for slot in range(4):
            self.copy(slot).start()

    def forward(self):
        self.copy(0).wait_recv()
        self.copy(4).start()
        self.copy(1).wait_recv()
        self.copy(5).start()

    def wait_near(self):
        self.copy(2).wait_recv()
        self.copy(3).wait_recv()

    def wait_far(self):
        self.copy(4).wait_recv()
        self.copy(5).wait_recv()

    def drain(self):
        for slot in range(6):
            self.copy(slot).wait_send()


class Scatter:
    def __init__(self, part, via, land, sems, place):
        self.part, self.via, self.land, self.sems, self.place = part, via, land, sems, place
        self.right, self.left = lax.rem(place + 1, TENSOR), lax.rem(place + TENSOR - 1, TENSOR)
        self.far = lax.rem(place + 2, TENSOR)
        half = part.shape[1] // 2
        self.low, self.high = pl.ds(0, half), pl.ds(half, half)

    def copy(self, slot):
        block, half, to, dst = (
            (self.far, self.low, self.right, self.via),
            (self.far, self.high, self.left, self.via),
            (self.right, self.high, self.right, self.land.at[0]),
            (self.left, self.low, self.left, self.land.at[1]),
            (self.right, self.low, self.right, self.land.at[0]),
            (self.left, self.high, self.left, self.land.at[1]),
        )[slot]
        return remote(self.part.at[block, half], dst.at[half], self.sems, slot, "tensor", to)

    def start_far(self):
        self.copy(0).start()
        self.copy(1).start()

    def start_own(self):
        self.copy(2).start()
        self.copy(3).start()

    def add_far(self):
        self.copy(0).wait_recv()
        self.part[self.right, self.low] = (
            self.part[self.right, self.low].astype(F32) + self.via[self.low].astype(F32)
        ).astype(BF16)
        self.copy(1).wait_recv()
        self.part[self.left, self.high] = (
            self.part[self.left, self.high].astype(F32) + self.via[self.high].astype(F32)
        ).astype(BF16)

    def start_sums(self):
        self.copy(4).start()
        self.copy(5).start()

    def wait(self):
        for slot in range(2, 6):
            self.copy(slot).wait_recv()

    def landed(self, rows):
        return self.land[0, rows].astype(F32) + self.land[1, rows].astype(F32)

    def drain(self):
        for slot in range(6):
            self.copy(slot).wait_send()


def layer_kernel(
    prefix_ref,
    tok_hbm,
    gain_one_hbm,
    gain_two_hbm,
    wq_hbm,
    wk_hbm,
    wv_hbm,
    wo_hbm,
    router_hbm,
    win_hbm,
    wout_hbm,
    cot_hbm,
    routes_hbm,
    prio_hbm,
    out_ref,
    gtok_ref,
    gq_ref,
    gk_ref,
    gv_ref,
    go_ref,
    small_ref,
    dfirst_ref,
    dwin_ref,
    dwout_ref,
    tok_s,
    gain_one,
    gain_two,
    w_s,
    wo_s,
    router_s,
    win_s,
    wout_s,
    cot_s,
    routes_s,
    prio_s,
    seq_s,
    q_s,
    k_s,
    v_s,
    kept_s,
    ctx_s,
    lse_s,
    ctx_all,
    wide_router,
    res_s,
    scaled_s,
    spread_s,
    pair_s,
    weight_s,
    low_s,
    out_s,
    in_s,
    done_s,
    ret_s,
    acc_s,
    hidden_s,
    gpre_s,
    gctx_s,
    gctx_all,
    gatt_s,
    glog_s,
    dgain_s,
    dwin_s,
    dwout_s,
    via_win,
    via_wout,
    land_win,
    land_wout,
    wop_s,
    wop_in,
    wop_sum,
    wop_all,
    dq_acc,
    dk_acc,
    dv_acc,
    inner_s,
    grads_s,
    rows_s,
    via_rows,
    land_rows,
    mine_s,
    piece_s,
    piece_in,
    sum_s,
    sum_all,
    first_s,
    local_sems,
    store_sems,
    tok_sems,
    win_sems,
    wout_sems,
    wo_sems,
    ctx_sems,
    mix_sems,
    ret_sems,
    back_sems,
    dwin_sems,
    dwout_sems,
    wop_sems,
    wopz_sems,
    wopb_sems,
    row_sems,
    piece_sems,
    sum_sems,
    first_sems,
    *,
    experts,
    capacity,
):
    place = lax.axis_index("tensor")
    me = lax.axis_index("expert")
    right, left = lax.rem(place + 1, TENSOR), lax.rem(place + TENSOR - 1, TENSOR)
    far = lax.rem(place + 2, TENSOR)
    _, rows, width = tok_s.shape
    length, hcols = q_s.shape
    heads = hcols // HEAD_DIM
    groups = rows // GROUP
    wide = experts * groups
    peers = experts
    barrier = pltpu.get_barrier_semaphore()
    greet("tensor", TENSOR)
    greet("expert", peers)

    loads = [
        (tok_hbm, tok_s.at[place]),
        (gain_one_hbm, gain_one),
        (wq_hbm, w_s.at[:, pl.ds(0, hcols)]),
        (wk_hbm, w_s.at[:, pl.ds(hcols, hcols)]),
        (wv_hbm, w_s.at[:, pl.ds(2 * hcols, hcols)]),
        (routes_hbm, routes_s),
        (prio_hbm, prio_s),
        (wo_hbm, wo_s.at[place]),
        (win_hbm, win_s.at[place]),
        (wout_hbm, wout_s.at[place]),
        (gain_two_hbm, gain_two),
        (router_hbm, router_s),
        (cot_hbm, cot_s),
    ]
    loads = [
        pltpu.make_async_copy(src, dst, local_sems.at[at]) for at, (src, dst) in enumerate(loads)
    ]
    for load in loads:
        load.start()

    tok_ring = Gather(tok_s, tok_sems, place)
    win_ring = Gather(win_s, win_sems, place)
    wout_ring = Gather(wout_s, wout_sems, place)
    wo_ring = Gather(wo_s, wo_sems, place)
    loads[0].wait()
    pl.semaphore_wait(barrier, TENSOR - 1 + peers - 1)
    tok_ring.start()
    for load in loads[1:5]:
        load.wait()

    half = rows // 2

    def project(owner, part):
        @pl.loop(0, 2)
        def _(at):
            count = half // 2
            start = part * half + at * count
            scaled, _ = norm_parts(tok_s[owner, block_of(start, count)].astype(F32))
            normed = (scaled * gain_one[...]).astype(BF16)
            to = block_of(owner * rows + start, count)
            seq_s[to, :] = normed
            out = dotf(normed, w_s[...]).astype(BF16)
            q_s[to, :] = out[:, 0:hcols] * SCORE_SCALE
            k_s[to, :] = out[:, hcols : 2 * hcols]
            v_s[to, :] = out[:, 2 * hcols : 3 * hcols]

    project(place, 0)
    project(place, 1)
    tok_ring.forward()

    loads[5].wait()
    loads[6].wait()
    size = GROUP
    to_wide = one_hot(iota((experts, wide), 0) == iota((experts, wide), 1) // groups)
    prio = prio_s[...].astype(F32).astype(BF16)
    spread_rows = dotf(one_hot((iota((rows, groups), 0) // size) == iota((rows, groups), 1)), prio)
    at_col = (iota((rows, size), 0) % size) == iota((rows, size), 1)
    prio_col = jnp.sum(jnp.where(at_col, spread_rows, 0.0), axis=1, keepdims=True)
    group_tok = one_hot((iota((groups, rows), 1) // size) == iota((groups, rows), 0))
    spread_cols = dotf(prio, group_tok, ((0,), (0,)))
    at_row = (iota((size, rows), 1) % size) == iota((size, rows), 0)
    prio_row = jnp.sum(jnp.where(at_row, spread_cols, 0.0), axis=0, keepdims=True)
    named = routes_s[0:1, :] == iota((experts, rows), 0)
    for pick in range(1, TOP):
        named = named | (routes_s[pick : pick + 1, :] == iota((experts, rows), 0))
    own_group = (iota((rows, wide), 0) // size) == (iota((rows, wide), 1) % groups)
    member = jnp.where(own_group, dotf(one_hot(named), to_wide, ((0,), (0,))), 0.0)
    rank = dotf(one_hot(prio_row < prio_col), member.astype(BF16))
    kept_s[...] = jnp.where(rank < capacity, member, 0.0).astype(BF16)

    tok_ring.copy(2).wait_recv()
    project(left, 0)
    project(left, 1)
    tok_ring.copy(3).wait_recv()
    project(right, 0)
    project(right, 1)
    for load in loads[7:10]:
        load.wait()
    tok_ring.copy(4).wait_recv()
    project(far, 0)
    tok_ring.copy(5).wait_recv()
    wo_ring.start()
    win_ring.start()
    project(far, 1)

    prefix = prefix_ref[0]
    block = rows

    @pl.loop(0, length // block)
    def _(blk):
        row0 = pl.multiple_of(blk * block, block)
        q = q_s[pl.ds(row0, block), :]
        q_heads = [pick_head(q, head) for head in range(heads)]

        def step(kb, carry, masked):
            col0 = pl.multiple_of(kb * block, block)
            keys = k_s[pl.ds(col0, block), :]
            vals = v_s[pl.ds(col0, block), :]
            out = []
            if masked:
                row_ids = iota((block, block), 0) + row0
                col_ids = iota((block, block), 1) + col0
                seen = (col_ids <= row_ids) | (col_ids < prefix)
            for head in range(heads):
                peak, acc = carry[2 * head : 2 * head + 2]
                scores = dotf(q_heads[head], keys, ((1,), (1,)))
                if masked:
                    scores = jnp.where(seen, scores, NEG)
                new_peak = jnp.maximum(peak, jnp.max(scores, axis=1, keepdims=True))
                soft = jnp.exp(scores - new_peak).astype(BF16)
                acc = jnp.exp(peak - new_peak) * acc + dotf(soft, pick_head(vals, head, 1.0))
                out += [new_peak, acc]
            return tuple(out)

        init = (jnp.full((block, 1), NEG, F32), jnp.zeros((block, hcols), F32)) * heads
        carry = lax.fori_loop(0, blk, functools.partial(step, masked=False), init)
        seen_blocks = jnp.maximum(blk + 1, PREFIX_MOST // block)
        carry = lax.fori_loop(blk, seen_blocks, functools.partial(step, masked=True), carry)
        merged = jnp.zeros((block, hcols), F32)
        for head in range(heads):
            peak, acc = carry[2 * head : 2 * head + 2]
            lane = HEAD_DIM if head == 0 else 0
            total = acc[:, lane : lane + 1]
            merged = merged + pick_head(acc * (1.0 / total), head)
            lse = jnp.broadcast_to(peak + jnp.log(total), (block, 128))
            lse_s[pl.ds(8 * head, 8), pl.ds(row0, block)] = jnp.transpose(lse)[:8]
        ctx_s[pl.ds(row0, block), :] = merged.astype(BF16)

        @pl.when(blk == 2)
        def _():
            wo_ring.forward()

    def ctx_copy(off):
        to = lax.rem(place + off, TENSOR)
        src = ctx_s.at[block_of(to * rows, rows), :]
        return remote(src, ctx_all.at[place], ctx_sems, off, "tensor", to)

    for off in (2, 1, 3):
        ctx_copy(off).start()
    ctx_all[place] = ctx_s[block_of(place * rows, rows), :]
    for load in loads[10:]:
        load.wait()
    wide_router[...] = dotf(to_wide, router_s[...], ((0,), (0,))).astype(BF16)
    pair_s[:, 0:width] = cot_s[...].astype(BF16)
    wo_ring.wait_near()
    wo_ring.wait_far()
    wo_full = wo_s.reshape(TENSOR * hcols, width)
    for off in (2, 1, 3):
        ctx_copy(off).wait_recv()
    wout_ring.start()
    win_ring.forward()

    step_rows = 128

    @pl.loop(0, rows // step_rows)
    def _(step):
        part = block_of(step * step_rows, step_rows)
        ctx = jnp.concatenate([ctx_all[at, part, :] for at in range(TENSOR)], axis=1)
        residual = tok_s[place, part].astype(F32) + dotf(ctx, wo_full[...])
        res_s[part, :] = residual
        scaled, spread = norm_parts(residual)
        scaled_s[part, :] = scaled
        spread_s[part, :] = jnp.broadcast_to(spread, (step_rows, 128))
        mixer = (scaled * gain_two[...]).astype(BF16)
        pair_s[part, width : 2 * width] = mixer
        logits = dotf(mixer, wide_router[...], ((1,), (1,)))
        kept = kept_s[part, :].astype(F32)
        terms = jnp.where(kept > 0.0, jnp.exp(logits), 0.0)
        total = jnp.sum(terms, axis=0, keepdims=True)
        count = jnp.sum(kept, axis=0, keepdims=True)
        weight = terms / jnp.where(count > 0.0, total, 1.0)
        weight_s[part, :] = weight
        low_s[part, :] = weight.astype(BF16)

    @pl.loop(0, wide // 128)
    def _(blk):
        mixed = dotf(low_s[:, block_of(blk * 128, 128)], pair_s[...], ((0,), (0,))).astype(BF16)
        count = 128 // groups
        out_s[pl.ds(blk * count, count)] = mixed.reshape(count, groups, 2 * width)

    def mix_copy(off):
        to = lax.rem(me + off, peers)
        return remote(out_s.at[to], in_s.at[off], mix_sems, off, "expert", to)

    each(1, peers, lambda off: mix_copy(off).start())
    in_s[0] = out_s[me]

    def ret_copy(off):
        to = lax.rem(me + peers - off, peers)
        return remote(done_s.at[off], ret_s.at[me], ret_sems, off, "expert", to)

    batch = 128 // groups

    def expert_part(chunk, slices, start):
        part = block_of(chunk * 128, 128)
        rows_in = in_s[pl.ds(chunk * batch, batch)].reshape(128, 2 * width)
        grad = rows_in[:, 0:width]
        mixed = rows_in[:, width : 2 * width]
        for at in slices:
            pre = dotf(mixed, win_s[at])
            sigma = 1.0 / (1.0 + jnp.exp(-pre))
            hidden = (pre * sigma).astype(BF16)
            grad_hidden = dotf(grad, wout_s[at], ((1,), (1,)))
            grad_pre = (grad_hidden * (sigma * (1.0 + pre * (1.0 - sigma)))).astype(BF16)
            hidden_s[at, part, :] = hidden
            gpre_s[at, part, :] = grad_pre
            returned = dotf(hidden, wout_s[at])
            grad_mixed = dotf(grad_pre, win_s[at], ((1,), (1,)))
            if start:
                acc_s[0, part, :] = returned
                acc_s[1, part, :] = grad_mixed
                start = False
            else:
                acc_s[0, part, :] += returned
                acc_s[1, part, :] += grad_mixed

    win_ring.wait_near()

    @pl.loop(0, peers // batch)
    def _(chunk):
        begin = chunk * batch
        each(jnp.maximum(begin, 1), begin + batch, lambda off: mix_copy(off).wait_recv())
        expert_part(chunk, (place,), True)

        @pl.when(chunk == 1)
        def _():
            wout_ring.forward()

    wout_ring.wait_near()

    @pl.loop(0, peers // batch)
    def _(chunk):
        expert_part(chunk, (left, right), False)

    win_ring.wait_far()
    wout_ring.wait_far()

    @pl.loop(0, peers // batch)
    def _(chunk):
        expert_part(chunk, (far,), False)
        part = block_of(chunk * 128, 128)
        begin = chunk * batch
        done = jnp.concatenate([acc_s[0, part, :], acc_s[1, part, :]], axis=1).astype(BF16)
        done_s[pl.ds(begin, batch)] = done.reshape(batch, groups, 2 * width)
        each(jnp.maximum(begin, 1), begin + batch, lambda off: ret_copy(off).start())

    ret_s[me] = done_s[0]

    dwin_ring = Scatter(dwin_s, via_win, land_win, dwin_sems, place)
    dwout_ring = Scatter(dwout_s, via_wout, land_wout, dwout_sems, place)

    def expert_grads(off):
        at = lax.rem(place + off, TENSOR)
        rows_in = in_s[...].reshape(wide, 2 * width)
        dwin_s[at] = dotf(rows_in[:, width : 2 * width], gpre_s[at], ((0,), (0,))).astype(BF16)
        dwout_s[at] = dotf(hidden_s[at], rows_in[:, 0:width], ((0,), (0,))).astype(BF16)

    @pl.loop(0, TENSOR)
    def _(turn):
        expert_grads(lax.rem(turn + 2, TENSOR))

        @pl.when(turn == 0)
        def _():
            dwin_ring.start_far()
            dwout_ring.start_far()

    dwin_ring.start_own()
    each(1, peers, lambda off: ret_copy(off).wait_recv())

    dgain_s[...] = jnp.zeros_like(dgain_s)
    from_wide = one_hot(iota((wide, experts), 0) // groups == iota((wide, experts), 1))

    @pl.loop(0, rows // step_rows)
    def _(step):
        part = block_of(step * step_rows, step_rows)
        came = ret_s[...].reshape(wide, 2 * width)
        low = low_s[part, :]
        weight = weight_s[part, :]
        back = dotf(low, came)
        kept_s[part, :] = (res_s[part, :] + back[:, 0:width]).astype(BF16)
        grad_weight = dotf(pair_s[part, :], came, ((1,), (1,)))
        inner = jnp.sum(weight * grad_weight, axis=0, keepdims=True)
        grad_logits = (weight * (grad_weight - inner)).astype(BF16)
        glog_s[part, :] = dotf(grad_logits, from_wide).astype(BF16)
        grad_mixer = back[:, width : 2 * width] + dotf(grad_logits, wide_router[...])
        scaled = scaled_s[part, :]
        dgain_s[...] += jnp.sum(grad_mixer * scaled, axis=0, keepdims=True)
        grad_scaled = grad_mixer * gain_two[...]
        centered = grad_scaled - jnp.mean(grad_scaled, axis=1, keepdims=True)
        along = jnp.mean(grad_scaled * scaled, axis=1, keepdims=True)
        grad_res = cot_s[part, :] + spread_s[part, 0:1] * (centered - scaled * along)
        res_s[part, :] = grad_res
        grad_att = grad_res.astype(BF16)
        gatt_s[part, :] = grad_att
        grad_ctx = dotf(grad_att, wo_full[...], ((1,), (1,))).astype(BF16)
        for at in range(TENSOR):
            gctx_s[at, part, :] = grad_ctx[:, at * hcols : (at + 1) * hcols]

    def back_copy(off):
        to = lax.rem(place + off, TENSOR)
        dst = gctx_all.at[block_of(place * rows, rows), :]
        return remote(gctx_s.at[to], dst, back_sems, off, "tensor", to)

    for off in (2, 1, 3):
        back_copy(off).start()
    out_store = pltpu.make_async_copy(kept_s, out_ref, store_sems.at[0])
    out_store.start()
    gctx_all[block_of(place * rows, rows), :] = gctx_s[place]

    each_rows = width // peers
    for at in range(TENSOR):
        grad_wo = dotf(ctx_all[at], gatt_s[...], ((0,), (0,))).astype(BF16)
        count = peers // TENSOR
        wop_s[at * count : (at + 1) * count, :, 0:width] = grad_wo.reshape(count, each_rows, width)
    grad_router = dotf(glog_s[...], pair_s[:, width : 2 * width], ((0,), (0,)))
    blocks = width // hcols
    small_rows = jnp.concatenate(
        [grad_router, dgain_s[...], jnp.zeros((width // blocks - experts - 1, width), F32)], axis=0
    ).astype(BF16)
    small_tall = jnp.concatenate(
        [small_rows[:, at * hcols : (at + 1) * hcols] for at in range(blocks)], axis=0
    )
    wop_s[:, :, width : width + hcols] = small_tall.reshape(peers, each_rows, hcols)

    def wop_copy(off):
        to = lax.rem(me + off, peers)
        return remote(wop_s.at[to], wop_in.at[off], wop_sems, off, "expert", to)

    each(1, peers, lambda off: wop_copy(off).start())
    wop_in[0] = wop_s[me]
    dwin_ring.add_far()
    dwout_ring.add_far()
    for off in (2, 1, 3):
        back_copy(off).wait_recv()
    dwin_ring.start_sums()
    dwout_ring.start_own()
    dwout_ring.start_sums()

    dq_acc[...] = jnp.zeros_like(dq_acc)
    ones = [pick_head(jnp.ones((8, hcols), F32), head) for head in range(heads)]

    @pl.loop(0, length // block)
    def _(blk):
        part = block_of(blk * block, block)
        product = gctx_all[part, :].astype(F32) * ctx_s[part, :].astype(F32)
        for head in range(heads):
            inner_s[pl.ds(8 * head, 8), part] = dotf(
                ones[head], product, ((1,), (1,)), lax.Precision.HIGHEST
            )

    def wopz_copy(off):
        to = lax.rem(place + off, TENSOR)
        return remote(wop_sum.at[place], wop_sum.at[place], wopz_sems, off, "tensor", to)

    def wopb_copy(off):
        to = lax.rem(me + off, peers)
        return remote(wop_all.at[me], wop_all.at[me], wopb_sems, off, "expert", to)

    @pl.loop(0, length // block)
    def _(kb):
        col0 = pl.multiple_of(kb * block, block)
        keys = k_s[pl.ds(col0, block), :]
        vals = v_s[pl.ds(col0, block), :]
        key_heads = [pick_head(keys, head) for head in range(heads)]
        dk_acc[...] = jnp.zeros_like(dk_acc)
        dv_acc[...] = jnp.zeros_like(dv_acc)

        def step(blk, masked):
            row0 = pl.multiple_of(blk * block, block)
            part = pl.ds(row0, block)
            q = q_s[part, :]
            grad = gctx_all[part, :]
            if masked:
                key_ids = iota((block, block), 0) + col0
                row_ids = iota((block, block), 1) + row0
                seen = (key_ids <= row_ids) | (key_ids < prefix)
            dq = dq_acc[part, :]
            dk = dk_acc[...]
            dv = dv_acc[...]
            for head in range(heads):
                q_head = pick_head(q, head)
                grad_head = pick_head(grad, head)
                scores = dotf(keys, q_head, ((1,), (1,)))
                if masked:
                    scores = jnp.where(seen, scores, NEG)
                soft = jnp.exp(scores - lse_s[pl.ds(8 * head, 1), part])
                grad_soft = dotf(vals, grad_head, ((1,), (1,)))
                grad_scores = (soft * (grad_soft - inner_s[pl.ds(8 * head, 1), part])).astype(BF16)
                dv += dotf(soft.astype(BF16), grad_head)
                dk += dotf(grad_scores, q_head)
                dq += dotf(grad_scores, key_heads[head], ((0,), (0,)))
            dq_acc[part, :] = dq
            dk_acc[...] = dk
            dv_acc[...] = dv

        first = jnp.where(kb < PREFIX_MOST // block, 0, kb)
        each(first, kb + 1, functools.partial(step, masked=True))
        each(kb + 1, length // block, functools.partial(step, masked=False))
        grads_s[pl.ds(col0, block), hcols : 2 * hcols] = dk_acc[...].astype(BF16)
        grads_s[pl.ds(col0, block), 2 * hcols : 3 * hcols] = dv_acc[...].astype(BF16)

        @pl.when(kb == 0)
        def _():
            each(1, peers, lambda off: wop_copy(off).wait_recv())
            total = jnp.zeros(wop_sum.shape[1:], F32)
            total = lax.fori_loop(0, peers, lambda off, acc: acc + wop_in[off].astype(F32), total)
            wop_sum[place] = total.astype(BF16)
            for off in (2, 1, 3):
                wopz_copy(off).start()

        @pl.when(kb == 1)
        def _():
            for off in (2, 1, 3):
                wopz_copy(off).wait_recv()
            total = jnp.zeros(wop_sum.shape[1:], F32)
            for at in range(TENSOR):
                total = total + wop_sum[at].astype(F32)
            wop_all[me] = total.astype(BF16)
            each(1, peers, lambda off: wopb_copy(off).start())

    grads_s[:, 0:hcols] = (dq_acc[...] * SCORE_SCALE).astype(BF16)

    def partial_rows(owner, part):
        start = owner * rows + part * half
        return dotf(grads_s[block_of(start, half), :], w_s[...], ((1,), (1,)))

    row_ring = Scatter(rows_s, via_rows, land_rows, row_sems, place)
    low, high = row_ring.low, row_ring.high
    rows_s[far, low] = partial_rows(far, 0).astype(BF16)
    rows_s[far, high] = partial_rows(far, 1).astype(BF16)
    row_ring.start_far()
    rows_s[right, high] = partial_rows(right, 1).astype(BF16)
    rows_s[left, low] = partial_rows(left, 0).astype(BF16)
    row_ring.start_own()

    @pl.loop(0, 3)
    def _(at):
        cols = block_of(at * hcols, hcols)
        grad = dotf(seq_s[...], grads_s[:, cols], ((0,), (0,)))
        piece_s[at] = grad.astype(BF16).reshape(peers, each_rows, hcols)

    def piece_copy(off):
        to = lax.rem(me + off, peers)
        return remote(piece_s.at[:, to], piece_in.at[off], piece_sems, off, "expert", to)

    each(1, peers, lambda off: piece_copy(off).start())
    for at in range(3):
        piece_in[0, at] = piece_s[at, me]
    rows_s[right, low] = partial_rows(right, 0).astype(BF16)
    rows_s[left, high] = partial_rows(left, 1).astype(BF16)
    row_ring.add_far()
    row_ring.start_sums()
    mine_s[low, :] = partial_rows(place, 0)
    mine_s[high, :] = partial_rows(place, 1)

    each(1, peers, lambda off: piece_copy(off).wait_recv())
    total = jnp.zeros(sum_s.shape, F32)
    total = lax.fori_loop(0, peers, lambda off, acc: acc + piece_in[off].astype(F32), total)
    sum_s[...] = total.astype(BF16)

    def sum_copy(off):
        to = lax.rem(me + off, peers)
        return remote(sum_s, sum_all.at[:, me], sum_sems, off, "expert", to)

    each(1, peers, lambda off: sum_copy(off).start())
    for at in range(3):
        sum_all[at, me] = sum_s[at]

    dwin_ring.wait()
    dwout_ring.wait()
    for at, (ring, part_s) in enumerate(((dwin_ring, dwin_s), (dwout_ring, dwout_s))):
        for part in (low, high):
            acc_s[at, part, :] = part_s[place, part].astype(F32) + ring.landed(part)
    win_store = pltpu.make_async_copy(acc_s.at[0], dwin_ref, store_sems.at[1])
    wout_store = pltpu.make_async_copy(acc_s.at[1], dwout_ref, store_sems.at[2])
    win_store.start()
    wout_store.start()
    each(1, peers, lambda off: wopb_copy(off).wait_recv())
    count = peers // TENSOR
    go_ref[...] = wop_all[pl.ds(place * count, count), :, 0:width].reshape(hcols, width).astype(F32)
    small = wop_all[:, :, width : width + hcols].reshape(width, hcols)
    tall = width // blocks
    kept_rows = small_ref.shape[0]
    small_ref[...] = jnp.concatenate(
        [small[at * tall : at * tall + kept_rows] for at in range(blocks)], axis=1
    ).astype(F32)

    row_ring.wait()
    for part in (low, high):
        grad_normed = mine_s[part, :] + row_ring.landed(part)
        scaled, spread = norm_parts(tok_s[place, part].astype(F32))
        grad_scaled = grad_normed * gain_one[...]
        centered = grad_scaled - jnp.mean(grad_scaled, axis=1, keepdims=True)
        along = jnp.mean(grad_scaled * scaled, axis=1, keepdims=True)
        scaled_s[part, :] = res_s[part, :] + spread * (centered - scaled * along)
    tok_store = pltpu.make_async_copy(scaled_s, gtok_ref, store_sems.at[3])
    tok_store.start()

    each(1, peers, lambda off: sum_copy(off).wait_recv())
    dfirst = jnp.zeros((8, width), F32)
    for at, grad_ref in enumerate((gq_ref, gk_ref, gv_ref)):
        grad = sum_all[at].reshape(width, hcols).astype(F32)
        grad_ref[...] = grad
        product = grad * w_s[:, at * hcols : (at + 1) * hcols].astype(F32)
        dfirst = dfirst + dotf(
            jnp.ones((8, hcols), F32), product, ((1,), (1,)), lax.Precision.HIGHEST
        )
    first_s[place] = dfirst / gain_one[...]

    def first_copy(off):
        to = lax.rem(place + off, TENSOR)
        return remote(first_s.at[place], first_s.at[place], first_sems, off, "tensor", to)

    for off in (2, 1, 3):
        first_copy(off).start()

    for ring in (tok_ring, win_ring, wout_ring, wo_ring, dwin_ring, dwout_ring, row_ring):
        ring.drain()
    for off in (2, 1, 3):
        ctx_copy(off).wait_send()
        back_copy(off).wait_send()
        wopz_copy(off).wait_send()

    def drain(off):
        for copy in (mix_copy, ret_copy, wop_copy, wopb_copy, piece_copy, sum_copy):
            copy(off).wait_send()

    each(1, peers, drain)
    for off in (2, 1, 3):
        first_copy(off).wait_recv()
    dfirst_ref[...] = first_s[0] + first_s[1] + first_s[2] + first_s[3]
    for off in (2, 1, 3):
        first_copy(off).wait_send()
    for store in (out_store, win_store, wout_store, tok_store):
        store.wait()


def layer(prefix, tokens, gain_one, gain_two, wq, wk, wv, wo, router, win, wout, cot, routes, prio):
    rows, width = tokens.shape
    experts = router.shape[0]
    hcols = wq.shape[1]
    fcols = win.shape[1]
    groups = rows // GROUP
    wide = experts * groups
    length = TENSOR * rows
    heads = hcols // HEAD_DIM
    peers = experts
    each_rows = width // peers
    capacity = (5 * GROUP * TOP + 4 * experts - 1) // (4 * experts)

    def dev(shape, kind):
        return jax.ShapeDtypeStruct(shape, kind)

    def low(*shape):
        return pltpu.VMEM(shape, BF16)

    def full(*shape):
        return pltpu.VMEM(shape, F32)

    def sems(count):
        return pltpu.SemaphoreType.DMA((2, count))

    small_rows = (experts + 1 + 15) // 16 * 16
    return pl.pallas_call(
        functools.partial(layer_kernel, experts=experts, capacity=float(capacity)),
        out_shape=(
            dev((rows, width), BF16),
            dev((rows, width), F32),
            dev(wq.shape, F32),
            dev(wq.shape, F32),
            dev(wq.shape, F32),
            dev(wo.shape, F32),
            dev((small_rows, width), F32),
            dev((8, width), F32),
            dev(win.shape, F32),
            dev(wout.shape, F32),
        ),
        in_specs=[SM] + [HB] * 13,
        out_specs=(HB,) * 2 + (VM,) * 6 + (HB,) * 2,
        scratch_shapes=[
            low(TENSOR, rows, width),
            full(1, width),
            full(1, width),
            low(width, 3 * hcols),
            low(TENSOR, hcols, width),
            low(experts, width),
            low(TENSOR, width, fcols),
            low(TENSOR, fcols, width),
            full(rows, width),
            pltpu.VMEM(routes.shape, jnp.int32),
            pltpu.VMEM(prio.shape, jnp.int32),
            low(length, width),
            low(length, hcols),
            low(length, hcols),
            low(length, hcols),
            low(rows, wide),
            low(length, hcols),
            full(8 * heads, length),
            low(TENSOR, rows, hcols),
            low(wide, width),
            full(rows, width),
            full(rows, width),
            full(rows, 128),
            low(rows, 2 * width),
            full(rows, wide),
            low(rows, wide),
            low(experts, groups, 2 * width),
            low(experts, groups, 2 * width),
            low(experts, groups, 2 * width),
            low(experts, groups, 2 * width),
            full(2, wide, width),
            low(TENSOR, wide, fcols),
            low(TENSOR, wide, fcols),
            low(TENSOR, rows, hcols),
            low(length, hcols),
            low(rows, width),
            low(rows, experts),
            full(1, width),
            low(TENSOR, width, fcols),
            low(TENSOR, fcols, width),
            low(width, fcols),
            low(fcols, width),
            low(2, width, fcols),
            low(2, fcols, width),
            low(peers, each_rows, width + hcols),
            low(peers, each_rows, width + hcols),
            low(TENSOR, each_rows, width + hcols),
            low(peers, each_rows, width + hcols),
            full(length, hcols),
            full(rows, hcols),
            full(rows, hcols),
            full(8 * heads, length),
            low(length, 3 * hcols),
            low(TENSOR, rows, width),
            low(rows, width),
            low(2, rows, width),
            full(rows, width),
            low(3, peers, each_rows, hcols),
            low(peers, 3, each_rows, hcols),
            low(3, each_rows, hcols),
            low(3, peers, each_rows, hcols),
            full(TENSOR, 8, width),
            pltpu.SemaphoreType.DMA((13,)),
            pltpu.SemaphoreType.DMA((4,)),
            sems(6),
            sems(6),
            sems(6),
            sems(6),
            sems(TENSOR),
            sems(peers),
            sems(peers),
            sems(TENSOR),
            sems(6),
            sems(6),
            sems(peers),
            sems(TENSOR),
            sems(peers),
            sems(6),
            sems(peers),
            sems(peers),
            sems(TENSOR),
        ],
        compiler_params=pltpu.CompilerParams(
            collective_id=0, has_side_effects=True, vmem_limit_bytes=VMEM_BYTES
        ),
        name="layer",
    )(prefix, tokens, gain_one, gain_two, wq, wk, wv, wo, router, win, wout, cot, routes, prio)


def body(
    tokens,
    first_gain,
    second_gain,
    query_weight,
    key_weight,
    value_weight,
    output_weight,
    router_weight,
    expert_in,
    expert_out,
    cotangent,
    routes,
    priority,
    prefix_len,
):
    width = tokens.shape[1]
    experts = router_weight.shape[1]
    out, gtok, gq, gk, gv, go, small, dfirst, dwin, dwout = layer(
        prefix_len,
        tokens,
        first_gain.reshape(1, width),
        second_gain.reshape(1, width),
        query_weight,
        key_weight,
        value_weight,
        output_weight,
        router_weight.T,
        expert_in[0],
        expert_out[0],
        cotangent,
        routes.T,
        priority,
    )
    return (
        out,
        gtok,
        dfirst[0],
        small[experts],
        gq,
        gk,
        gv,
        go,
        small[:experts].T,
        dwin[None],
        dwout[None],
    )


def solution(mesh):
    in_specs = (
        P(("expert", "tensor"), None),
        P(),
        P(),
        P(None, "tensor"),
        P(None, "tensor"),
        P(None, "tensor"),
        P("tensor", None),
        P(),
        P("expert", None, "tensor"),
        P("expert", "tensor", None),
        P(("expert", "tensor"), None),
        P(("expert", "tensor"), None),
        P(("expert", "tensor"), None),
        P("expert"),
    )
    out_specs = (
        P(("expert", "tensor"), None),
        P(("expert", "tensor"), None),
        P(),
        P(),
        P(None, "tensor"),
        P(None, "tensor"),
        P(None, "tensor"),
        P("tensor", None),
        P(),
        P("expert", None, "tensor"),
        P("expert", "tensor", None),
    )
    return jax.shard_map(body, mesh=mesh, in_specs=in_specs, out_specs=out_specs, check_vma=False)
```

```python
import functools

import jax
import jax.numpy as jnp
from jax import lax
from jax.experimental import pallas as pl
from jax.experimental.pallas import tpu as pltpu
from jax.sharding import PartitionSpec as P

HEAD_DIM = 64
GROUP = 32
TOP = 4
EPS = 1e-05
NEG = -1e30
SCORE_SCALE = HEAD_DIM**-0.5
PREFIX_MOST = 1024
ROW = 8
MESH = pl.DeviceIdType.MESH
VM = pl.BlockSpec(memory_space=pltpu.VMEM)
SM = pl.BlockSpec(memory_space=pltpu.SMEM)
HB = pl.BlockSpec(memory_space=pltpu.HBM)
TENSOR = 4
VMEM_BYTES = 58 << 20
BF16 = jnp.bfloat16
F32 = jnp.float32


def dotf(left, right, dims=((1,), (0,)), precision=None):
    return lax.dot_general(
        left, right, (dims, ((), ())), preferred_element_type=F32, precision=precision
    )


def iota(shape, axis):
    return lax.broadcasted_iota(jnp.int32, shape, axis)


def one_hot(test):
    return jnp.where(test, 1.0, 0.0).astype(BF16)


def norm_parts(values):
    center = values - jnp.mean(values, axis=1, keepdims=True)
    spread = lax.rsqrt(jnp.mean(center * center, axis=1, keepdims=True) + EPS)
    return center * spread, spread


def remote(src, dst, sems, slot, axis, to):
    return pltpu.make_async_remote_copy(
        src_ref=src,
        dst_ref=dst,
        send_sem=sems.at[0, slot],
        recv_sem=sems.at[1, slot],
        device_id={axis: to},
        device_id_type=MESH,
    )


def fan(src, dst, sems, to, lane=0):
    return pltpu.make_async_remote_copy(
        src_ref=src,
        dst_ref=dst,
        send_sem=sems.at[0],
        recv_sem=sems.at[1 + lane],
        device_id={"expert": to},
        device_id_type=MESH,
    )


def greet(peers):
    barrier = pltpu.get_barrier_semaphore()
    place = lax.axis_index("tensor")
    me = lax.axis_index("expert")

    def signal(axis, to):
        pl.semaphore_signal(barrier, inc=1, device_id={axis: to}, device_id_type=MESH)

    for off in range(1, TENSOR):
        signal("tensor", lax.rem(place + off, TENSOR))
    for off in range(1, ROW):
        signal("expert", me // ROW * ROW + lax.rem(me + off, ROW))
    for off in range(ROW, peers, ROW):
        signal("expert", lax.rem(me + off, peers))
    return TENSOR - 1 + ROW - 1 + peers // ROW - 1


def each(first, last, act):
    def one(at, _):
        act(at)
        return 0

    lax.fori_loop(first, last, one, 0)


def block_of(start, size):
    return pl.ds(pl.multiple_of(start, size), size)


def pick_head(values, head, other=0.0):
    lane = iota(values.shape, 1)
    inside = (lane >= head * HEAD_DIM) & (lane < (head + 1) * HEAD_DIM)
    return jnp.where(inside, values, jnp.full_like(values, other))


class Gather:
    def __init__(self, buf, sems, place):
        self.buf, self.sems, self.place = buf, sems, place
        self.right, self.left = lax.rem(place + 1, TENSOR), lax.rem(place + TENSOR - 1, TENSOR)
        half = buf.shape[1] // 2
        self.low, self.high = pl.ds(0, half), pl.ds(half, half)

    def copy(self, slot):
        owner, part, to = (
            (self.place, self.low, self.right),
            (self.place, self.high, self.left),
            (self.place, self.high, self.right),
            (self.place, self.low, self.left),
            (self.left, self.low, self.right),
            (self.right, self.high, self.left),
        )[slot]
        block = self.buf.at[owner, part]
        return remote(block, block, self.sems, slot, "tensor", to)

    def start(self, slots=range(4)):
        for slot in slots:
            self.copy(slot).start()

    def forward(self):
        self.copy(0).wait_recv()
        self.copy(4).start()
        self.copy(1).wait_recv()
        self.copy(5).start()

    def wait_near(self):
        self.copy(2).wait_recv()
        self.copy(3).wait_recv()

    def wait_far(self):
        self.copy(4).wait_recv()
        self.copy(5).wait_recv()

    def drain(self):
        for slot in range(6):
            self.copy(slot).wait_send()


class Scatter:
    def __init__(self, part, via, land, sems, place):
        self.part, self.via, self.land, self.sems, self.place = part, via, land, sems, place
        self.right, self.left = lax.rem(place + 1, TENSOR), lax.rem(place + TENSOR - 1, TENSOR)
        self.far = lax.rem(place + 2, TENSOR)
        half = part.shape[1] // 2
        self.low, self.high = pl.ds(0, half), pl.ds(half, half)

    def copy(self, slot):
        block, half, to, dst = (
            (self.far, self.low, self.right, self.via),
            (self.far, self.high, self.left, self.via),
            (self.right, self.high, self.right, self.land.at[0]),
            (self.left, self.low, self.left, self.land.at[1]),
            (self.right, self.low, self.right, self.land.at[0]),
            (self.left, self.high, self.left, self.land.at[1]),
        )[slot]
        return remote(self.part.at[block, half], dst.at[half], self.sems, slot, "tensor", to)

    def start_far(self):
        self.copy(0).start()
        self.copy(1).start()

    def start_own(self):
        self.copy(2).start()
        self.copy(3).start()

    def add_far(self):
        self.copy(0).wait_recv()
        self.part[self.right, self.low] = (
            self.part[self.right, self.low].astype(F32) + self.via[self.low].astype(F32)
        ).astype(BF16)
        self.copy(1).wait_recv()
        self.part[self.left, self.high] = (
            self.part[self.left, self.high].astype(F32) + self.via[self.high].astype(F32)
        ).astype(BF16)

    def start_sums(self):
        self.copy(4).start()
        self.copy(5).start()

    def wait(self):
        for slot in range(2, 6):
            self.copy(slot).wait_recv()

    def landed(self, rows):
        return self.land[0, rows].astype(F32) + self.land[1, rows].astype(F32)

    def drain(self):
        for slot in range(6):
            self.copy(slot).wait_send()


def layer_kernel(
    prefix_ref,
    tok_hbm,
    gain_one_hbm,
    gain_two_hbm,
    wq_hbm,
    wk_hbm,
    wv_hbm,
    wo_hbm,
    router_hbm,
    win_hbm,
    wout_hbm,
    cot_hbm,
    routes_hbm,
    prio_hbm,
    out_ref,
    gtok_ref,
    gq_ref,
    gk_ref,
    gv_ref,
    go_ref,
    router_ref,
    dsecond_ref,
    dfirst_ref,
    dwin_ref,
    dwout_ref,
    tok_s,
    gain_one,
    gain_two,
    w_s,
    wo_s,
    router_s,
    win_s,
    wout_s,
    cot_s,
    routes_s,
    prio_s,
    seqt_s,
    q_s,
    k_s,
    kt_s,
    v_s,
    kept_s,
    ctx_s,
    lse_s,
    ctx_all,
    wide_router,
    res_s,
    scaled_s,
    spread_s,
    pair_s,
    weight_s,
    low_s,
    out_s,
    in_s,
    done_s,
    ret_s,
    acc_s,
    hidden_s,
    gpre_s,
    gctx_s,
    gctx_all,
    gatt_s,
    glog_s,
    dgain_s,
    dwin_s,
    dwout_s,
    via_win,
    via_wout,
    land_win,
    land_wout,
    wop_s,
    wop_in,
    wop_sum,
    wop_all,
    dk_acc,
    dv_acc,
    grads_s,
    rows_s,
    via_rows,
    land_rows,
    mine_s,
    piece_s,
    piece_in,
    sum_all,
    first_s,
    gain_all,
    local_sems,
    store_sems,
    plane_sem,
    tok_sems,
    win_sems,
    wout_sems,
    wo_sems,
    ctx_sems,
    mix_sems,
    ret_sems,
    back_sems,
    dwin_sems,
    dwout_sems,
    wop_sems,
    wopz_sems,
    wopb_sems,
    row_sems,
    piece_sems,
    sum_sems,
    first_sems,
    gain_sems,
    *,
    experts,
    capacity,
):
    place = lax.axis_index("tensor")
    me = lax.axis_index("expert")
    right, left = lax.rem(place + 1, TENSOR), lax.rem(place + TENSOR - 1, TENSOR)
    far = lax.rem(place + 2, TENSOR)
    _, rows, width = tok_s.shape
    length, hcols = q_s.shape
    heads = hcols // HEAD_DIM
    groups = rows // GROUP
    wide = experts * groups
    peers = experts
    greeted = greet(peers)

    loads = [
        (tok_hbm, tok_s.at[place]),
        (gain_one_hbm, gain_one),
        (wq_hbm, w_s.at[:, pl.ds(0, hcols)]),
        (wk_hbm, w_s.at[:, pl.ds(hcols, hcols)]),
        (wv_hbm, w_s.at[:, pl.ds(2 * hcols, hcols)]),
        (routes_hbm, routes_s),
        (prio_hbm, prio_s),
        (wo_hbm, wo_s.at[place]),
        (win_hbm, win_s.at[place]),
        (wout_hbm, wout_s.at[place]),
        (gain_two_hbm, gain_two),
        (router_hbm, router_s),
        (cot_hbm, cot_s),
    ]
    loads = [
        pltpu.make_async_copy(src, dst, local_sems.at[at]) for at, (src, dst) in enumerate(loads)
    ]
    for load in loads:
        load.start()

    def all_of(buf, sems):
        most = buf.at[pl.ds(1, peers - 1)]
        return fan(most, most, sems, lax.rem(me + 1, peers))

    batch = 128 // groups

    tok_ring = Gather(tok_s, tok_sems, place)
    win_ring = Gather(win_s, win_sems, place)
    wout_ring = Gather(wout_s, wout_sems, place)
    wo_ring = Gather(wo_s, wo_sems, place)
    loads[0].wait()
    pl.semaphore_wait(pltpu.get_barrier_semaphore(), greeted)
    tok_ring.start()
    for off in range(ROW, peers, ROW):
        to = lax.rem(me + off, peers)
        pl.semaphore_signal(plane_sem, inc=1, device_id={"expert": to}, device_id_type=MESH)
    for load in loads[1:5]:
        load.wait()

    half = rows // 2

    def project(owner):
        @pl.loop(0, rows // 128)
        def _(at):
            start = at * 128
            scaled, _ = norm_parts(tok_s[owner, block_of(start, 128)].astype(F32))
            normed = (scaled * gain_one[...]).astype(BF16)
            to = block_of(owner * rows + start, 128)
            seqt_s[:, to] = jnp.transpose(normed)
            out = dotf(normed, w_s[...]).astype(BF16)
            q_s[to, :] = out[:, 0:hcols] * SCORE_SCALE
            k_s[to, :] = out[:, hcols : 2 * hcols]
            kt_s[:, to] = jnp.transpose(out[:, hcols : 2 * hcols])
            v_s[to, :] = out[:, 2 * hcols : 3 * hcols]

    project(place)
    tok_ring.forward()

    loads[5].wait()
    loads[6].wait()
    size = GROUP
    to_wide = one_hot(iota((experts, wide), 0) == iota((experts, wide), 1) // groups)
    prio = prio_s[...].astype(F32).astype(BF16)
    spread_rows = dotf(one_hot((iota((rows, groups), 0) // size) == iota((rows, groups), 1)), prio)
    at_col = (iota((rows, size), 0) % size) == iota((rows, size), 1)
    prio_col = jnp.sum(jnp.where(at_col, spread_rows, 0.0), axis=1, keepdims=True)
    group_tok = one_hot((iota((groups, rows), 1) // size) == iota((groups, rows), 0))
    spread_cols = dotf(prio, group_tok, ((0,), (0,)))
    at_row = (iota((size, rows), 1) % size) == iota((size, rows), 0)
    prio_row = jnp.sum(jnp.where(at_row, spread_cols, 0.0), axis=0, keepdims=True)
    named = routes_s[0:1, :] == iota((experts, rows), 0)
    for pick in range(1, TOP):
        named = named | (routes_s[pick : pick + 1, :] == iota((experts, rows), 0))
    own_group = (iota((rows, wide), 0) // size) == (iota((rows, wide), 1) % groups)
    member = jnp.where(own_group, dotf(one_hot(named), to_wide, ((0,), (0,))), 0.0)
    rank = dotf(one_hot(prio_row < prio_col), member.astype(BF16))
    kept_s[...] = jnp.where(rank < capacity, member, 0.0).astype(BF16)

    tok_ring.copy(2).wait_recv()
    project(left)
    tok_ring.copy(3).wait_recv()
    project(right)
    for load in loads[7:10]:
        load.wait()
    tok_ring.wait_far()
    wo_ring.start()
    win_ring.start((0, 1))
    project(far)

    prefix = prefix_ref[0]
    block = rows

    def hidden_keys(scores, row0, col0, row_axis):
        if isinstance(row0, int) and col0 + block - 1 <= row0:
            return scores
        row_ids = iota((block, block), row_axis) + row0
        col_ids = iota((block, block), 1 - row_axis) + col0
        seen = col_ids <= row_ids
        if col0 < PREFIX_MOST:
            seen = seen | (col_ids < prefix)
        return jnp.where(seen, scores, NEG)

    def ctx_copy(off):
        to = lax.rem(place + off, TENSOR)
        src = ctx_s.at[block_of(to * rows, rows), :]
        return remote(src, ctx_all.at[place], ctx_sems, off, "tensor", to)

    def attend(row0, seen_rows):
        part_rows = pl.ds(row0, block)
        q = q_s[part_rows, :]
        starts = range(0, seen_rows, block)
        merged = jnp.zeros((block, hcols), F32)
        for head in range(heads):
            q_head = pick_head(q, head)
            scores = []
            for col0 in starts:
                part = dotf(q_head, k_s[col0 : col0 + block, :], ((1,), (1,)))
                scores.append(hidden_keys(part, row0, col0, 0))
            peak = functools.reduce(
                jnp.maximum, [jnp.max(part, axis=1, keepdims=True) for part in scores]
            )
            acc = jnp.zeros((block, hcols), F32)
            for part, col0 in zip(scores, starts):
                soft = jnp.exp(part - peak).astype(BF16)
                acc = acc + dotf(soft, pick_head(v_s[col0 : col0 + block, :], head, 1.0))
            lane = HEAD_DIM if head == 0 else 0
            total = acc[:, lane : lane + 1]
            merged = merged + pick_head(acc * (1.0 / total), head)
            lse = jnp.broadcast_to(peak + jnp.log(total), (block, 128))
            lse_s[8 * head : 8 * head + 8, part_rows] = jnp.transpose(lse)[:8]
        ctx_s[part_rows, :] = merged.astype(BF16)

    def by_length(act, blk):
        short = PREFIX_MOST // block
        pl.when(blk < short)(lambda: act(pl.multiple_of(blk * block, block), PREFIX_MOST))
        for at in range(short, TENSOR):
            pl.when(blk == at)(functools.partial(act, at * block, (at + 1) * block))

    @pl.loop(0, TENSOR)
    def _(turn):
        blk = lax.rem(place + 1 + turn, TENSOR)
        by_length(attend, blk)

        @pl.when(turn < TENSOR - 1)
        def _():
            ctx_copy(turn + 1).start()

        @pl.when(turn == 1)
        def _():
            wo_ring.forward()

    win_ring.start((2, 3))
    win_ring.forward()
    wout_ring.start()
    ctx_all[place] = ctx_s[block_of(place * rows, rows), :]
    for load in loads[10:]:
        load.wait()
    wide_router[...] = dotf(to_wide, router_s[...], ((0,), (0,))).astype(BF16)
    pair_s[:, 0:width] = cot_s[...].astype(BF16)
    wo_ring.wait_near()
    wo_ring.wait_far()
    wo_full = wo_s.reshape(TENSOR * hcols, width)
    for off in (2, 1, 3):
        ctx_copy(off).wait_recv()

    step_rows = 128

    @pl.loop(0, rows // step_rows)
    def _(step):
        part = block_of(step * step_rows, step_rows)
        ctx = jnp.concatenate([ctx_all[at, part, :] for at in range(TENSOR)], axis=1)
        residual = tok_s[place, part].astype(F32) + dotf(ctx, wo_full[...])
        res_s[part, :] = residual
        scaled, spread = norm_parts(residual)
        scaled_s[part, :] = scaled
        spread_s[part, :] = jnp.broadcast_to(spread, (step_rows, 128))
        mixer = (scaled * gain_two[...]).astype(BF16)
        pair_s[part, width : 2 * width] = mixer
        logits = dotf(mixer, wide_router[...], ((1,), (1,)))
        kept = kept_s[part, :].astype(F32)
        terms = jnp.where(kept > 0.0, jnp.exp(logits), 0.0)
        total = jnp.sum(terms, axis=0, keepdims=True)
        count = jnp.sum(kept, axis=0, keepdims=True)
        weight = terms / jnp.where(count > 0.0, total, 1.0)
        weight_s[part, :] = weight
        low_s[part, :] = weight.astype(BF16)

    @pl.loop(0, wide // 128)
    def _(blk):
        mixed = dotf(low_s[:, block_of(blk * 128, 128)], pair_s[...], ((0,), (0,))).astype(BF16)
        count = 128 // groups
        out_s[pl.ds(blk * count, count)] = mixed.reshape(count, groups, 2 * width)

    def mix_copy(off):
        to = lax.rem(me + off, peers)
        return fan(out_s.at[to], in_s.at[off], mix_sems, to, off // batch)

    pl.semaphore_wait(plane_sem, peers // ROW - 1)
    each(1, peers, lambda off: mix_copy(off).start())
    in_s[0] = out_s[me]

    def ret_copy(off):
        to = lax.rem(me + peers - off, peers)
        return fan(done_s.at[off], ret_s.at[me], ret_sems, to)

    def expert_part(chunk, slices, start):
        part = block_of(chunk * 128, 128)
        rows_in = in_s[pl.ds(chunk * batch, batch)].reshape(128, 2 * width)
        grad = rows_in[:, 0:width]
        mixed = rows_in[:, width : 2 * width]
        for at in slices:
            at = lax.rem(place + at, TENSOR)
            pre = dotf(mixed, win_s[at])
            sigma = 1.0 / (1.0 + jnp.exp(-pre))
            hidden = (pre * sigma).astype(BF16)
            grad_hidden = dotf(grad, wout_s[at], ((1,), (1,)))
            grad_pre = (grad_hidden * (sigma * (1.0 + pre * (1.0 - sigma)))).astype(BF16)
            hidden_s[at, part, :] = hidden
            gpre_s[at, part, :] = grad_pre
            returned = dotf(hidden, wout_s[at])
            grad_mixed = dotf(grad_pre, win_s[at], ((1,), (1,)))
            if start:
                acc_s[0, part, :] = returned
                acc_s[1, part, :] = grad_mixed
                start = False
            else:
                acc_s[0, part, :] += returned
                acc_s[1, part, :] += grad_mixed

    win_ring.wait_near()

    @pl.loop(0, peers // batch)
    def _(chunk):

        @pl.when(chunk == 0)
        def _():
            came = in_s.at[pl.ds(1, batch - 1)]
            fan(came, came, mix_sems, lax.rem(me + 1, peers), 0).wait_recv()

        @pl.when(chunk > 0)
        def _():
            came = in_s.at[pl.ds(chunk * batch, batch)]
            fan(came, came, mix_sems, lax.rem(me + 1, peers), chunk).wait_recv()

        expert_part(chunk, (0,), True)

        @pl.when(chunk == 2)
        def _():
            wout_ring.forward()

    wout_ring.wait_near()

    @pl.loop(0, 2 * peers // batch)
    def _(turn):
        expert_part(turn // 2, (3 - 2 * lax.rem(turn, 2),), False)

    win_ring.wait_far()
    wout_ring.wait_far()

    @pl.loop(0, peers // batch)
    def _(chunk):
        expert_part(chunk, (2,), False)
        part = block_of(chunk * 128, 128)
        begin = chunk * batch
        done = jnp.concatenate([acc_s[0, part, :], acc_s[1, part, :]], axis=1).astype(BF16)
        done_s[pl.ds(begin, batch)] = done.reshape(batch, groups, 2 * width)
        each(jnp.maximum(begin, 1), begin + batch, lambda off: ret_copy(off).start())

    ret_s[me] = done_s[0]

    dwin_ring = Scatter(dwin_s, via_win, land_win, dwin_sems, place)
    dwout_ring = Scatter(dwout_s, via_wout, land_wout, dwout_sems, place)

    def expert_grads(off):
        at = lax.rem(place + off, TENSOR)
        rows_in = in_s[...].reshape(wide, 2 * width)
        dwin_s[at] = dotf(rows_in[:, width : 2 * width], gpre_s[at], ((0,), (0,))).astype(BF16)
        dwout_s[at] = dotf(hidden_s[at], rows_in[:, 0:width], ((0,), (0,))).astype(BF16)

    @pl.loop(0, TENSOR)
    def _(turn):
        expert_grads(lax.rem(turn + 2, TENSOR))

        @pl.when(turn == 0)
        def _():
            dwin_ring.start_far()
            dwout_ring.start_far()

    dwin_ring.start_own()
    all_of(ret_s, ret_sems).wait_recv()

    dgain_s[...] = jnp.zeros_like(dgain_s)
    from_wide = one_hot(iota((wide, experts), 0) // groups == iota((wide, experts), 1))

    @pl.loop(0, rows // step_rows)
    def _(step):
        part = block_of(step * step_rows, step_rows)
        came = ret_s[...].reshape(wide, 2 * width)
        low = low_s[part, :]
        weight = weight_s[part, :]
        back = dotf(low, came)
        kept_s[part, :] = (res_s[part, :] + back[:, 0:width]).astype(BF16)
        grad_weight = dotf(pair_s[part, :], came, ((1,), (1,)))
        inner = jnp.sum(weight * grad_weight, axis=0, keepdims=True)
        grad_logits = (weight * (grad_weight - inner)).astype(BF16)
        glog_s[part, :] = dotf(grad_logits, from_wide).astype(BF16)
        grad_mixer = back[:, width : 2 * width] + dotf(grad_logits, wide_router[...])
        scaled = scaled_s[part, :]
        dgain_s[...] += jnp.sum(grad_mixer * scaled, axis=0, keepdims=True)
        grad_scaled = grad_mixer * gain_two[...]
        centered = grad_scaled - jnp.mean(grad_scaled, axis=1, keepdims=True)
        along = jnp.mean(grad_scaled * scaled, axis=1, keepdims=True)
        grad_res = cot_s[part, :] + spread_s[part, 0:1] * (centered - scaled * along)
        res_s[part, :] = grad_res
        grad_att = grad_res.astype(BF16)
        gatt_s[part, :] = grad_att
        grad_ctx = dotf(grad_att, wo_full[...], ((1,), (1,))).astype(BF16)
        for at in range(TENSOR):
            gctx_s[at, part, :] = grad_ctx[:, at * hcols : (at + 1) * hcols]

    def back_copy(off):
        to = lax.rem(place + off, TENSOR)
        dst = gctx_all.at[block_of(place * rows, rows), :]
        return remote(gctx_s.at[to], dst, back_sems, off, "tensor", to)

    for off in (2, 1, 3):
        back_copy(off).start()
    out_store = pltpu.make_async_copy(kept_s, out_ref, store_sems.at[0])
    out_store.start()
    gctx_all[block_of(place * rows, rows), :] = gctx_s[place]

    each_rows = width // peers
    for at in range(TENSOR):
        grad_wo = dotf(ctx_all[at], gatt_s[...], ((0,), (0,))).astype(BF16)
        count = peers // TENSOR
        wop_s[at * count : (at + 1) * count, :, 0:width] = grad_wo.reshape(count, each_rows, width)
    grad_router = dotf(glog_s[...], pair_s[:, width : 2 * width], ((0,), (0,)))
    blocks = width // hcols
    small_rows = jnp.concatenate(
        [grad_router, dgain_s[...], jnp.zeros((width // blocks - experts - 1, width), F32)], axis=0
    ).astype(BF16)
    small_tall = jnp.concatenate(
        [small_rows[:, at * hcols : (at + 1) * hcols] for at in range(blocks)], axis=0
    )
    wop_s[:, :, width : width + hcols] = small_tall.reshape(peers, each_rows, hcols)

    def wop_copy(off):
        to = lax.rem(me + off, peers)
        return fan(wop_s.at[to], wop_in.at[off], wop_sems, to)

    each(1, peers, lambda off: wop_copy(off).start())
    wop_in[0] = wop_s[me]
    dwin_ring.add_far()
    dwout_ring.add_far()

    dk_acc[...] = jnp.zeros_like(dk_acc)
    dv_acc[...] = jnp.zeros_like(dv_acc)
    ones = [pick_head(jnp.ones((8, hcols), F32), head) for head in range(heads)]

    def wopz_copy(off):
        to = lax.rem(place + off, TENSOR)
        return remote(wop_sum.at[place], wop_sum.at[place], wopz_sems, off, "tensor", to)

    def wopb_copy(off):
        to = lax.rem(me + off, peers)
        return fan(wop_all.at[me], wop_all.at[me], wopb_sems, to)

    def attend_back(row0, seen_rows):
        part = pl.ds(row0, block)
        q = q_s[part, :]
        grad = gctx_all[part, :]
        product = grad.astype(F32) * ctx_s[part, :].astype(F32)
        dq = []
        for head in range(heads):
            inner = dotf(ones[head], product, ((1,), (1,)), lax.Precision.HIGHEST)[0:1]
            lse = lse_s[8 * head : 8 * head + 1, part]
            q_head = pick_head(q, head)
            grad_head = pick_head(grad, head)
            dq_head = jnp.zeros((HEAD_DIM, block), F32)
            for col0 in range(0, seen_rows, block):
                keys = pl.ds(col0, block)
                scores = dotf(k_s[keys, :], q_head, ((1,), (1,)))
                soft = jnp.exp(hidden_keys(scores, row0, col0, 1) - lse)
                grad_soft = dotf(v_s[keys, :], grad_head, ((1,), (1,)))
                grad_scores = (soft * (grad_soft - inner)).astype(BF16)
                dv_acc[keys, :] += dotf(soft.astype(BF16), grad_head)
                dk_acc[keys, :] += dotf(grad_scores, q_head)
                dq_head += dotf(kt_s[head * HEAD_DIM : (head + 1) * HEAD_DIM, keys], grad_scores)
            dq.append(dq_head)
        dq = jnp.transpose(jnp.concatenate(dq, axis=0))
        grads_s[part, 0:hcols] = (dq * SCORE_SCALE).astype(BF16)

    @pl.loop(0, TENSOR)
    def _(turn):
        blk = lax.rem(place + turn, TENSOR)

        @pl.when(turn > 0)
        def _():
            back_copy(TENSOR - turn).wait_recv()

        by_length(attend_back, blk)

        @pl.when(turn == 1)
        def _():
            dwin_ring.start_sums()
            dwout_ring.start_own()
            dwout_ring.start_sums()
            all_of(wop_in, wop_sems).wait_recv()
            total = jnp.zeros(wop_sum.shape[1:], F32)
            total = lax.fori_loop(0, peers, lambda off, acc: acc + wop_in[off].astype(F32), total)
            wop_sum[place] = total.astype(BF16)
            for off in (2, 1, 3):
                wopz_copy(off).start()

        @pl.when(turn == 2)
        def _():
            for off in (2, 1, 3):
                wopz_copy(off).wait_recv()
            total = jnp.zeros(wop_sum.shape[1:], F32)
            for at in range(TENSOR):
                total = total + wop_sum[at].astype(F32)
            wop_all[me] = total.astype(BF16)
            each(1, peers, lambda off: wopb_copy(off).start())

    grads_s[:, hcols : 2 * hcols] = dk_acc[...].astype(BF16)
    grads_s[:, 2 * hcols : 3 * hcols] = dv_acc[...].astype(BF16)

    def partial_rows(owner, part):
        start = owner * rows + part * half
        return dotf(grads_s[block_of(start, half), :], w_s[...], ((1,), (1,)))

    row_ring = Scatter(rows_s, via_rows, land_rows, row_sems, place)
    low, high = row_ring.low, row_ring.high
    rows_s[far, low] = partial_rows(far, 0).astype(BF16)
    rows_s[far, high] = partial_rows(far, 1).astype(BF16)
    row_ring.start_far()

    def piece_copy(off):
        to = lax.rem(me + off, peers)
        return fan(piece_s.at[to], piece_in.at[off], piece_sems, to)

    tall = width // ROW
    count = tall // each_rows

    @pl.loop(0, ROW)
    def _(turn):
        at = lax.rem(me // count + turn, ROW)
        grads = dotf(seqt_s[block_of(at * tall, tall), :], grads_s[...]).astype(BF16)
        for kind in range(3):
            piece = grads[:, kind * hcols : (kind + 1) * hcols].reshape(count, each_rows, hcols)
            piece_s[pl.ds(at * count, count), kind] = piece

        def send(to):
            off = lax.rem(to + peers - me, peers)
            pl.when(off > 0)(lambda: piece_copy(off).start())

        each(at * count, (at + 1) * count, send)

    piece_in[0] = piece_s[me]
    rows_s[right, high] = partial_rows(right, 1).astype(BF16)
    rows_s[left, low] = partial_rows(left, 0).astype(BF16)
    row_ring.start_own()
    rows_s[right, low] = partial_rows(right, 0).astype(BF16)
    rows_s[left, high] = partial_rows(left, 1).astype(BF16)
    row_ring.add_far()
    row_ring.start_sums()
    mine_s[low, :] = partial_rows(place, 0)
    mine_s[high, :] = partial_rows(place, 1)

    for ring in (tok_ring, win_ring, wout_ring, wo_ring, dwin_ring):
        ring.drain()
    for off in (2, 1, 3):
        ctx_copy(off).wait_send()
        back_copy(off).wait_send()
        wopz_copy(off).wait_send()
    all_of(out_s, mix_sems).wait_send()
    all_of(done_s, ret_sems).wait_send()
    all_of(wop_s, wop_sems).wait_send()
    all_of(piece_in, piece_sems).wait_recv()
    total = jnp.zeros(piece_in.shape[1:], F32)
    total = lax.fori_loop(0, peers, lambda off, acc: acc + piece_in[off].astype(F32), total)
    sum_all[me] = total.astype(BF16)

    def sum_copy(off):
        to = lax.rem(me + off, peers)
        return fan(sum_all.at[me], sum_all.at[me], sum_sems, to)

    each(1, peers, lambda off: sum_copy(off).start())

    cols = block_of(me * each_rows, each_rows)
    along = jnp.zeros((each_rows, 1), F32)
    for kind in range(3):
        weight = w_s[cols, kind * hcols : (kind + 1) * hcols].astype(F32)
        along = along + jnp.sum(total[kind] * weight, axis=1, keepdims=True)
    first_s[place] = jnp.broadcast_to(along, (each_rows, 128))

    def first_copy(off):
        to = lax.rem(place + off, TENSOR)
        return remote(first_s.at[place], first_s.at[place], first_sems, off, "tensor", to)

    for off in (2, 1, 3):
        first_copy(off).start()

    def gain_copy(off):
        to = lax.rem(me + off, peers)
        return fan(gain_all.at[me], gain_all.at[me], gain_sems, to)

    dwin_ring.wait()
    dwout_ring.wait()
    for at, (ring, part_s) in enumerate(((dwin_ring, dwin_s), (dwout_ring, dwout_s))):
        for part in (low, high):
            acc_s[at, part, :] = part_s[place, part].astype(F32) + ring.landed(part)
    win_store = pltpu.make_async_copy(acc_s.at[0], dwin_ref, store_sems.at[1])
    wout_store = pltpu.make_async_copy(acc_s.at[1], dwout_ref, store_sems.at[2])
    win_store.start()
    wout_store.start()
    all_of(wop_all, wopb_sems).wait_recv()
    all_of(wop_all, wopb_sems).wait_send()
    count = peers // TENSOR
    go_ref[...] = wop_all[pl.ds(place * count, count), :, 0:width].reshape(hcols, width).astype(F32)
    small = wop_all[:, :, width : width + hcols].reshape(width, hcols)
    tall = width // blocks
    kept_rows = (experts + 1 + 15) // 16 * 16
    sums = jnp.concatenate(
        [small[at * tall : at * tall + kept_rows] for at in range(blocks)], axis=1
    ).astype(F32)
    router_ref[...] = sums[0:experts]
    dsecond_ref[...] = sums[experts : experts + 1]

    for off in (2, 1, 3):
        first_copy(off).wait_recv()
    gain_all[me] = first_s[0] + first_s[1] + first_s[2] + first_s[3]
    each(1, peers, lambda off: gain_copy(off).start())

    row_ring.wait()
    for part in (low, high):
        grad_normed = mine_s[part, :] + row_ring.landed(part)
        scaled, spread = norm_parts(tok_s[place, part].astype(F32))
        grad_scaled = grad_normed * gain_one[...]
        centered = grad_scaled - jnp.mean(grad_scaled, axis=1, keepdims=True)
        along = jnp.mean(grad_scaled * scaled, axis=1, keepdims=True)
        scaled_s[part, :] = res_s[part, :] + spread * (centered - scaled * along)
    tok_store = pltpu.make_async_copy(scaled_s, gtok_ref, store_sems.at[3])
    tok_store.start()

    all_of(piece_s, piece_sems).wait_send()
    for off in (2, 1, 3):
        first_copy(off).wait_send()
    dwout_ring.drain()
    row_ring.drain()
    all_of(sum_all, sum_sems).wait_recv()
    for at, grad_ref in enumerate((gq_ref, gk_ref, gv_ref)):
        grad_ref[...] = sum_all[:, at].reshape(width, hcols).astype(F32)
    all_of(gain_all, gain_sems).wait_recv()
    dfirst_ref[...] = jnp.transpose(gain_all[...].reshape(width, 128))[0:1] / gain_one[...]

    all_of(sum_all, sum_sems).wait_send()
    all_of(gain_all, gain_sems).wait_send()
    for store in (out_store, win_store, wout_store, tok_store):
        store.wait()


def layer(prefix, tokens, gain_one, gain_two, wq, wk, wv, wo, router, win, wout, cot, routes, prio):
    rows, width = tokens.shape
    experts = router.shape[0]
    hcols = wq.shape[1]
    fcols = win.shape[1]
    groups = rows // GROUP
    wide = experts * groups
    length = TENSOR * rows
    heads = hcols // HEAD_DIM
    peers = experts
    each_rows = width // peers
    capacity = (5 * GROUP * TOP + 4 * experts - 1) // (4 * experts)

    def dev(shape, kind):
        return jax.ShapeDtypeStruct(shape, kind)

    def low(*shape):
        return pltpu.VMEM(shape, BF16)

    def full(*shape):
        return pltpu.VMEM(shape, F32)

    def sems(count):
        return pltpu.SemaphoreType.DMA((2, count))

    return pl.pallas_call(
        functools.partial(layer_kernel, experts=experts, capacity=float(capacity)),
        out_shape=(
            dev((rows, width), BF16),
            dev((rows, width), F32),
            dev(wq.shape, F32),
            dev(wq.shape, F32),
            dev(wq.shape, F32),
            dev(wo.shape, F32),
            dev((experts, width), F32),
            dev((1, width), F32),
            dev((1, width), F32),
            dev(win.shape, F32),
            dev(wout.shape, F32),
        ),
        in_specs=[SM] + [HB] * 13,
        out_specs=(HB,) * 2 + (VM,) * 7 + (HB,) * 2,
        scratch_shapes=[
            low(TENSOR, rows, width),
            full(1, width),
            full(1, width),
            low(width, 3 * hcols),
            low(TENSOR, hcols, width),
            low(experts, width),
            low(TENSOR, width, fcols),
            low(TENSOR, fcols, width),
            full(rows, width),
            pltpu.VMEM(routes.shape, jnp.int32),
            pltpu.VMEM(prio.shape, jnp.int32),
            low(width, length),
            low(length, hcols),
            low(length, hcols),
            low(hcols, length),
            low(length, hcols),
            low(rows, wide),
            low(length, hcols),
            full(8 * heads, length),
            low(TENSOR, rows, hcols),
            low(wide, width),
            full(rows, width),
            full(rows, width),
            full(rows, 128),
            low(rows, 2 * width),
            full(rows, wide),
            low(rows, wide),
            low(experts, groups, 2 * width),
            low(experts, groups, 2 * width),
            low(experts, groups, 2 * width),
            low(experts, groups, 2 * width),
            full(2, wide, width),
            low(TENSOR, wide, fcols),
            low(TENSOR, wide, fcols),
            low(TENSOR, rows, hcols),
            low(length, hcols),
            low(rows, width),
            low(rows, experts),
            full(1, width),
            low(TENSOR, width, fcols),
            low(TENSOR, fcols, width),
            low(width, fcols),
            low(fcols, width),
            low(2, width, fcols),
            low(2, fcols, width),
            low(peers, each_rows, width + hcols),
            low(peers, each_rows, width + hcols),
            low(TENSOR, each_rows, width + hcols),
            low(peers, each_rows, width + hcols),
            full(length, hcols),
            full(length, hcols),
            low(length, 3 * hcols),
            low(TENSOR, rows, width),
            low(rows, width),
            low(2, rows, width),
            full(rows, width),
            low(peers, 3, each_rows, hcols),
            low(peers, 3, each_rows, hcols),
            low(peers, 3, each_rows, hcols),
            full(TENSOR, each_rows, 128),
            full(peers, each_rows, 128),
            pltpu.SemaphoreType.DMA((13,)),
            pltpu.SemaphoreType.DMA((4,)),
            pltpu.SemaphoreType.REGULAR,
            sems(6),
            sems(6),
            sems(6),
            sems(6),
            sems(TENSOR),
            pltpu.SemaphoreType.DMA((1 + wide // 128,)),
            pltpu.SemaphoreType.DMA((2,)),
            sems(TENSOR),
            sems(6),
            sems(6),
            pltpu.SemaphoreType.DMA((2,)),
            sems(TENSOR),
            pltpu.SemaphoreType.DMA((2,)),
            sems(6),
            pltpu.SemaphoreType.DMA((2,)),
            pltpu.SemaphoreType.DMA((2,)),
            sems(TENSOR),
            pltpu.SemaphoreType.DMA((2,)),
        ],
        compiler_params=pltpu.CompilerParams(
            collective_id=0, has_side_effects=True, vmem_limit_bytes=VMEM_BYTES
        ),
        name="layer",
    )(prefix, tokens, gain_one, gain_two, wq, wk, wv, wo, router, win, wout, cot, routes, prio)


def write_kernel(*refs):
    count = (len(refs) - 2) // 3
    in_sems, out_sems = refs[-2:]
    loads = [
        pltpu.make_async_copy(refs[at], refs[2 * count + at], in_sems.at[at]) for at in range(count)
    ]
    stores = [
        pltpu.make_async_copy(refs[2 * count + at], refs[count + at], out_sems.at[at])
        for at in range(count)
    ]
    for load in loads:
        load.start()
    for load, store in zip(loads, stores):
        load.wait()
        store.start()
    for store in stores:
        store.wait()


def write_out(results):
    count = len(results)
    return pl.pallas_call(
        write_kernel,
        out_shape=tuple(jax.ShapeDtypeStruct(x.shape, x.dtype) for x in results),
        in_specs=[HB] * count,
        out_specs=(HB,) * count,
        scratch_shapes=[pltpu.VMEM(x.shape, x.dtype) for x in results]
        + [pltpu.SemaphoreType.DMA((count,)), pltpu.SemaphoreType.DMA((count,))],
        compiler_params=pltpu.CompilerParams(vmem_limit_bytes=VMEM_BYTES),
        name="write_out",
    )(*results)


def body(
    tokens,
    first_gain,
    second_gain,
    query_weight,
    key_weight,
    value_weight,
    output_weight,
    router_weight,
    expert_in,
    expert_out,
    cotangent,
    routes,
    priority,
    prefix_len,
):
    width = tokens.shape[1]
    results = layer(
        prefix_len,
        tokens,
        first_gain.reshape(1, width),
        second_gain.reshape(1, width),
        query_weight,
        key_weight,
        value_weight,
        output_weight,
        router_weight.T,
        expert_in[0],
        expert_out[0],
        cotangent,
        routes.T,
        priority,
    )
    out, gtok, gq, gk, gv, go, grouter, dsecond, dfirst, dwin, dwout = write_out(results)
    return (
        out,
        gtok,
        dfirst.reshape(width),
        dsecond.reshape(width),
        gq,
        gk,
        gv,
        go,
        grouter.T,
        dwin[None],
        dwout[None],
    )


def solution(mesh):
    in_specs = (
        P(("expert", "tensor"), None),
        P(),
        P(),
        P(None, "tensor"),
        P(None, "tensor"),
        P(None, "tensor"),
        P("tensor", None),
        P(),
        P("expert", None, "tensor"),
        P("expert", "tensor", None),
        P(("expert", "tensor"), None),
        P(("expert", "tensor"), None),
        P(("expert", "tensor"), None),
        P("expert"),
    )
    out_specs = (
        P(("expert", "tensor"), None),
        P(("expert", "tensor"), None),
        P(),
        P(),
        P(None, "tensor"),
        P(None, "tensor"),
        P(None, "tensor"),
        P("tensor", None),
        P(),
        P("expert", None, "tensor"),
        P("expert", "tensor", None),
    )
    return jax.shard_map(body, mesh=mesh, in_specs=in_specs, out_specs=out_specs, check_vma=False)
```

```python
import functools

import jax
import jax.numpy as jnp
from jax import lax
from jax.experimental import pallas as pl
from jax.experimental.pallas import tpu as pltpu
from jax.sharding import PartitionSpec as P

HEAD_DIM = 64
GROUP = 32
TOP = 4
EPS = 1e-05
NEG = -1e30
SCORE_SCALE = HEAD_DIM**-0.5
PREFIX_MOST = 1024
ROW = 8
MESH = pl.DeviceIdType.MESH
VM = pl.BlockSpec(memory_space=pltpu.VMEM)
SM = pl.BlockSpec(memory_space=pltpu.SMEM)
HB = pl.BlockSpec(memory_space=pltpu.HBM)
TENSOR = 4
VMEM_BYTES = 58 << 20
BF16 = jnp.bfloat16
F32 = jnp.float32


def dotf(left, right, dims=((1,), (0,)), precision=None):
    return lax.dot_general(
        left, right, (dims, ((), ())), preferred_element_type=F32, precision=precision
    )


def iota(shape, axis):
    return lax.broadcasted_iota(jnp.int32, shape, axis)


def one_hot(test):
    return jnp.where(test, 1.0, 0.0).astype(BF16)


def norm_parts(values):
    center = values - jnp.mean(values, axis=1, keepdims=True)
    spread = lax.rsqrt(jnp.mean(center * center, axis=1, keepdims=True) + EPS)
    return center * spread, spread


def remote(src, dst, sems, slot, axis, to):
    return pltpu.make_async_remote_copy(
        src_ref=src,
        dst_ref=dst,
        send_sem=sems.at[0, slot],
        recv_sem=sems.at[1, slot],
        device_id={axis: to},
        device_id_type=MESH,
    )


def fan(src, dst, sems, to, lane=0):
    return pltpu.make_async_remote_copy(
        src_ref=src,
        dst_ref=dst,
        send_sem=sems.at[0],
        recv_sem=sems.at[1 + lane],
        device_id={"expert": to},
        device_id_type=MESH,
    )


def greet(peers):
    barrier = pltpu.get_barrier_semaphore()
    place = lax.axis_index("tensor")
    me = lax.axis_index("expert")

    def signal(axis, to):
        pl.semaphore_signal(barrier, inc=1, device_id={axis: to}, device_id_type=MESH)

    for off in range(1, TENSOR):
        signal("tensor", lax.rem(place + off, TENSOR))
    for off in range(1, ROW):
        signal("expert", me // ROW * ROW + lax.rem(me + off, ROW))
    for off in range(ROW, peers, ROW):
        signal("expert", lax.rem(me + off, peers))
    return TENSOR - 1 + ROW - 1 + peers // ROW - 1


def each(first, last, act):
    def one(at, _):
        act(at)
        return 0

    lax.fori_loop(first, last, one, 0)


def block_of(start, size):
    return pl.ds(pl.multiple_of(start, size), size)


def pick_head(values, head, other=0.0):
    lane = iota(values.shape, 1)
    inside = (lane >= head * HEAD_DIM) & (lane < (head + 1) * HEAD_DIM)
    return jnp.where(inside, values, jnp.full_like(values, other))


class Gather:
    def __init__(self, buf, sems, place, eighths=4):
        self.buf, self.sems, self.place = buf, sems, place
        self.right, self.left = lax.rem(place + 1, TENSOR), lax.rem(place + TENSOR - 1, TENSOR)
        size = buf.shape[1]
        cut = size * eighths // 8
        self.low, self.high = pl.ds(0, cut), pl.ds(cut, size - cut)

    def copy(self, slot):
        owner, part, to = (
            (self.place, self.low, self.right),
            (self.place, self.high, self.left),
            (self.place, self.high, self.right),
            (self.place, self.low, self.left),
            (self.left, self.low, self.right),
            (self.right, self.high, self.left),
        )[slot]
        block = self.buf.at[owner, part]
        return remote(block, block, self.sems, slot, "tensor", to)

    def start(self, slots=range(4)):
        for slot in slots:
            self.copy(slot).start()

    def forward(self):
        self.copy(0).wait_recv()
        self.copy(4).start()
        self.copy(1).wait_recv()
        self.copy(5).start()

    def wait_near(self):
        self.copy(2).wait_recv()
        self.copy(3).wait_recv()

    def wait_far(self):
        self.copy(4).wait_recv()
        self.copy(5).wait_recv()

    def drain(self):
        for slot in range(6):
            self.copy(slot).wait_send()


class Scatter:
    def __init__(self, part, via, land, sems, place):
        self.part, self.via, self.land, self.sems, self.place = part, via, land, sems, place
        self.right, self.left = lax.rem(place + 1, TENSOR), lax.rem(place + TENSOR - 1, TENSOR)
        self.far = lax.rem(place + 2, TENSOR)
        half = part.shape[1] // 2
        self.low, self.high = pl.ds(0, half), pl.ds(half, half)

    def copy(self, slot):
        block, half, to, dst = (
            (self.far, self.low, self.right, self.via),
            (self.far, self.high, self.left, self.via),
            (self.right, self.high, self.right, self.land.at[0]),
            (self.left, self.low, self.left, self.land.at[1]),
            (self.right, self.low, self.right, self.land.at[0]),
            (self.left, self.high, self.left, self.land.at[1]),
        )[slot]
        return remote(self.part.at[block, half], dst.at[half], self.sems, slot, "tensor", to)

    def start_far(self):
        self.copy(0).start()
        self.copy(1).start()

    def start_own(self):
        self.copy(2).start()
        self.copy(3).start()

    def add_far(self):
        self.copy(0).wait_recv()
        self.part[self.right, self.low] = (
            self.part[self.right, self.low].astype(F32) + self.via[self.low].astype(F32)
        ).astype(BF16)
        self.copy(1).wait_recv()
        self.part[self.left, self.high] = (
            self.part[self.left, self.high].astype(F32) + self.via[self.high].astype(F32)
        ).astype(BF16)

    def start_sums(self):
        self.copy(4).start()
        self.copy(5).start()

    def wait(self):
        for slot in range(2, 6):
            self.copy(slot).wait_recv()

    def landed(self, rows):
        return self.land[0, rows].astype(F32) + self.land[1, rows].astype(F32)

    def drain(self):
        for slot in range(6):
            self.copy(slot).wait_send()


def layer_kernel(
    prefix_ref,
    tok_hbm,
    gain_one_hbm,
    gain_two_hbm,
    wq_hbm,
    wk_hbm,
    wv_hbm,
    wo_hbm,
    router_hbm,
    win_hbm,
    wout_hbm,
    cot_hbm,
    routes_hbm,
    prio_hbm,
    out_ref,
    gtok_ref,
    gq_ref,
    gk_ref,
    gv_ref,
    go_ref,
    router_ref,
    dsecond_ref,
    dfirst_ref,
    dwin_ref,
    dwout_ref,
    tok_s,
    gain_one,
    gain_two,
    w_s,
    wo_s,
    router_s,
    win_s,
    wout_s,
    cot_s,
    routes_s,
    prio_s,
    seqt_s,
    q_s,
    k_s,
    kt_s,
    v_s,
    kept_s,
    ctx_s,
    lse_s,
    ctx_all,
    wide_router,
    res_s,
    scaled_s,
    spread_s,
    pair_s,
    weight_s,
    low_s,
    out_s,
    in_s,
    done_s,
    ret_s,
    acc_s,
    hidden_s,
    gpre_s,
    gctx_s,
    gctx_all,
    gatt_s,
    glog_s,
    dgain_s,
    dwin_s,
    dwout_s,
    via_win,
    via_wout,
    land_win,
    land_wout,
    wop_s,
    wop_row,
    col_s,
    wop_col,
    wop_sum,
    col_all,
    wop_all,
    dk_acc,
    dv_acc,
    grads_s,
    rows_s,
    via_rows,
    land_rows,
    mine_s,
    piece_s,
    piece_in,
    sum_all,
    first_s,
    gain_all,
    local_sems,
    store_sems,
    plane_sem,
    tok_sems,
    win_sems,
    wout_sems,
    wo_sems,
    ctx_sems,
    mix_sems,
    ret_sems,
    back_sems,
    dwin_sems,
    dwout_sems,
    wop_sems,
    col_sems,
    colb_sems,
    wopz_sems,
    wopb_sems,
    row_sems,
    piece_sems,
    sum_sems,
    first_sems,
    gain_sems,
    *,
    experts,
    capacity,
):
    place = lax.axis_index("tensor")
    me = lax.axis_index("expert")
    right, left = lax.rem(place + 1, TENSOR), lax.rem(place + TENSOR - 1, TENSOR)
    far = lax.rem(place + 2, TENSOR)
    _, rows, width = tok_s.shape
    length, hcols = q_s.shape
    heads = hcols // HEAD_DIM
    groups = rows // GROUP
    wide = experts * groups
    peers = experts
    greeted = greet(peers)

    loads = [
        (tok_hbm, tok_s.at[place]),
        (gain_one_hbm, gain_one),
        (wq_hbm, w_s.at[:, pl.ds(0, hcols)]),
        (wk_hbm, w_s.at[:, pl.ds(hcols, hcols)]),
        (wv_hbm, w_s.at[:, pl.ds(2 * hcols, hcols)]),
        (routes_hbm, routes_s),
        (prio_hbm, prio_s),
        (wo_hbm, wo_s.at[place]),
        (win_hbm, win_s.at[place]),
        (wout_hbm, wout_s.at[place]),
        (gain_two_hbm, gain_two),
        (router_hbm, router_s),
        (cot_hbm, cot_s),
    ]
    loads = [
        pltpu.make_async_copy(src, dst, local_sems.at[at]) for at, (src, dst) in enumerate(loads)
    ]
    for load in loads:
        load.start()

    def all_of(buf, sems):
        most = buf.at[pl.ds(1, buf.shape[0] - 1)]
        return fan(most, most, sems, lax.rem(me + 1, peers))

    batch = 128 // groups

    tok_ring = Gather(tok_s, tok_sems, place)
    win_ring = Gather(win_s, win_sems, place, 4)
    wout_ring = Gather(wout_s, wout_sems, place, 4)
    wo_ring = Gather(wo_s, wo_sems, place)
    loads[0].wait()
    pl.semaphore_wait(pltpu.get_barrier_semaphore(), greeted)
    tok_ring.start()
    for off in range(ROW, peers, ROW):
        to = lax.rem(me + off, peers)
        pl.semaphore_signal(plane_sem, inc=1, device_id={"expert": to}, device_id_type=MESH)
    for load in loads[1:5]:
        load.wait()

    half = rows // 2

    def project(owner):
        @pl.loop(0, rows // 128)
        def _(at):
            start = at * 128
            scaled, _ = norm_parts(tok_s[owner, block_of(start, 128)].astype(F32))
            normed = (scaled * gain_one[...]).astype(BF16)
            to = block_of(owner * rows + start, 128)
            seqt_s[:, to] = jnp.transpose(normed)
            out = dotf(normed, w_s[...]).astype(BF16)
            q_s[to, :] = out[:, 0:hcols] * SCORE_SCALE
            k_s[to, :] = out[:, hcols : 2 * hcols]
            kt_s[:, to] = jnp.transpose(out[:, hcols : 2 * hcols])
            v_s[to, :] = out[:, 2 * hcols : 3 * hcols]

    project(place)
    tok_ring.forward()

    loads[5].wait()
    loads[6].wait()
    size = GROUP
    to_wide = one_hot(iota((experts, wide), 0) == iota((experts, wide), 1) // groups)
    prio = prio_s[...].astype(F32).astype(BF16)
    spread_rows = dotf(one_hot((iota((rows, groups), 0) // size) == iota((rows, groups), 1)), prio)
    at_col = (iota((rows, size), 0) % size) == iota((rows, size), 1)
    prio_col = jnp.sum(jnp.where(at_col, spread_rows, 0.0), axis=1, keepdims=True)
    group_tok = one_hot((iota((groups, rows), 1) // size) == iota((groups, rows), 0))
    spread_cols = dotf(prio, group_tok, ((0,), (0,)))
    at_row = (iota((size, rows), 1) % size) == iota((size, rows), 0)
    prio_row = jnp.sum(jnp.where(at_row, spread_cols, 0.0), axis=0, keepdims=True)
    named = routes_s[0:1, :] == iota((experts, rows), 0)
    for pick in range(1, TOP):
        named = named | (routes_s[pick : pick + 1, :] == iota((experts, rows), 0))
    own_group = (iota((rows, wide), 0) // size) == (iota((rows, wide), 1) % groups)
    member = jnp.where(own_group, dotf(one_hot(named), to_wide, ((0,), (0,))), 0.0)
    rank = dotf(one_hot(prio_row < prio_col), member.astype(BF16))
    kept_s[...] = jnp.where(rank < capacity, member, 0.0).astype(BF16)

    tok_ring.copy(2).wait_recv()
    project(left)
    tok_ring.copy(3).wait_recv()
    project(right)
    for load in loads[7:10]:
        load.wait()
    tok_ring.wait_far()
    wo_ring.start()
    win_ring.start((0, 1))
    project(far)

    prefix = prefix_ref[0]
    block = rows

    def hidden_keys(scores, row0, col0, row_axis):
        if isinstance(row0, int) and col0 + block - 1 <= row0:
            return scores
        row_ids = iota((block, block), row_axis) + row0
        col_ids = iota((block, block), 1 - row_axis) + col0
        seen = col_ids <= row_ids
        if col0 < PREFIX_MOST:
            seen = seen | (col_ids < prefix)
        return jnp.where(seen, scores, NEG)

    def ctx_copy(off):
        to = lax.rem(place + off, TENSOR)
        src = ctx_s.at[block_of(to * rows, rows), :]
        return remote(src, ctx_all.at[place], ctx_sems, off, "tensor", to)

    def attend(row0, seen_rows):
        part_rows = pl.ds(row0, block)
        q = q_s[part_rows, :]
        starts = range(0, seen_rows, block)
        merged = jnp.zeros((block, hcols), F32)
        for head in range(heads):
            q_head = pick_head(q, head)
            scores = []
            for col0 in starts:
                part = dotf(q_head, k_s[col0 : col0 + block, :], ((1,), (1,)))
                scores.append(hidden_keys(part, row0, col0, 0))
            peak = functools.reduce(
                jnp.maximum, [jnp.max(part, axis=1, keepdims=True) for part in scores]
            )
            acc = jnp.zeros((block, hcols), F32)
            for part, col0 in zip(scores, starts):
                soft = jnp.exp(part - peak).astype(BF16)
                acc = acc + dotf(soft, pick_head(v_s[col0 : col0 + block, :], head, 1.0))
            lane = HEAD_DIM if head == 0 else 0
            total = acc[:, lane : lane + 1]
            merged = merged + pick_head(acc * (1.0 / total), head)
            lse = jnp.broadcast_to(peak + jnp.log(total), (block, 128))
            lse_s[8 * head : 8 * head + 8, part_rows] = jnp.transpose(lse)[:8]
        ctx_s[part_rows, :] = merged.astype(BF16)

    def by_length(act, blk):
        short = PREFIX_MOST // block
        pl.when(blk < short)(lambda: act(pl.multiple_of(blk * block, block), PREFIX_MOST))
        for at in range(short, TENSOR):
            pl.when(blk == at)(functools.partial(act, at * block, (at + 1) * block))

    @pl.loop(0, TENSOR)
    def _(turn):
        blk = lax.rem(place + 1 + turn, TENSOR)
        by_length(attend, blk)

        @pl.when(turn < TENSOR - 1)
        def _():
            ctx_copy(turn + 1).start()

        @pl.when(turn == 1)
        def _():
            wo_ring.forward()

    win_ring.start((2, 3))
    win_ring.forward()
    wout_ring.start()
    ctx_all[place] = ctx_s[block_of(place * rows, rows), :]
    for load in loads[10:]:
        load.wait()
    wide_router[...] = dotf(to_wide, router_s[...], ((0,), (0,))).astype(BF16)
    pair_s[:, 0:width] = cot_s[...].astype(BF16)
    wo_ring.wait_near()
    wo_ring.wait_far()
    wo_full = wo_s.reshape(TENSOR * hcols, width)
    for off in (2, 1, 3):
        ctx_copy(off).wait_recv()

    step_rows = 128

    @pl.loop(0, rows // step_rows)
    def _(step):
        part = block_of(step * step_rows, step_rows)
        ctx = jnp.concatenate([ctx_all[at, part, :] for at in range(TENSOR)], axis=1)
        residual = tok_s[place, part].astype(F32) + dotf(ctx, wo_full[...])
        res_s[part, :] = residual
        scaled, spread = norm_parts(residual)
        scaled_s[part, :] = scaled
        spread_s[part, :] = jnp.broadcast_to(spread, (step_rows, 128))
        mixer = (scaled * gain_two[...]).astype(BF16)
        pair_s[part, width : 2 * width] = mixer
        logits = dotf(mixer, wide_router[...], ((1,), (1,)))
        kept = kept_s[part, :].astype(F32)
        terms = jnp.where(kept > 0.0, jnp.exp(logits), 0.0)
        total = jnp.sum(terms, axis=0, keepdims=True)
        count = jnp.sum(kept, axis=0, keepdims=True)
        weight = terms / jnp.where(count > 0.0, total, 1.0)
        weight_s[part, :] = weight
        low_s[part, :] = weight.astype(BF16)

    @pl.loop(0, wide // 128)
    def _(blk):
        mixed = dotf(low_s[:, block_of(blk * 128, 128)], pair_s[...], ((0,), (0,))).astype(BF16)
        count = 128 // groups
        out_s[pl.ds(blk * count, count)] = mixed.reshape(count, groups, 2 * width)

    def mix_copy(off):
        to = lax.rem(me + off, peers)
        return fan(out_s.at[to], in_s.at[off], mix_sems, to, off // batch)

    pl.semaphore_wait(plane_sem, peers // ROW - 1)
    each(1, peers, lambda off: mix_copy(off).start())
    in_s[0] = out_s[me]

    def ret_copy(off):
        to = lax.rem(me + peers - off, peers)
        return fan(done_s.at[off], ret_s.at[me], ret_sems, to)

    def expert_part(chunk, slices, start, count=128):
        part = block_of(chunk * count, count)
        sources = count // groups
        rows_in = in_s[pl.ds(chunk * sources, sources)].reshape(count, 2 * width)
        grad = rows_in[:, 0:width]
        mixed = rows_in[:, width : 2 * width]
        for at in slices:
            at = lax.rem(place + at, TENSOR)
            pre = dotf(mixed, win_s[at])
            sigma = 1.0 / (1.0 + jnp.exp(-pre))
            hidden = (pre * sigma).astype(BF16)
            grad_hidden = dotf(grad, wout_s[at], ((1,), (1,)))
            grad_pre = (grad_hidden * (sigma * (1.0 + pre * (1.0 - sigma)))).astype(BF16)
            hidden_s[at, part, :] = hidden
            gpre_s[at, part, :] = grad_pre
            returned = dotf(hidden, wout_s[at])
            grad_mixed = dotf(grad_pre, win_s[at], ((1,), (1,)))
            if start:
                acc_s[0, part, :] = returned
                acc_s[1, part, :] = grad_mixed
                start = False
            else:
                acc_s[0, part, :] += returned
                acc_s[1, part, :] += grad_mixed

    win_ring.wait_near()

    @pl.loop(0, peers // batch)
    def _(chunk):

        @pl.when(chunk == 0)
        def _():
            came = in_s.at[pl.ds(1, batch - 1)]
            fan(came, came, mix_sems, lax.rem(me + 1, peers), 0).wait_recv()

        @pl.when(chunk > 0)
        def _():
            came = in_s.at[pl.ds(chunk * batch, batch)]
            fan(came, came, mix_sems, lax.rem(me + 1, peers), chunk).wait_recv()

        expert_part(chunk, (0,), True)

        @pl.when(chunk == 2)
        def _():
            wout_ring.forward()

    wout_ring.wait_near()

    @pl.loop(0, peers // batch)
    def _(turn):
        expert_part(turn // 2, (3 - 2 * lax.rem(turn, 2),), False, 256)

    win_ring.wait_far()
    wout_ring.wait_far()

    @pl.loop(0, peers // (2 * batch))
    def _(chunk):
        expert_part(chunk, (2,), False, 256)
        part = block_of(chunk * 256, 256)
        begin = chunk * 2 * batch
        done = jnp.concatenate([acc_s[0, part, :], acc_s[1, part, :]], axis=1).astype(BF16)
        done_s[pl.ds(begin, 2 * batch)] = done.reshape(2 * batch, groups, 2 * width)
        each(jnp.maximum(begin, 1), begin + 2 * batch, lambda off: ret_copy(off).start())

    ret_s[me] = done_s[0]

    dwin_ring = Scatter(dwin_s, via_win, land_win, dwin_sems, place)
    dwout_ring = Scatter(dwout_s, via_wout, land_wout, dwout_sems, place)

    def expert_grads(off):
        at = lax.rem(place + off, TENSOR)
        rows_in = in_s[...].reshape(wide, 2 * width)
        dwin_s[at] = dotf(rows_in[:, width : 2 * width], gpre_s[at], ((0,), (0,))).astype(BF16)
        dwout_s[at] = dotf(hidden_s[at], rows_in[:, 0:width], ((0,), (0,))).astype(BF16)

    @pl.loop(0, TENSOR)
    def _(turn):
        expert_grads(lax.rem(turn + 2, TENSOR))

        @pl.when(turn == 0)
        def _():
            dwin_ring.start_far()
            dwout_ring.start_far()

    dwin_ring.start_own()
    all_of(ret_s, ret_sems).wait_recv()

    dgain_s[...] = jnp.zeros_like(dgain_s)
    from_wide = one_hot(iota((wide, experts), 0) // groups == iota((wide, experts), 1))

    step_rows = 256

    @pl.loop(0, rows // step_rows)
    def _(step):
        part = block_of(step * step_rows, step_rows)
        came = ret_s[...].reshape(wide, 2 * width)
        low = low_s[part, :]
        weight = weight_s[part, :]
        back = dotf(low, came)
        kept_s[part, :] = (res_s[part, :] + back[:, 0:width]).astype(BF16)
        grad_weight = dotf(pair_s[part, :], came, ((1,), (1,)))
        inner = jnp.sum(weight * grad_weight, axis=0, keepdims=True)
        grad_logits = (weight * (grad_weight - inner)).astype(BF16)
        glog_s[part, :] = dotf(grad_logits, from_wide).astype(BF16)
        grad_mixer = back[:, width : 2 * width] + dotf(grad_logits, wide_router[...])
        scaled = scaled_s[part, :]
        dgain_s[...] += jnp.sum(grad_mixer * scaled, axis=0, keepdims=True)
        grad_scaled = grad_mixer * gain_two[...]
        centered = grad_scaled - jnp.mean(grad_scaled, axis=1, keepdims=True)
        along = jnp.mean(grad_scaled * scaled, axis=1, keepdims=True)
        grad_res = cot_s[part, :] + spread_s[part, 0:1] * (centered - scaled * along)
        res_s[part, :] = grad_res
        grad_att = grad_res.astype(BF16)
        gatt_s[part, :] = grad_att
        grad_ctx = dotf(grad_att, wo_full[...], ((1,), (1,))).astype(BF16)
        for at in range(TENSOR):
            gctx_s[at, part, :] = grad_ctx[:, at * hcols : (at + 1) * hcols]

    def back_copy(off):
        to = lax.rem(place + off, TENSOR)
        dst = gctx_all.at[block_of(place * rows, rows), :]
        return remote(gctx_s.at[to], dst, back_sems, off, "tensor", to)

    for off in (3, 2, 1):
        back_copy(off).start()
    dwin_ring.add_far()
    dwin_ring.start_sums()
    out_store = pltpu.make_async_copy(kept_s, out_ref, store_sems.at[0])
    out_store.start()
    gctx_all[block_of(place * rows, rows), :] = gctx_s[place]

    each_rows = width // peers
    for at in range(TENSOR):
        grad_wo = dotf(ctx_all[at], gatt_s[...], ((0,), (0,))).astype(BF16)
        wop_s[:, at, :, 0:width] = grad_wo.reshape(ROW, each_rows, width)
    grad_router = dotf(glog_s[...], pair_s[:, width : 2 * width], ((0,), (0,)))
    blocks = width // hcols
    small_rows = jnp.concatenate(
        [grad_router, dgain_s[...], jnp.zeros((width // blocks - experts - 1, width), F32)], axis=0
    ).astype(BF16)
    for at in range(blocks):
        small = small_rows[:, at * hcols : (at + 1) * hcols]
        wop_s[:, at, :, width : width + hcols] = small.reshape(ROW, each_rows, hcols)

    my_row, my_col = me // ROW, lax.rem(me, ROW)

    def to_row(off, sems, src, dst):
        return fan(src, dst, sems, my_row * ROW + lax.rem(me + off, ROW))

    def wop_copy(off):
        return to_row(off, wop_sems, wop_s.at[lax.rem(me + off, ROW)], wop_row.at[off])

    def col_copy(off):
        to = lax.rem(me + off * ROW, peers)
        return fan(col_s.at[to // ROW], wop_col.at[off], col_sems, to)

    def colb_copy(off):
        to = lax.rem(me + off * ROW, peers)
        return fan(col_all.at[my_row], col_all.at[my_row], colb_sems, to)

    def wopb_copy(off):
        return to_row(off, wopb_sems, col_all, wop_all.at[my_col])

    cols = peers // ROW
    each(1, ROW, lambda off: wop_copy(off).start())
    wop_row[0] = wop_s[my_col]
    dwout_ring.add_far()

    dk_acc[...] = jnp.zeros_like(dk_acc)
    dv_acc[...] = jnp.zeros_like(dv_acc)
    ones = [pick_head(jnp.ones((8, hcols), F32), head) for head in range(heads)]

    def wopz_copy(off):
        to = lax.rem(place + off, TENSOR)
        return remote(wop_sum.at[place], wop_sum.at[place], wopz_sems, off, "tensor", to)

    def attend_back(row0, seen_rows):
        part = pl.ds(row0, block)
        q = q_s[part, :]
        grad = gctx_all[part, :]
        product = grad.astype(F32) * ctx_s[part, :].astype(F32)
        dq = []
        for head in range(heads):
            inner = dotf(ones[head], product, ((1,), (1,)), lax.Precision.HIGHEST)[0:1]
            lse = lse_s[8 * head : 8 * head + 1, part]
            q_head = pick_head(q, head)
            grad_head = pick_head(grad, head)
            dq_head = jnp.zeros((HEAD_DIM, block), F32)
            for col0 in range(0, seen_rows, block):
                keys = pl.ds(col0, block)
                scores = dotf(k_s[keys, :], q_head, ((1,), (1,)))
                soft = jnp.exp(hidden_keys(scores, row0, col0, 1) - lse)
                grad_soft = dotf(v_s[keys, :], grad_head, ((1,), (1,)))
                grad_scores = (soft * (grad_soft - inner)).astype(BF16)
                dv_acc[keys, :] += dotf(soft.astype(BF16), grad_head)
                dk_acc[keys, :] += dotf(grad_scores, q_head)
                dq_head += dotf(kt_s[head * HEAD_DIM : (head + 1) * HEAD_DIM, keys], grad_scores)
            dq.append(dq_head)
        dq = jnp.transpose(jnp.concatenate(dq, axis=0))
        grads_s[part, 0:hcols] = (dq * SCORE_SCALE).astype(BF16)

    @pl.loop(0, TENSOR)
    def _(turn):
        blk = lax.rem(place + turn, TENSOR)

        @pl.when(turn > 0)
        def _():
            back_copy(TENSOR - turn).wait_recv()

        by_length(attend_back, blk)

        @pl.when(turn == 0)
        def _():
            dwout_ring.start_own()
            all_of(wop_row, wop_sems).wait_recv()
            total = jnp.zeros(col_s.shape, F32)
            total = lax.fori_loop(0, ROW, lambda off, acc: acc + wop_row[off].astype(F32), total)
            col_s[...] = total.astype(BF16)
            each(1, cols, lambda off: col_copy(off).start())
            wop_col[0] = col_s[my_row]

        @pl.when(turn == 1)
        def _():
            dwout_ring.start_sums()
            all_of(wop_col, col_sems).wait_recv()
            total = jnp.zeros(wop_sum.shape[1:], F32)
            for at in range(cols):
                total = total + wop_col[at].astype(F32)
            wop_sum[place] = total.astype(BF16)
            for off in (2, 1, 3):
                wopz_copy(off).start()

        @pl.when(turn == 2)
        def _():
            for off in (2, 1, 3):
                wopz_copy(off).wait_recv()
            total = jnp.zeros(wop_sum.shape[1:], F32)
            for at in range(TENSOR):
                total = total + wop_sum[at].astype(F32)
            col_all[my_row] = total.astype(BF16)
            each(1, cols, lambda off: colb_copy(off).start())

        @pl.when(turn == 3)
        def _():
            all_of(col_all, colb_sems).wait_recv()
            each(1, ROW, lambda off: wopb_copy(off).start())
            wop_all[my_col] = col_all[...]

    grads_s[:, hcols : 2 * hcols] = dk_acc[...].astype(BF16)
    grads_s[:, 2 * hcols : 3 * hcols] = dv_acc[...].astype(BF16)

    def partial_rows(owner, part):
        start = owner * rows + part * half
        return dotf(grads_s[block_of(start, half), :], w_s[...], ((1,), (1,)))

    row_ring = Scatter(rows_s, via_rows, land_rows, row_sems, place)
    low, high = row_ring.low, row_ring.high
    rows_s[far, low] = partial_rows(far, 0).astype(BF16)
    rows_s[far, high] = partial_rows(far, 1).astype(BF16)
    row_ring.start_far()

    def piece_copy(off):
        to = lax.rem(me + off, peers)
        return fan(piece_s.at[to], piece_in.at[off], piece_sems, to)

    tall = width // ROW
    count = tall // each_rows

    @pl.loop(0, ROW)
    def _(turn):
        at = lax.rem(me // count + turn, ROW)
        grads = dotf(seqt_s[block_of(at * tall, tall), :], grads_s[...]).astype(BF16)
        for kind in range(3):
            piece = grads[:, kind * hcols : (kind + 1) * hcols].reshape(count, each_rows, hcols)
            piece_s[pl.ds(at * count, count), kind] = piece

        def send(to):
            off = lax.rem(to + peers - me, peers)
            pl.when(off > 0)(lambda: piece_copy(off).start())

        each(at * count, (at + 1) * count, send)

    piece_in[0] = piece_s[me]
    rows_s[right, high] = partial_rows(right, 1).astype(BF16)
    rows_s[left, low] = partial_rows(left, 0).astype(BF16)
    row_ring.start_own()
    rows_s[right, low] = partial_rows(right, 0).astype(BF16)
    rows_s[left, high] = partial_rows(left, 1).astype(BF16)
    row_ring.add_far()
    row_ring.start_sums()
    mine_s[low, :] = partial_rows(place, 0)
    mine_s[high, :] = partial_rows(place, 1)

    for ring in (tok_ring, win_ring, wout_ring, wo_ring, dwin_ring):
        ring.drain()
    for off in (2, 1, 3):
        ctx_copy(off).wait_send()
        back_copy(off).wait_send()
        wopz_copy(off).wait_send()
    all_of(out_s, mix_sems).wait_send()
    all_of(done_s, ret_sems).wait_send()
    all_of(wop_s, wop_sems).wait_send()
    all_of(wop_col, col_sems).wait_send()
    all_of(col_all, colb_sems).wait_send()
    all_of(piece_in, piece_sems).wait_recv()
    total = jnp.zeros(piece_in.shape[1:], F32)
    total = lax.fori_loop(0, peers, lambda off, acc: acc + piece_in[off].astype(F32), total)
    sum_all[me] = total.astype(BF16)

    def sum_copy(off):
        to = lax.rem(me + off, peers)
        return fan(sum_all.at[me], sum_all.at[me], sum_sems, to)

    each(1, peers, lambda off: sum_copy(off).start())

    cols = block_of(me * each_rows, each_rows)
    along = jnp.zeros((each_rows, 1), F32)
    for kind in range(3):
        weight = w_s[cols, kind * hcols : (kind + 1) * hcols].astype(F32)
        along = along + jnp.sum(total[kind] * weight, axis=1, keepdims=True)
    first_s[place] = jnp.broadcast_to(along, (each_rows, 128))

    def first_copy(off):
        to = lax.rem(place + off, TENSOR)
        return remote(first_s.at[place], first_s.at[place], first_sems, off, "tensor", to)

    for off in (2, 1, 3):
        first_copy(off).start()

    def gain_copy(off):
        to = lax.rem(me + off, peers)
        return fan(gain_all.at[me], gain_all.at[me], gain_sems, to)

    dwin_ring.wait()
    dwout_ring.wait()
    for at, (ring, part_s) in enumerate(((dwin_ring, dwin_s), (dwout_ring, dwout_s))):
        for part in (low, high):
            acc_s[at, part, :] = part_s[place, part].astype(F32) + ring.landed(part)
    win_store = pltpu.make_async_copy(acc_s.at[0], dwin_ref, store_sems.at[1])
    wout_store = pltpu.make_async_copy(acc_s.at[1], dwout_ref, store_sems.at[2])
    win_store.start()
    wout_store.start()
    all_of(wop_all, wopb_sems).wait_recv()
    all_of(wop_all, wopb_sems).wait_send()
    go_ref[...] = wop_all[:, place, :, 0:width].reshape(hcols, width).astype(F32)
    kept_rows = (experts + 1 + 15) // 16 * 16
    sums = jnp.concatenate(
        [
            wop_all[:, at, :, width : width + hcols].reshape(ROW * each_rows, hcols)[:kept_rows]
            for at in range(blocks)
        ],
        axis=1,
    ).astype(F32)
    router_ref[...] = sums[0:experts]
    dsecond_ref[...] = sums[experts : experts + 1]

    for off in (2, 1, 3):
        first_copy(off).wait_recv()
    gain_all[me] = first_s[0] + first_s[1] + first_s[2] + first_s[3]
    each(1, peers, lambda off: gain_copy(off).start())

    row_ring.wait()
    for part in (low, high):
        grad_normed = mine_s[part, :] + row_ring.landed(part)
        scaled, spread = norm_parts(tok_s[place, part].astype(F32))
        grad_scaled = grad_normed * gain_one[...]
        centered = grad_scaled - jnp.mean(grad_scaled, axis=1, keepdims=True)
        along = jnp.mean(grad_scaled * scaled, axis=1, keepdims=True)
        scaled_s[part, :] = res_s[part, :] + spread * (centered - scaled * along)
    tok_store = pltpu.make_async_copy(scaled_s, gtok_ref, store_sems.at[3])
    tok_store.start()

    all_of(piece_s, piece_sems).wait_send()
    for off in (2, 1, 3):
        first_copy(off).wait_send()
    dwout_ring.drain()
    row_ring.drain()
    all_of(sum_all, sum_sems).wait_recv()
    for at, grad_ref in enumerate((gq_ref, gk_ref, gv_ref)):
        grad_ref[...] = sum_all[:, at].reshape(width, hcols).astype(F32)
    all_of(gain_all, gain_sems).wait_recv()
    dfirst_ref[...] = jnp.transpose(gain_all[...].reshape(width, 128))[0:1] / gain_one[...]

    all_of(sum_all, sum_sems).wait_send()
    all_of(gain_all, gain_sems).wait_send()
    for store in (out_store, win_store, wout_store, tok_store):
        store.wait()


def layer(prefix, tokens, gain_one, gain_two, wq, wk, wv, wo, router, win, wout, cot, routes, prio):
    rows, width = tokens.shape
    experts = router.shape[0]
    hcols = wq.shape[1]
    fcols = win.shape[1]
    groups = rows // GROUP
    wide = experts * groups
    length = TENSOR * rows
    heads = hcols // HEAD_DIM
    peers = experts
    each_rows = width // peers
    capacity = (5 * GROUP * TOP + 4 * experts - 1) // (4 * experts)

    def dev(shape, kind):
        return jax.ShapeDtypeStruct(shape, kind)

    def low(*shape):
        return pltpu.VMEM(shape, BF16)

    def full(*shape):
        return pltpu.VMEM(shape, F32)

    def sems(count):
        return pltpu.SemaphoreType.DMA((2, count))

    return pl.pallas_call(
        functools.partial(layer_kernel, experts=experts, capacity=float(capacity)),
        out_shape=(
            dev((rows, width), BF16),
            dev((rows, width), F32),
            dev(wq.shape, F32),
            dev(wq.shape, F32),
            dev(wq.shape, F32),
            dev(wo.shape, F32),
            dev((experts, width), F32),
            dev((1, width), F32),
            dev((1, width), F32),
            dev(win.shape, F32),
            dev(wout.shape, F32),
        ),
        in_specs=[SM] + [HB] * 13,
        out_specs=(HB,) * 2 + (VM,) * 7 + (HB,) * 2,
        scratch_shapes=[
            low(TENSOR, rows, width),
            full(1, width),
            full(1, width),
            low(width, 3 * hcols),
            low(TENSOR, hcols, width),
            low(experts, width),
            low(TENSOR, width, fcols),
            low(TENSOR, fcols, width),
            full(rows, width),
            pltpu.VMEM(routes.shape, jnp.int32),
            pltpu.VMEM(prio.shape, jnp.int32),
            low(width, length),
            low(length, hcols),
            low(length, hcols),
            low(hcols, length),
            low(length, hcols),
            low(rows, wide),
            low(length, hcols),
            full(8 * heads, length),
            low(TENSOR, rows, hcols),
            low(wide, width),
            full(rows, width),
            full(rows, width),
            full(rows, 128),
            low(rows, 2 * width),
            full(rows, wide),
            low(rows, wide),
            low(experts, groups, 2 * width),
            low(experts, groups, 2 * width),
            low(experts, groups, 2 * width),
            low(experts, groups, 2 * width),
            full(2, wide, width),
            low(TENSOR, wide, fcols),
            low(TENSOR, wide, fcols),
            low(TENSOR, rows, hcols),
            low(length, hcols),
            low(rows, width),
            low(rows, experts),
            full(1, width),
            low(TENSOR, width, fcols),
            low(TENSOR, fcols, width),
            low(width, fcols),
            low(fcols, width),
            low(2, width, fcols),
            low(2, fcols, width),
            low(ROW, peers // ROW, each_rows, width + hcols),
            low(ROW, peers // ROW, each_rows, width + hcols),
            low(peers // ROW, each_rows, width + hcols),
            low(peers // ROW, each_rows, width + hcols),
            low(TENSOR, each_rows, width + hcols),
            low(peers // ROW, each_rows, width + hcols),
            low(ROW, peers // ROW, each_rows, width + hcols),
            full(length, hcols),
            full(length, hcols),
            low(length, 3 * hcols),
            low(TENSOR, rows, width),
            low(rows, width),
            low(2, rows, width),
            full(rows, width),
            low(peers, 3, each_rows, hcols),
            low(peers, 3, each_rows, hcols),
            low(peers, 3, each_rows, hcols),
            full(TENSOR, each_rows, 128),
            full(peers, each_rows, 128),
            pltpu.SemaphoreType.DMA((13,)),
            pltpu.SemaphoreType.DMA((4,)),
            pltpu.SemaphoreType.REGULAR,
            sems(6),
            sems(6),
            sems(6),
            sems(6),
            sems(TENSOR),
            pltpu.SemaphoreType.DMA((1 + wide // 128,)),
            pltpu.SemaphoreType.DMA((2,)),
            sems(TENSOR),
            sems(6),
            sems(6),
            pltpu.SemaphoreType.DMA((2,)),
            pltpu.SemaphoreType.DMA((2,)),
            pltpu.SemaphoreType.DMA((2,)),
            sems(TENSOR),
            pltpu.SemaphoreType.DMA((2,)),
            sems(6),
            pltpu.SemaphoreType.DMA((2,)),
            pltpu.SemaphoreType.DMA((2,)),
            sems(TENSOR),
            pltpu.SemaphoreType.DMA((2,)),
        ],
        compiler_params=pltpu.CompilerParams(
            collective_id=0, has_side_effects=True, vmem_limit_bytes=VMEM_BYTES
        ),
        name="layer",
    )(prefix, tokens, gain_one, gain_two, wq, wk, wv, wo, router, win, wout, cot, routes, prio)


def write_kernel(*refs):
    count = (len(refs) - 2) // 3
    in_sems, out_sems = refs[-2:]
    loads = [
        pltpu.make_async_copy(refs[at], refs[2 * count + at], in_sems.at[at]) for at in range(count)
    ]
    stores = [
        pltpu.make_async_copy(refs[2 * count + at], refs[count + at], out_sems.at[at])
        for at in range(count)
    ]
    for load in loads:
        load.start()
    for load, store in zip(loads, stores):
        load.wait()
        store.start()
    for store in stores:
        store.wait()


def write_out(results):
    count = len(results)
    return pl.pallas_call(
        write_kernel,
        out_shape=tuple(jax.ShapeDtypeStruct(x.shape, x.dtype) for x in results),
        in_specs=[HB] * count,
        out_specs=(HB,) * count,
        scratch_shapes=[pltpu.VMEM(x.shape, x.dtype) for x in results]
        + [pltpu.SemaphoreType.DMA((count,)), pltpu.SemaphoreType.DMA((count,))],
        compiler_params=pltpu.CompilerParams(vmem_limit_bytes=VMEM_BYTES),
        name="write_out",
    )(*results)


def body(
    tokens,
    first_gain,
    second_gain,
    query_weight,
    key_weight,
    value_weight,
    output_weight,
    router_weight,
    expert_in,
    expert_out,
    cotangent,
    routes,
    priority,
    prefix_len,
):
    width = tokens.shape[1]
    results = layer(
        prefix_len,
        tokens,
        first_gain.reshape(1, width),
        second_gain.reshape(1, width),
        query_weight,
        key_weight,
        value_weight,
        output_weight,
        router_weight.T,
        expert_in[0],
        expert_out[0],
        cotangent,
        routes.T,
        priority,
    )
    out, gtok, gq, gk, gv, go, grouter, dsecond, dfirst, dwin, dwout = write_out(results)
    return (
        out,
        gtok,
        dfirst.reshape(width),
        dsecond.reshape(width),
        gq,
        gk,
        gv,
        go,
        grouter.T,
        dwin[None],
        dwout[None],
    )


def solution(mesh):
    in_specs = (
        P(("expert", "tensor"), None),
        P(),
        P(),
        P(None, "tensor"),
        P(None, "tensor"),
        P(None, "tensor"),
        P("tensor", None),
        P(),
        P("expert", None, "tensor"),
        P("expert", "tensor", None),
        P(("expert", "tensor"), None),
        P(("expert", "tensor"), None),
        P(("expert", "tensor"), None),
        P("expert"),
    )
    out_specs = (
        P(("expert", "tensor"), None),
        P(("expert", "tensor"), None),
        P(),
        P(),
        P(None, "tensor"),
        P(None, "tensor"),
        P(None, "tensor"),
        P("tensor", None),
        P(),
        P("expert", None, "tensor"),
        P("expert", "tensor", None),
    )
    return jax.shard_map(body, mesh=mesh, in_specs=in_specs, out_specs=out_specs, check_vma=False)
```

```python
import functools

import jax
import jax.numpy as jnp
from jax import lax
from jax.experimental import pallas as pl
from jax.experimental.pallas import tpu as pltpu
from jax.sharding import PartitionSpec as P

HEAD_DIM = 64
GROUP = 32
TOP = 4
EPS = 1e-05
NEG = -1e30
SCORE_SCALE = HEAD_DIM**-0.5
PREFIX_MOST = 1024
ROW = 8
MESH = pl.DeviceIdType.MESH
VM = pl.BlockSpec(memory_space=pltpu.VMEM)
SM = pl.BlockSpec(memory_space=pltpu.SMEM)
HB = pl.BlockSpec(memory_space=pltpu.HBM)
TENSOR = 4
VMEM_BYTES = 58 << 20
BF16 = jnp.bfloat16
F32 = jnp.float32


def dotf(left, right, dims=((1,), (0,)), precision=None):
    return lax.dot_general(
        left, right, (dims, ((), ())), preferred_element_type=F32, precision=precision
    )


def iota(shape, axis):
    return lax.broadcasted_iota(jnp.int32, shape, axis)


def one_hot(test):
    return jnp.where(test, 1.0, 0.0).astype(BF16)


def norm_parts(values):
    center = values - jnp.mean(values, axis=1, keepdims=True)
    spread = lax.rsqrt(jnp.mean(center * center, axis=1, keepdims=True) + EPS)
    return center * spread, spread


def remote(src, dst, sems, slot, axis, to):
    return pltpu.make_async_remote_copy(
        src_ref=src,
        dst_ref=dst,
        send_sem=sems.at[0, slot],
        recv_sem=sems.at[1, slot],
        device_id={axis: to},
        device_id_type=MESH,
    )


def fan(src, dst, sems, to, lane=0):
    return pltpu.make_async_remote_copy(
        src_ref=src,
        dst_ref=dst,
        send_sem=sems.at[0],
        recv_sem=sems.at[1 + lane],
        device_id={"expert": to},
        device_id_type=MESH,
    )


def greet(peers):
    barrier = pltpu.get_barrier_semaphore()
    place = lax.axis_index("tensor")
    me = lax.axis_index("expert")

    def signal(axis, to):
        pl.semaphore_signal(barrier, inc=1, device_id={axis: to}, device_id_type=MESH)

    for off in range(1, TENSOR):
        signal("tensor", lax.rem(place + off, TENSOR))
    for off in range(1, ROW):
        signal("expert", me // ROW * ROW + lax.rem(me + off, ROW))
    for off in range(ROW, peers, ROW):
        signal("expert", lax.rem(me + off, peers))
    return TENSOR - 1 + ROW - 1 + peers // ROW - 1


def each(first, last, act):
    def one(at, _):
        act(at)
        return 0

    lax.fori_loop(first, last, one, 0)


def block_of(start, size):
    return pl.ds(pl.multiple_of(start, size), size)


def pick_head(values, head, other=0.0):
    lane = iota(values.shape, 1)
    inside = (lane >= head * HEAD_DIM) & (lane < (head + 1) * HEAD_DIM)
    return jnp.where(inside, values, jnp.full_like(values, other))


class Gather:
    def __init__(self, buf, sems, place, eighths=4):
        self.buf, self.sems, self.place = buf, sems, place
        self.right, self.left = lax.rem(place + 1, TENSOR), lax.rem(place + TENSOR - 1, TENSOR)
        size = buf.shape[1]
        cut = size * eighths // 8
        self.low, self.high = pl.ds(0, cut), pl.ds(cut, size - cut)

    def copy(self, slot):
        owner, part, to = (
            (self.place, self.low, self.right),
            (self.place, self.high, self.left),
            (self.place, self.high, self.right),
            (self.place, self.low, self.left),
            (self.left, self.low, self.right),
            (self.right, self.high, self.left),
        )[slot]
        block = self.buf.at[owner, part]
        return remote(block, block, self.sems, slot, "tensor", to)

    def start(self, slots=range(4)):
        for slot in slots:
            self.copy(slot).start()

    def forward(self):
        self.copy(0).wait_recv()
        self.copy(4).start()
        self.copy(1).wait_recv()
        self.copy(5).start()

    def wait_near(self):
        self.copy(2).wait_recv()
        self.copy(3).wait_recv()

    def wait_far(self):
        self.copy(4).wait_recv()
        self.copy(5).wait_recv()

    def drain(self):
        for slot in range(6):
            self.copy(slot).wait_send()


class Scatter:
    def __init__(self, part, via, land, sems, place):
        self.part, self.via, self.land, self.sems, self.place = part, via, land, sems, place
        self.right, self.left = lax.rem(place + 1, TENSOR), lax.rem(place + TENSOR - 1, TENSOR)
        self.far = lax.rem(place + 2, TENSOR)
        half = part.shape[1] // 2
        self.low, self.high = pl.ds(0, half), pl.ds(half, half)

    def copy(self, slot):
        block, half, to, dst = (
            (self.far, self.low, self.right, self.via),
            (self.far, self.high, self.left, self.via),
            (self.right, self.high, self.right, self.land.at[0]),
            (self.left, self.low, self.left, self.land.at[1]),
            (self.right, self.low, self.right, self.land.at[0]),
            (self.left, self.high, self.left, self.land.at[1]),
        )[slot]
        return remote(self.part.at[block, half], dst.at[half], self.sems, slot, "tensor", to)

    def start_far(self):
        self.copy(0).start()
        self.copy(1).start()

    def start_own(self):
        self.copy(2).start()
        self.copy(3).start()

    def add_far(self):
        self.copy(0).wait_recv()
        self.part[self.right, self.low] = (
            self.part[self.right, self.low].astype(F32) + self.via[self.low].astype(F32)
        ).astype(BF16)
        self.copy(1).wait_recv()
        self.part[self.left, self.high] = (
            self.part[self.left, self.high].astype(F32) + self.via[self.high].astype(F32)
        ).astype(BF16)

    def start_sums(self):
        self.copy(4).start()
        self.copy(5).start()

    def wait(self):
        for slot in range(2, 6):
            self.copy(slot).wait_recv()

    def landed(self, rows):
        return self.land[0, rows].astype(F32) + self.land[1, rows].astype(F32)

    def drain(self):
        for slot in range(6):
            self.copy(slot).wait_send()


def layer_kernel(
    prefix_ref,
    tok_hbm,
    gain_one_hbm,
    gain_two_hbm,
    wq_hbm,
    wk_hbm,
    wv_hbm,
    wo_hbm,
    router_hbm,
    win_hbm,
    wout_hbm,
    cot_hbm,
    routes_hbm,
    prio_hbm,
    out_ref,
    gtok_ref,
    gq_ref,
    gk_ref,
    gv_ref,
    go_ref,
    router_ref,
    dsecond_ref,
    dfirst_ref,
    dwin_ref,
    dwout_ref,
    tok_s,
    gain_one,
    gain_two,
    w_s,
    wo_s,
    router_s,
    win_s,
    wout_s,
    cot_s,
    routes_s,
    prio_s,
    seqt_s,
    q_s,
    k_s,
    kt_s,
    v_s,
    kept_s,
    ctx_s,
    lse_s,
    ctx_all,
    wide_router,
    res_s,
    scaled_s,
    spread_s,
    pair_s,
    weight_s,
    low_s,
    out_s,
    in_s,
    done_s,
    ret_s,
    acc_s,
    hidden_s,
    gpre_s,
    gctx_s,
    gctx_all,
    gatt_s,
    glog_s,
    dgain_s,
    dwin_s,
    dwout_s,
    via_win,
    via_wout,
    land_win,
    land_wout,
    wop_s,
    wop_row,
    col_s,
    wop_col,
    wop_sum,
    col_all,
    wop_all,
    dk_acc,
    dv_acc,
    grads_s,
    rows_s,
    via_rows,
    land_rows,
    mine_s,
    piece_s,
    piece_in,
    sum_all,
    first_s,
    gain_all,
    local_sems,
    store_sems,
    plane_sem,
    tok_sems,
    win_sems,
    wout_sems,
    wo_sems,
    ctx_sems,
    mix_sems,
    ret_sems,
    back_sems,
    dwin_sems,
    dwout_sems,
    wop_sems,
    col_sems,
    colb_sems,
    wopz_sems,
    wopb_sems,
    row_sems,
    piece_sems,
    sum_sems,
    first_sems,
    gain_sems,
    *,
    experts,
    capacity,
):
    place = lax.axis_index("tensor")
    me = lax.axis_index("expert")
    right, left = lax.rem(place + 1, TENSOR), lax.rem(place + TENSOR - 1, TENSOR)
    far = lax.rem(place + 2, TENSOR)
    _, rows, width = tok_s.shape
    length, hcols = q_s.shape
    heads = hcols // HEAD_DIM
    groups = rows // GROUP
    wide = experts * groups
    peers = experts
    greeted = greet(peers)

    loads = [
        (tok_hbm, tok_s.at[place]),
        (gain_one_hbm, gain_one),
        (wq_hbm, w_s.at[:, pl.ds(0, hcols)]),
        (wk_hbm, w_s.at[:, pl.ds(hcols, hcols)]),
        (wv_hbm, w_s.at[:, pl.ds(2 * hcols, hcols)]),
        (routes_hbm, routes_s),
        (prio_hbm, prio_s),
        (wo_hbm, wo_s.at[place]),
        (win_hbm, win_s.at[place]),
        (wout_hbm, wout_s.at[place]),
        (gain_two_hbm, gain_two),
        (router_hbm, router_s),
        (cot_hbm, cot_s),
    ]
    loads = [
        pltpu.make_async_copy(src, dst, local_sems.at[at]) for at, (src, dst) in enumerate(loads)
    ]
    for load in loads:
        load.start()

    def all_of(buf, sems):
        most = buf.at[pl.ds(1, buf.shape[0] - 1)]
        return fan(most, most, sems, lax.rem(me + 1, peers))

    batch = 128 // groups

    tok_ring = Gather(tok_s, tok_sems, place)
    win_ring = Gather(win_s, win_sems, place, 4)
    wout_ring = Gather(wout_s, wout_sems, place, 4)
    wo_ring = Gather(wo_s, wo_sems, place)
    loads[0].wait()
    pl.semaphore_wait(pltpu.get_barrier_semaphore(), greeted)
    tok_ring.start()
    for off in range(ROW, peers, ROW):
        to = lax.rem(me + off, peers)
        pl.semaphore_signal(plane_sem, inc=1, device_id={"expert": to}, device_id_type=MESH)
    for load in loads[1:5]:
        load.wait()

    half = rows // 2

    def project(owner):
        @pl.loop(0, rows // 128)
        def _(at):
            start = at * 128
            scaled, _ = norm_parts(tok_s[owner, block_of(start, 128)].astype(F32))
            normed = (scaled * gain_one[...]).astype(BF16)
            to = block_of(owner * rows + start, 128)
            seqt_s[:, to] = jnp.transpose(normed)
            out = dotf(normed, w_s[...]).astype(BF16)
            q_s[to, :] = out[:, 0:hcols] * SCORE_SCALE
            k_s[to, :] = out[:, hcols : 2 * hcols]
            kt_s[:, to] = jnp.transpose(out[:, hcols : 2 * hcols])
            v_s[to, :] = out[:, 2 * hcols : 3 * hcols]

    project(place)
    tok_ring.forward()

    loads[5].wait()
    loads[6].wait()
    size = GROUP
    to_wide = one_hot(iota((experts, wide), 0) == iota((experts, wide), 1) // groups)
    prio = prio_s[...].astype(F32).astype(BF16)
    spread_rows = dotf(one_hot((iota((rows, groups), 0) // size) == iota((rows, groups), 1)), prio)
    at_col = (iota((rows, size), 0) % size) == iota((rows, size), 1)
    prio_col = jnp.sum(jnp.where(at_col, spread_rows, 0.0), axis=1, keepdims=True)
    group_tok = one_hot((iota((groups, rows), 1) // size) == iota((groups, rows), 0))
    spread_cols = dotf(prio, group_tok, ((0,), (0,)))
    at_row = (iota((size, rows), 1) % size) == iota((size, rows), 0)
    prio_row = jnp.sum(jnp.where(at_row, spread_cols, 0.0), axis=0, keepdims=True)
    named = routes_s[0:1, :] == iota((experts, rows), 0)
    for pick in range(1, TOP):
        named = named | (routes_s[pick : pick + 1, :] == iota((experts, rows), 0))
    own_group = (iota((rows, wide), 0) // size) == (iota((rows, wide), 1) % groups)
    member = jnp.where(own_group, dotf(one_hot(named), to_wide, ((0,), (0,))), 0.0)
    rank = dotf(one_hot(prio_row < prio_col), member.astype(BF16))
    kept_s[...] = jnp.where(rank < capacity, member, 0.0).astype(BF16)

    tok_ring.copy(2).wait_recv()
    project(left)
    tok_ring.copy(3).wait_recv()
    project(right)
    for load in loads[7:10]:
        load.wait()
    tok_ring.wait_far()
    wo_ring.start()
    win_ring.start((0, 1))
    project(far)

    prefix = prefix_ref[0]
    block = rows

    def hidden_keys(scores, row0, col0, row_axis):
        if isinstance(row0, int) and col0 + block - 1 <= row0:
            return scores
        line = (block, 1) if row_axis == 0 else (1, block)
        until = iota(line, row_axis) + (row0 + 1 - col0)
        if col0 < PREFIX_MOST:
            until = jnp.maximum(until, prefix - col0)
        seen = iota((block, block), 1 - row_axis) < until
        return jnp.where(seen, scores, NEG)

    def ctx_copy(off):
        to = lax.rem(place + off, TENSOR)
        src = ctx_s.at[block_of(to * rows, rows), :]
        return remote(src, ctx_all.at[place], ctx_sems, off, "tensor", to)

    def attend(row0, seen_rows):
        part_rows = pl.ds(row0, block)
        q = q_s[part_rows, :]
        starts = range(0, seen_rows, block)
        merged = jnp.zeros((block, hcols), F32)
        for head in range(heads):
            q_head = pick_head(q, head)
            scores = []
            for col0 in starts:
                part = dotf(q_head, k_s[col0 : col0 + block, :], ((1,), (1,)))
                scores.append(hidden_keys(part, row0, col0, 0))
            peak = functools.reduce(
                jnp.maximum, [jnp.max(part, axis=1, keepdims=True) for part in scores]
            )
            acc = jnp.zeros((block, hcols), F32)
            for part, col0 in zip(scores, starts):
                soft = jnp.exp(part - peak).astype(BF16)
                acc = acc + dotf(soft, pick_head(v_s[col0 : col0 + block, :], head, 1.0))
            lane = HEAD_DIM if head == 0 else 0
            total = acc[:, lane : lane + 1]
            merged = merged + pick_head(acc * (1.0 / total), head)
            lse = jnp.broadcast_to(peak + jnp.log(total), (block, 128))
            lse_s[8 * head : 8 * head + 8, part_rows] = jnp.transpose(lse)[:8]
        ctx_s[part_rows, :] = merged.astype(BF16)

    def by_length(act, blk):
        short = PREFIX_MOST // block
        pl.when(blk < short)(lambda: act(pl.multiple_of(blk * block, block), PREFIX_MOST))
        for at in range(short, TENSOR):
            pl.when(blk == at)(functools.partial(act, at * block, (at + 1) * block))

    @pl.loop(0, TENSOR)
    def _(turn):
        blk = lax.rem(place + 1 + turn, TENSOR)
        by_length(attend, blk)

        @pl.when(turn < TENSOR - 1)
        def _():
            ctx_copy(turn + 1).start()

        @pl.when(turn == 1)
        def _():
            wo_ring.forward()

    win_ring.start((2, 3))
    win_ring.forward()
    wout_ring.start()
    ctx_all[place] = ctx_s[block_of(place * rows, rows), :]
    for load in loads[10:]:
        load.wait()
    wide_router[...] = dotf(to_wide, router_s[...], ((0,), (0,))).astype(BF16)
    pair_s[:, 0:width] = cot_s[...].astype(BF16)
    wo_ring.wait_near()
    wo_ring.wait_far()
    wo_full = wo_s.reshape(TENSOR * hcols, width)
    for off in (2, 1, 3):
        ctx_copy(off).wait_recv()

    step_rows = 128

    @pl.loop(0, rows // step_rows)
    def _(step):
        part = block_of(step * step_rows, step_rows)
        ctx = jnp.concatenate([ctx_all[at, part, :] for at in range(TENSOR)], axis=1)
        residual = tok_s[place, part].astype(F32) + dotf(ctx, wo_full[...])
        res_s[part, :] = residual
        scaled, spread = norm_parts(residual)
        scaled_s[part, :] = scaled
        spread_s[part, :] = jnp.broadcast_to(spread, (step_rows, 128))
        mixer = (scaled * gain_two[...]).astype(BF16)
        pair_s[part, width : 2 * width] = mixer
        logits = dotf(mixer, wide_router[...], ((1,), (1,)))
        kept = kept_s[part, :].astype(F32)
        terms = jnp.where(kept > 0.0, jnp.exp(logits), 0.0)
        total = jnp.sum(terms, axis=0, keepdims=True)
        count = jnp.sum(kept, axis=0, keepdims=True)
        weight = terms / jnp.where(count > 0.0, total, 1.0)
        weight_s[part, :] = weight
        low_s[part, :] = weight.astype(BF16)

    @pl.loop(0, wide // 128)
    def _(blk):
        mixed = dotf(low_s[:, block_of(blk * 128, 128)], pair_s[...], ((0,), (0,))).astype(BF16)
        count = 128 // groups
        out_s[pl.ds(blk * count, count)] = mixed.reshape(count, groups, 2 * width)

    def mix_copy(off):
        to = lax.rem(me + off, peers)
        return fan(out_s.at[to], in_s.at[off], mix_sems, to, off // batch)

    pl.semaphore_wait(plane_sem, peers // ROW - 1)
    each(1, peers, lambda off: mix_copy(off).start())
    in_s[0] = out_s[me]

    def ret_copy(off):
        to = lax.rem(me + peers - off, peers)
        return fan(done_s.at[off], ret_s.at[me], ret_sems, to)

    def expert_part(chunk, slices, start, count=128):
        part = block_of(chunk * count, count)
        sources = count // groups
        rows_in = in_s[pl.ds(chunk * sources, sources)].reshape(count, 2 * width)
        grad = rows_in[:, 0:width]
        mixed = rows_in[:, width : 2 * width]
        for at in slices:
            at = lax.rem(place + at, TENSOR)
            pre = dotf(mixed, win_s[at])
            sigma = 1.0 / (1.0 + jnp.exp(-pre))
            hidden = (pre * sigma).astype(BF16)
            grad_hidden = dotf(grad, wout_s[at], ((1,), (1,)))
            grad_pre = (grad_hidden * (sigma * (1.0 + pre * (1.0 - sigma)))).astype(BF16)
            hidden_s[at, part, :] = hidden
            gpre_s[at, part, :] = grad_pre
            returned = dotf(hidden, wout_s[at])
            grad_mixed = dotf(grad_pre, win_s[at], ((1,), (1,)))
            if start:
                acc_s[0, part, :] = returned
                acc_s[1, part, :] = grad_mixed
                start = False
            else:
                acc_s[0, part, :] += returned
                acc_s[1, part, :] += grad_mixed

    win_ring.wait_near()

    @pl.loop(0, peers // batch)
    def _(chunk):

        @pl.when(chunk == 0)
        def _():
            came = in_s.at[pl.ds(1, batch - 1)]
            fan(came, came, mix_sems, lax.rem(me + 1, peers), 0).wait_recv()

        @pl.when(chunk > 0)
        def _():
            came = in_s.at[pl.ds(chunk * batch, batch)]
            fan(came, came, mix_sems, lax.rem(me + 1, peers), chunk).wait_recv()

        expert_part(chunk, (0,), True)

        @pl.when(chunk == 2)
        def _():
            wout_ring.forward()

    wout_ring.wait_near()

    @pl.loop(0, peers // batch)
    def _(turn):
        expert_part(turn // 2, (3 - 2 * lax.rem(turn, 2),), False, 256)

    win_ring.wait_far()
    wout_ring.wait_far()

    @pl.loop(0, peers // (2 * batch))
    def _(chunk):
        expert_part(chunk, (2,), False, 256)
        part = block_of(chunk * 256, 256)
        begin = chunk * 2 * batch
        done = jnp.concatenate([acc_s[0, part, :], acc_s[1, part, :]], axis=1).astype(BF16)
        done_s[pl.ds(begin, 2 * batch)] = done.reshape(2 * batch, groups, 2 * width)
        each(jnp.maximum(begin, 1), begin + 2 * batch, lambda off: ret_copy(off).start())

    ret_s[me] = done_s[0]

    dwin_ring = Scatter(dwin_s, via_win, land_win, dwin_sems, place)
    dwout_ring = Scatter(dwout_s, via_wout, land_wout, dwout_sems, place)

    def expert_grads(off):
        at = lax.rem(place + off, TENSOR)
        rows_in = in_s[...].reshape(wide, 2 * width)
        dwin_s[at] = dotf(rows_in[:, width : 2 * width], gpre_s[at], ((0,), (0,))).astype(BF16)
        dwout_s[at] = dotf(hidden_s[at], rows_in[:, 0:width], ((0,), (0,))).astype(BF16)

    @pl.loop(0, TENSOR)
    def _(turn):
        expert_grads(lax.rem(turn + 2, TENSOR))

        @pl.when(turn == 0)
        def _():
            dwin_ring.start_far()
            dwout_ring.start_far()

    dwin_ring.start_own()
    dwout_ring.start_own()
    all_of(ret_s, ret_sems).wait_recv()

    dgain_s[...] = jnp.zeros_like(dgain_s)
    from_wide = one_hot(iota((wide, experts), 0) // groups == iota((wide, experts), 1))

    step_rows = 256

    @pl.loop(0, rows // step_rows)
    def _(step):
        part = block_of(step * step_rows, step_rows)
        came = ret_s[...].reshape(wide, 2 * width)
        low = low_s[part, :]
        weight = weight_s[part, :]
        back = dotf(low, came)
        kept_s[part, :] = (res_s[part, :] + back[:, 0:width]).astype(BF16)
        grad_weight = dotf(pair_s[part, :], came, ((1,), (1,)))
        inner = jnp.sum(weight * grad_weight, axis=0, keepdims=True)
        grad_logits = (weight * (grad_weight - inner)).astype(BF16)
        glog_s[part, :] = dotf(grad_logits, from_wide).astype(BF16)
        grad_mixer = back[:, width : 2 * width] + dotf(grad_logits, wide_router[...])
        scaled = scaled_s[part, :]
        dgain_s[...] += jnp.sum(grad_mixer * scaled, axis=0, keepdims=True)
        grad_scaled = grad_mixer * gain_two[...]
        centered = grad_scaled - jnp.mean(grad_scaled, axis=1, keepdims=True)
        along = jnp.mean(grad_scaled * scaled, axis=1, keepdims=True)
        grad_res = cot_s[part, :] + spread_s[part, 0:1] * (centered - scaled * along)
        res_s[part, :] = grad_res
        grad_att = grad_res.astype(BF16)
        gatt_s[part, :] = grad_att
        grad_ctx = dotf(grad_att, wo_full[...], ((1,), (1,))).astype(BF16)
        for at in range(TENSOR):
            gctx_s[at, part, :] = grad_ctx[:, at * hcols : (at + 1) * hcols]

    def back_copy(off):
        to = lax.rem(place + off, TENSOR)
        dst = gctx_all.at[block_of(place * rows, rows), :]
        return remote(gctx_s.at[to], dst, back_sems, off, "tensor", to)

    for off in (3, 2, 1):
        back_copy(off).start()
    dwin_ring.add_far()
    dwin_ring.start_sums()
    out_store = pltpu.make_async_copy(kept_s, out_ref, store_sems.at[0])
    out_store.start()
    gctx_all[block_of(place * rows, rows), :] = gctx_s[place]

    each_rows = width // peers
    for at in range(TENSOR):
        grad_wo = dotf(ctx_all[at], gatt_s[...], ((0,), (0,))).astype(BF16)
        wop_s[:, at, :, 0:width] = grad_wo.reshape(ROW, each_rows, width)
    grad_router = dotf(glog_s[...], pair_s[:, width : 2 * width], ((0,), (0,)))
    blocks = width // hcols
    small_rows = jnp.concatenate(
        [grad_router, dgain_s[...], jnp.zeros((width // blocks - experts - 1, width), F32)], axis=0
    ).astype(BF16)
    for at in range(blocks):
        small = small_rows[:, at * hcols : (at + 1) * hcols]
        wop_s[:, at, :, width : width + hcols] = small.reshape(ROW, each_rows, hcols)

    my_row, my_col = me // ROW, lax.rem(me, ROW)

    def to_row(off, sems, src, dst):
        return fan(src, dst, sems, my_row * ROW + lax.rem(me + off, ROW))

    def wop_copy(off):
        return to_row(off, wop_sems, wop_s.at[lax.rem(me + off, ROW)], wop_row.at[off])

    def col_copy(off):
        to = lax.rem(me + off * ROW, peers)
        return fan(col_s.at[to // ROW], wop_col.at[off], col_sems, to)

    def colb_copy(off):
        to = lax.rem(me + off * ROW, peers)
        return fan(col_all.at[my_row], col_all.at[my_row], colb_sems, to)

    def wopb_copy(off):
        return to_row(off, wopb_sems, col_all, wop_all.at[my_col])

    cols = peers // ROW
    each(1, ROW, lambda off: wop_copy(off).start())
    wop_row[0] = wop_s[my_col]
    dwout_ring.add_far()

    dk_acc[...] = jnp.zeros_like(dk_acc)
    dv_acc[...] = jnp.zeros_like(dv_acc)
    ones = [pick_head(jnp.ones((8, hcols), F32), head) for head in range(heads)]

    def wopz_copy(off):
        to = lax.rem(place + off, TENSOR)
        return remote(wop_sum.at[place], wop_sum.at[place], wopz_sems, off, "tensor", to)

    def attend_back(row0, seen_rows):
        part = pl.ds(row0, block)
        q = q_s[part, :]
        grad = gctx_all[part, :]
        product = grad.astype(F32) * ctx_s[part, :].astype(F32)
        inner = [
            dotf(ones[head], product, ((1,), (1,)), lax.Precision.HIGHEST)[0:1]
            for head in range(heads)
        ]
        lse = [lse_s[8 * head : 8 * head + 1, part] for head in range(heads)]
        q_heads = [pick_head(q, head) for head in range(heads)]
        grad_heads = [pick_head(grad, head) for head in range(heads)]
        dq = [jnp.zeros((HEAD_DIM, block), F32) for head in range(heads)]
        for col0 in range(0, seen_rows, block):
            keys = pl.ds(col0, block)
            dk = dk_acc[keys, :]
            dv = dv_acc[keys, :]
            for head in range(heads):
                scores = dotf(k_s[keys, :], q_heads[head], ((1,), (1,)))
                soft = jnp.exp(hidden_keys(scores, row0, col0, 1) - lse[head])
                grad_soft = dotf(v_s[keys, :], grad_heads[head], ((1,), (1,)))
                grad_scores = (soft * (grad_soft - inner[head])).astype(BF16)
                dv += dotf(soft.astype(BF16), grad_heads[head])
                dk += dotf(grad_scores, q_heads[head])
                lanes = slice(head * HEAD_DIM, (head + 1) * HEAD_DIM)
                dq[head] += dotf(kt_s[lanes, keys], grad_scores)
            dk_acc[keys, :] = dk
            dv_acc[keys, :] = dv
        dq = jnp.transpose(jnp.concatenate(dq, axis=0))
        grads_s[part, 0:hcols] = (dq * SCORE_SCALE).astype(BF16)

    @pl.loop(0, TENSOR)
    def _(turn):
        blk = lax.rem(place + turn, TENSOR)

        @pl.when(turn > 0)
        def _():
            back_copy(TENSOR - turn).wait_recv()

        by_length(attend_back, blk)

        @pl.when(turn == 0)
        def _():
            dwout_ring.start_sums()
            all_of(wop_row, wop_sems).wait_recv()
            total = jnp.zeros(col_s.shape, F32)
            total = lax.fori_loop(0, ROW, lambda off, acc: acc + wop_row[off].astype(F32), total)
            col_s[...] = total.astype(BF16)
            each(1, cols, lambda off: col_copy(off).start())
            wop_col[0] = col_s[my_row]

        @pl.when(turn == 1)
        def _():
            all_of(wop_col, col_sems).wait_recv()
            total = jnp.zeros(wop_sum.shape[1:], F32)
            for at in range(cols):
                total = total + wop_col[at].astype(F32)
            wop_sum[place] = total.astype(BF16)
            for off in (2, 1, 3):
                wopz_copy(off).start()

        @pl.when(turn == 2)
        def _():
            for off in (2, 1, 3):
                wopz_copy(off).wait_recv()
            total = jnp.zeros(wop_sum.shape[1:], F32)
            for at in range(TENSOR):
                total = total + wop_sum[at].astype(F32)
            col_all[my_row] = total.astype(BF16)
            each(1, cols, lambda off: colb_copy(off).start())

        @pl.when(turn == 3)
        def _():
            all_of(col_all, colb_sems).wait_recv()
            each(1, ROW, lambda off: wopb_copy(off).start())
            wop_all[my_col] = col_all[...]

    grads_s[:, hcols : 2 * hcols] = dk_acc[...].astype(BF16)
    grads_s[:, 2 * hcols : 3 * hcols] = dv_acc[...].astype(BF16)

    def partial_rows(owner, part):
        start = owner * rows + part * half
        return dotf(grads_s[block_of(start, half), :], w_s[...], ((1,), (1,)))

    row_ring = Scatter(rows_s, via_rows, land_rows, row_sems, place)
    low, high = row_ring.low, row_ring.high
    rows_s[far, low] = partial_rows(far, 0).astype(BF16)
    rows_s[far, high] = partial_rows(far, 1).astype(BF16)
    row_ring.start_far()

    def piece_copy(off):
        to = lax.rem(me + off, peers)
        return fan(piece_s.at[to], piece_in.at[off], piece_sems, to)

    tall = width // ROW
    count = tall // each_rows

    @pl.loop(0, ROW)
    def _(turn):
        at = lax.rem(me // count + turn, ROW)
        grads = dotf(seqt_s[block_of(at * tall, tall), :], grads_s[...]).astype(BF16)
        for kind in range(3):
            piece = grads[:, kind * hcols : (kind + 1) * hcols].reshape(count, each_rows, hcols)
            piece_s[pl.ds(at * count, count), kind] = piece

        def send(to):
            off = lax.rem(to + peers - me, peers)
            pl.when(off > 0)(lambda: piece_copy(off).start())

        each(at * count, (at + 1) * count, send)

    piece_in[0] = piece_s[me]
    rows_s[right, high] = partial_rows(right, 1).astype(BF16)
    rows_s[left, low] = partial_rows(left, 0).astype(BF16)
    row_ring.start_own()
    rows_s[right, low] = partial_rows(right, 0).astype(BF16)
    rows_s[left, high] = partial_rows(left, 1).astype(BF16)
    row_ring.add_far()
    row_ring.start_sums()
    mine_s[low, :] = partial_rows(place, 0)
    mine_s[high, :] = partial_rows(place, 1)

    for ring in (tok_ring, win_ring, wout_ring, wo_ring, dwin_ring):
        ring.drain()
    for off in (2, 1, 3):
        ctx_copy(off).wait_send()
        back_copy(off).wait_send()
        wopz_copy(off).wait_send()
    all_of(out_s, mix_sems).wait_send()
    all_of(done_s, ret_sems).wait_send()
    all_of(wop_s, wop_sems).wait_send()
    all_of(wop_col, col_sems).wait_send()
    all_of(col_all, colb_sems).wait_send()
    all_of(piece_in, piece_sems).wait_recv()
    total = jnp.zeros(piece_in.shape[1:], F32)
    total = lax.fori_loop(0, peers, lambda off, acc: acc + piece_in[off].astype(F32), total)
    sum_all[me] = total.astype(BF16)

    def sum_copy(off):
        to = lax.rem(me + off, peers)
        return fan(sum_all.at[me], sum_all.at[me], sum_sems, to)

    each(1, peers, lambda off: sum_copy(off).start())

    cols = block_of(me * each_rows, each_rows)
    along = jnp.zeros((each_rows, 1), F32)
    for kind in range(3):
        weight = w_s[cols, kind * hcols : (kind + 1) * hcols].astype(F32)
        along = along + jnp.sum(total[kind] * weight, axis=1, keepdims=True)
    first_s[place] = jnp.broadcast_to(along, (each_rows, 128))

    def first_copy(off):
        to = lax.rem(place + off, TENSOR)
        return remote(first_s.at[place], first_s.at[place], first_sems, off, "tensor", to)

    for off in (2, 1, 3):
        first_copy(off).start()

    def gain_copy(off):
        to = lax.rem(me + off, peers)
        return fan(gain_all.at[me], gain_all.at[me], gain_sems, to)

    dwin_ring.wait()
    dwout_ring.wait()
    for at, (ring, part_s) in enumerate(((dwin_ring, dwin_s), (dwout_ring, dwout_s))):
        for part in (low, high):
            acc_s[at, part, :] = part_s[place, part].astype(F32) + ring.landed(part)
    win_store = pltpu.make_async_copy(acc_s.at[0], dwin_ref, store_sems.at[1])
    wout_store = pltpu.make_async_copy(acc_s.at[1], dwout_ref, store_sems.at[2])
    win_store.start()
    wout_store.start()
    all_of(wop_all, wopb_sems).wait_recv()
    all_of(wop_all, wopb_sems).wait_send()
    go_ref[...] = wop_all[:, place, :, 0:width].reshape(hcols, width).astype(F32)
    kept_rows = (experts + 1 + 15) // 16 * 16
    sums = jnp.concatenate(
        [
            wop_all[:, at, :, width : width + hcols].reshape(ROW * each_rows, hcols)[:kept_rows]
            for at in range(blocks)
        ],
        axis=1,
    ).astype(F32)
    router_ref[...] = sums[0:experts]
    dsecond_ref[...] = sums[experts : experts + 1]

    for off in (2, 1, 3):
        first_copy(off).wait_recv()
    gain_all[me] = first_s[0] + first_s[1] + first_s[2] + first_s[3]
    each(1, peers, lambda off: gain_copy(off).start())

    row_ring.wait()
    for part in (low, high):
        grad_normed = mine_s[part, :] + row_ring.landed(part)
        scaled, spread = norm_parts(tok_s[place, part].astype(F32))
        grad_scaled = grad_normed * gain_one[...]
        centered = grad_scaled - jnp.mean(grad_scaled, axis=1, keepdims=True)
        along = jnp.mean(grad_scaled * scaled, axis=1, keepdims=True)
        scaled_s[part, :] = res_s[part, :] + spread * (centered - scaled * along)
    tok_store = pltpu.make_async_copy(scaled_s, gtok_ref, store_sems.at[3])
    tok_store.start()

    all_of(piece_s, piece_sems).wait_send()
    for off in (2, 1, 3):
        first_copy(off).wait_send()
    dwout_ring.drain()
    row_ring.drain()
    all_of(sum_all, sum_sems).wait_recv()
    for at, grad_ref in enumerate((gq_ref, gk_ref, gv_ref)):
        grad_ref[...] = sum_all[:, at].reshape(width, hcols).astype(F32)
    all_of(gain_all, gain_sems).wait_recv()
    dfirst_ref[...] = jnp.transpose(gain_all[...].reshape(width, 128))[0:1] / gain_one[...]

    all_of(sum_all, sum_sems).wait_send()
    all_of(gain_all, gain_sems).wait_send()
    for store in (out_store, win_store, wout_store, tok_store):
        store.wait()


def layer(prefix, tokens, gain_one, gain_two, wq, wk, wv, wo, router, win, wout, cot, routes, prio):
    rows, width = tokens.shape
    experts = router.shape[0]
    hcols = wq.shape[1]
    fcols = win.shape[1]
    groups = rows // GROUP
    wide = experts * groups
    length = TENSOR * rows
    heads = hcols // HEAD_DIM
    peers = experts
    each_rows = width // peers
    capacity = (5 * GROUP * TOP + 4 * experts - 1) // (4 * experts)

    def dev(shape, kind):
        return jax.ShapeDtypeStruct(shape, kind)

    def low(*shape):
        return pltpu.VMEM(shape, BF16)

    def full(*shape):
        return pltpu.VMEM(shape, F32)

    def sems(count):
        return pltpu.SemaphoreType.DMA((2, count))

    return pl.pallas_call(
        functools.partial(layer_kernel, experts=experts, capacity=float(capacity)),
        out_shape=(
            dev((rows, width), BF16),
            dev((rows, width), F32),
            dev(wq.shape, F32),
            dev(wq.shape, F32),
            dev(wq.shape, F32),
            dev(wo.shape, F32),
            dev((experts, width), F32),
            dev((1, width), F32),
            dev((1, width), F32),
            dev(win.shape, F32),
            dev(wout.shape, F32),
        ),
        in_specs=[SM] + [HB] * 13,
        out_specs=(HB,) * 2 + (VM,) * 7 + (HB,) * 2,
        scratch_shapes=[
            low(TENSOR, rows, width),
            full(1, width),
            full(1, width),
            low(width, 3 * hcols),
            low(TENSOR, hcols, width),
            low(experts, width),
            low(TENSOR, width, fcols),
            low(TENSOR, fcols, width),
            full(rows, width),
            pltpu.VMEM(routes.shape, jnp.int32),
            pltpu.VMEM(prio.shape, jnp.int32),
            low(width, length),
            low(length, hcols),
            low(length, hcols),
            low(hcols, length),
            low(length, hcols),
            low(rows, wide),
            low(length, hcols),
            full(8 * heads, length),
            low(TENSOR, rows, hcols),
            low(wide, width),
            full(rows, width),
            full(rows, width),
            full(rows, 128),
            low(rows, 2 * width),
            full(rows, wide),
            low(rows, wide),
            low(experts, groups, 2 * width),
            low(experts, groups, 2 * width),
            low(experts, groups, 2 * width),
            low(experts, groups, 2 * width),
            full(2, wide, width),
            low(TENSOR, wide, fcols),
            low(TENSOR, wide, fcols),
            low(TENSOR, rows, hcols),
            low(length, hcols),
            low(rows, width),
            low(rows, experts),
            full(1, width),
            low(TENSOR, width, fcols),
            low(TENSOR, fcols, width),
            low(width, fcols),
            low(fcols, width),
            low(2, width, fcols),
            low(2, fcols, width),
            low(ROW, peers // ROW, each_rows, width + hcols),
            low(ROW, peers // ROW, each_rows, width + hcols),
            low(peers // ROW, each_rows, width + hcols),
            low(peers // ROW, each_rows, width + hcols),
            low(TENSOR, each_rows, width + hcols),
            low(peers // ROW, each_rows, width + hcols),
            low(ROW, peers // ROW, each_rows, width + hcols),
            full(length, hcols),
            full(length, hcols),
            low(length, 3 * hcols),
            low(TENSOR, rows, width),
            low(rows, width),
            low(2, rows, width),
            full(rows, width),
            low(peers, 3, each_rows, hcols),
            low(peers, 3, each_rows, hcols),
            low(peers, 3, each_rows, hcols),
            full(TENSOR, each_rows, 128),
            full(peers, each_rows, 128),
            pltpu.SemaphoreType.DMA((13,)),
            pltpu.SemaphoreType.DMA((4,)),
            pltpu.SemaphoreType.REGULAR,
            sems(6),
            sems(6),
            sems(6),
            sems(6),
            sems(TENSOR),
            pltpu.SemaphoreType.DMA((1 + wide // 128,)),
            pltpu.SemaphoreType.DMA((2,)),
            sems(TENSOR),
            sems(6),
            sems(6),
            pltpu.SemaphoreType.DMA((2,)),
            pltpu.SemaphoreType.DMA((2,)),
            pltpu.SemaphoreType.DMA((2,)),
            sems(TENSOR),
            pltpu.SemaphoreType.DMA((2,)),
            sems(6),
            pltpu.SemaphoreType.DMA((2,)),
            pltpu.SemaphoreType.DMA((2,)),
            sems(TENSOR),
            pltpu.SemaphoreType.DMA((2,)),
        ],
        compiler_params=pltpu.CompilerParams(
            collective_id=0, has_side_effects=True, vmem_limit_bytes=VMEM_BYTES
        ),
        name="layer",
    )(prefix, tokens, gain_one, gain_two, wq, wk, wv, wo, router, win, wout, cot, routes, prio)


def write_kernel(*refs):
    count = (len(refs) - 2) // 3
    in_sems, out_sems = refs[-2:]
    loads = [
        pltpu.make_async_copy(refs[at], refs[2 * count + at], in_sems.at[at]) for at in range(count)
    ]
    stores = [
        pltpu.make_async_copy(refs[2 * count + at], refs[count + at], out_sems.at[at])
        for at in range(count)
    ]
    for load in loads:
        load.start()
    for load, store in zip(loads, stores):
        load.wait()
        store.start()
    for store in stores:
        store.wait()


def write_out(results):
    count = len(results)
    return pl.pallas_call(
        write_kernel,
        out_shape=tuple(jax.ShapeDtypeStruct(x.shape, x.dtype) for x in results),
        in_specs=[HB] * count,
        out_specs=(HB,) * count,
        scratch_shapes=[pltpu.VMEM(x.shape, x.dtype) for x in results]
        + [pltpu.SemaphoreType.DMA((count,)), pltpu.SemaphoreType.DMA((count,))],
        compiler_params=pltpu.CompilerParams(vmem_limit_bytes=VMEM_BYTES),
        name="write_out",
    )(*results)


def body(
    tokens,
    first_gain,
    second_gain,
    query_weight,
    key_weight,
    value_weight,
    output_weight,
    router_weight,
    expert_in,
    expert_out,
    cotangent,
    routes,
    priority,
    prefix_len,
):
    width = tokens.shape[1]
    results = layer(
        prefix_len,
        tokens,
        first_gain.reshape(1, width),
        second_gain.reshape(1, width),
        query_weight,
        key_weight,
        value_weight,
        output_weight,
        router_weight.T,
        expert_in[0],
        expert_out[0],
        cotangent,
        routes.T,
        priority,
    )
    out, gtok, gq, gk, gv, go, grouter, dsecond, dfirst, dwin, dwout = write_out(results)
    return (
        out,
        gtok,
        dfirst.reshape(width),
        dsecond.reshape(width),
        gq,
        gk,
        gv,
        go,
        grouter.T,
        dwin[None],
        dwout[None],
    )


def solution(mesh):
    in_specs = (
        P(("expert", "tensor"), None),
        P(),
        P(),
        P(None, "tensor"),
        P(None, "tensor"),
        P(None, "tensor"),
        P("tensor", None),
        P(),
        P("expert", None, "tensor"),
        P("expert", "tensor", None),
        P(("expert", "tensor"), None),
        P(("expert", "tensor"), None),
        P(("expert", "tensor"), None),
        P("expert"),
    )
    out_specs = (
        P(("expert", "tensor"), None),
        P(("expert", "tensor"), None),
        P(),
        P(),
        P(None, "tensor"),
        P(None, "tensor"),
        P(None, "tensor"),
        P("tensor", None),
        P(),
        P("expert", None, "tensor"),
        P("expert", "tensor", None),
    )
    return jax.shard_map(body, mesh=mesh, in_specs=in_specs, out_specs=out_specs, check_vma=False)
```

```python
import functools

import jax
import jax.numpy as jnp
from jax import lax
from jax.experimental import pallas as pl
from jax.experimental.pallas import tpu as pltpu
from jax.sharding import PartitionSpec as P

HEAD_DIM = 64
GROUP = 32
TOP = 4
EPS = 1e-05
NEG = -1e30
SCORE_SCALE = HEAD_DIM**-0.5
PREFIX_MOST = 1024
ROW = 8
MESH = pl.DeviceIdType.MESH
VM = pl.BlockSpec(memory_space=pltpu.VMEM)
SM = pl.BlockSpec(memory_space=pltpu.SMEM)
HB = pl.BlockSpec(memory_space=pltpu.HBM)
TENSOR = 4
VMEM_BYTES = 58 << 20
BF16 = jnp.bfloat16
F32 = jnp.float32


def dotf(left, right, dims=((1,), (0,)), precision=None):
    return lax.dot_general(
        left, right, (dims, ((), ())), preferred_element_type=F32, precision=precision
    )


def iota(shape, axis):
    return lax.broadcasted_iota(jnp.int32, shape, axis)


def one_hot(test):
    return jnp.where(test, 1.0, 0.0).astype(BF16)


def norm_parts(values):
    center = values - jnp.mean(values, axis=1, keepdims=True)
    spread = lax.rsqrt(jnp.mean(center * center, axis=1, keepdims=True) + EPS)
    return center * spread, spread


def remote(src, dst, sems, slot, axis, to):
    return pltpu.make_async_remote_copy(
        src_ref=src,
        dst_ref=dst,
        send_sem=sems.at[0, slot],
        recv_sem=sems.at[1, slot],
        device_id={axis: to},
        device_id_type=MESH,
    )


def fan(src, dst, sems, to, lane=0):
    return pltpu.make_async_remote_copy(
        src_ref=src,
        dst_ref=dst,
        send_sem=sems.at[0],
        recv_sem=sems.at[1 + lane],
        device_id={"expert": to},
        device_id_type=MESH,
    )


def greet(peers):
    barrier = pltpu.get_barrier_semaphore()
    place = lax.axis_index("tensor")
    me = lax.axis_index("expert")

    def signal(axis, to):
        pl.semaphore_signal(barrier, inc=1, device_id={axis: to}, device_id_type=MESH)

    for off in range(1, TENSOR):
        signal("tensor", lax.rem(place + off, TENSOR))
    for off in range(1, ROW):
        signal("expert", me // ROW * ROW + lax.rem(me + off, ROW))
    for off in range(ROW, peers, ROW):
        signal("expert", lax.rem(me + off, peers))
    return TENSOR - 1 + ROW - 1 + peers // ROW - 1


def each(first, last, act):
    def one(at, _):
        act(at)
        return 0

    lax.fori_loop(first, last, one, 0)


def block_of(start, size):
    return pl.ds(pl.multiple_of(start, size), size)


def pick_head(values, head, other=0.0):
    lane = iota(values.shape, 1)
    inside = (lane >= head * HEAD_DIM) & (lane < (head + 1) * HEAD_DIM)
    return jnp.where(inside, values, jnp.full_like(values, other))


class Gather:
    def __init__(self, buf, sems, place, eighths=4):
        self.buf, self.sems, self.place = buf, sems, place
        self.right, self.left = lax.rem(place + 1, TENSOR), lax.rem(place + TENSOR - 1, TENSOR)
        size = buf.shape[1]
        cut = size * eighths // 8
        self.low, self.high = pl.ds(0, cut), pl.ds(cut, size - cut)

    def copy(self, slot):
        owner, part, to = (
            (self.place, self.low, self.right),
            (self.place, self.high, self.left),
            (self.place, self.high, self.right),
            (self.place, self.low, self.left),
            (self.left, self.low, self.right),
            (self.right, self.high, self.left),
        )[slot]
        block = self.buf.at[owner, part]
        return remote(block, block, self.sems, slot, "tensor", to)

    def start(self, slots=range(4)):
        for slot in slots:
            self.copy(slot).start()

    def forward(self):
        self.copy(0).wait_recv()
        self.copy(4).start()
        self.copy(1).wait_recv()
        self.copy(5).start()

    def wait_near(self):
        self.copy(2).wait_recv()
        self.copy(3).wait_recv()

    def wait_far(self):
        self.copy(4).wait_recv()
        self.copy(5).wait_recv()

    def drain(self):
        for slot in range(6):
            self.copy(slot).wait_send()


class Scatter:
    def __init__(self, part, via, land, sems, place):
        self.part, self.via, self.land, self.sems, self.place = part, via, land, sems, place
        self.right, self.left = lax.rem(place + 1, TENSOR), lax.rem(place + TENSOR - 1, TENSOR)
        self.far = lax.rem(place + 2, TENSOR)
        half = part.shape[1] // 2
        self.low, self.high = pl.ds(0, half), pl.ds(half, half)

    def copy(self, slot):
        block, half, to, dst = (
            (self.far, self.low, self.right, self.via),
            (self.far, self.high, self.left, self.via),
            (self.right, self.high, self.right, self.land.at[0]),
            (self.left, self.low, self.left, self.land.at[1]),
            (self.right, self.low, self.right, self.land.at[0]),
            (self.left, self.high, self.left, self.land.at[1]),
        )[slot]
        return remote(self.part.at[block, half], dst.at[half], self.sems, slot, "tensor", to)

    def start_far(self):
        self.copy(0).start()
        self.copy(1).start()

    def start_own(self):
        self.copy(2).start()
        self.copy(3).start()

    def add_far(self):
        self.copy(0).wait_recv()
        self.part[self.right, self.low] = (
            self.part[self.right, self.low].astype(F32) + self.via[self.low].astype(F32)
        ).astype(BF16)
        self.copy(1).wait_recv()
        self.part[self.left, self.high] = (
            self.part[self.left, self.high].astype(F32) + self.via[self.high].astype(F32)
        ).astype(BF16)

    def start_sums(self):
        self.copy(4).start()
        self.copy(5).start()

    def wait(self):
        for slot in range(2, 6):
            self.copy(slot).wait_recv()

    def landed(self, rows):
        return self.land[0, rows].astype(F32) + self.land[1, rows].astype(F32)

    def drain(self):
        for slot in range(6):
            self.copy(slot).wait_send()


def layer_kernel(
    prefix_ref,
    tok_hbm,
    gain_one_hbm,
    gain_two_hbm,
    wq_hbm,
    wk_hbm,
    wv_hbm,
    wo_hbm,
    router_hbm,
    win_hbm,
    wout_hbm,
    cot_hbm,
    routes_hbm,
    prio_hbm,
    out_ref,
    gtok_ref,
    gq_ref,
    gk_ref,
    gv_ref,
    go_ref,
    router_ref,
    dsecond_ref,
    dfirst_ref,
    dwin_ref,
    dwout_ref,
    tok_s,
    gain_one,
    gain_two,
    w_s,
    wo_s,
    router_s,
    win_s,
    wout_s,
    cot_s,
    routes_s,
    prio_s,
    seqt_s,
    q_s,
    k_s,
    kt_s,
    v_s,
    kept_s,
    ctx_s,
    lse_s,
    ctx_all,
    wide_router,
    res_s,
    scaled_s,
    spread_s,
    pair_s,
    weight_s,
    low_s,
    out_s,
    in_s,
    done_s,
    ret_s,
    acc_s,
    hidden_s,
    gpre_s,
    gctx_s,
    gctx_all,
    gatt_s,
    glog_s,
    dgain_s,
    dwin_s,
    dwout_s,
    via_win,
    via_wout,
    land_win,
    land_wout,
    wop_s,
    wop_row,
    col_s,
    wop_col,
    wop_sum,
    col_all,
    wop_all,
    dk_acc,
    dv_acc,
    grads_s,
    rows_s,
    via_rows,
    land_rows,
    mine_s,
    piece_s,
    piece_in,
    sum_all,
    first_s,
    gain_all,
    local_sems,
    store_sems,
    plane_sem,
    tok_sems,
    win_sems,
    wout_sems,
    wo_sems,
    ctx_sems,
    mix_sems,
    ret_sems,
    back_sems,
    dwin_sems,
    dwout_sems,
    wop_sems,
    col_sems,
    colb_sems,
    wopz_sems,
    wopb_sems,
    row_sems,
    piece_sems,
    sum_sems,
    first_sems,
    gain_sems,
    *,
    experts,
    capacity,
):
    place = lax.axis_index("tensor")
    me = lax.axis_index("expert")
    right, left = lax.rem(place + 1, TENSOR), lax.rem(place + TENSOR - 1, TENSOR)
    far = lax.rem(place + 2, TENSOR)
    _, rows, width = tok_s.shape
    length, hcols = q_s.shape
    heads = hcols // HEAD_DIM
    groups = rows // GROUP
    wide = experts * groups
    peers = experts
    greeted = greet(peers)

    loads = [
        (tok_hbm, tok_s.at[place]),
        (gain_one_hbm, gain_one),
        (wq_hbm, w_s.at[:, pl.ds(0, hcols)]),
        (wk_hbm, w_s.at[:, pl.ds(hcols, hcols)]),
        (wv_hbm, w_s.at[:, pl.ds(2 * hcols, hcols)]),
        (routes_hbm, routes_s),
        (prio_hbm, prio_s),
        (wo_hbm, wo_s.at[place]),
        (win_hbm, win_s.at[place]),
        (wout_hbm, wout_s.at[place]),
        (gain_two_hbm, gain_two),
        (router_hbm, router_s),
        (cot_hbm, cot_s),
    ]
    loads = [
        pltpu.make_async_copy(src, dst, local_sems.at[at]) for at, (src, dst) in enumerate(loads)
    ]
    for load in loads:
        load.start()

    def all_of(buf, sems):
        most = buf.at[pl.ds(1, buf.shape[0] - 1)]
        return fan(most, most, sems, lax.rem(me + 1, peers))

    batch = 128 // groups

    tok_ring = Gather(tok_s, tok_sems, place)
    win_ring = Gather(win_s, win_sems, place, 4)
    wout_ring = Gather(wout_s, wout_sems, place, 4)
    wo_ring = Gather(wo_s, wo_sems, place)
    loads[0].wait()
    pl.semaphore_wait(pltpu.get_barrier_semaphore(), greeted)
    tok_ring.start()
    for off in range(ROW, peers, ROW):
        to = lax.rem(me + off, peers)
        pl.semaphore_signal(plane_sem, inc=1, device_id={"expert": to}, device_id_type=MESH)
    for load in loads[1:5]:
        load.wait()

    half = rows // 2

    def project(owner):
        @pl.loop(0, rows // 128)
        def _(at):
            start = at * 128
            scaled, _ = norm_parts(tok_s[owner, block_of(start, 128)].astype(F32))
            normed = (scaled * gain_one[...]).astype(BF16)
            to = block_of(owner * rows + start, 128)
            seqt_s[:, to] = jnp.transpose(normed)
            out = dotf(normed, w_s[...]).astype(BF16)
            q_s[to, :] = out[:, 0:hcols] * SCORE_SCALE
            k_s[to, :] = out[:, hcols : 2 * hcols]
            kt_s[:, to] = jnp.transpose(out[:, hcols : 2 * hcols])
            v_s[to, :] = out[:, 2 * hcols : 3 * hcols]

    project(place)
    tok_ring.forward()

    loads[5].wait()
    loads[6].wait()
    size = GROUP
    to_wide = one_hot(iota((experts, wide), 0) == iota((experts, wide), 1) // groups)
    prio = prio_s[...].astype(F32).astype(BF16)
    spread_rows = dotf(one_hot((iota((rows, groups), 0) // size) == iota((rows, groups), 1)), prio)
    at_col = (iota((rows, size), 0) % size) == iota((rows, size), 1)
    prio_col = jnp.sum(jnp.where(at_col, spread_rows, 0.0), axis=1, keepdims=True)
    group_tok = one_hot((iota((groups, rows), 1) // size) == iota((groups, rows), 0))
    spread_cols = dotf(prio, group_tok, ((0,), (0,)))
    at_row = (iota((size, rows), 1) % size) == iota((size, rows), 0)
    prio_row = jnp.sum(jnp.where(at_row, spread_cols, 0.0), axis=0, keepdims=True)
    named = routes_s[0:1, :] == iota((experts, rows), 0)
    for pick in range(1, TOP):
        named = named | (routes_s[pick : pick + 1, :] == iota((experts, rows), 0))
    own_group = (iota((rows, wide), 0) // size) == (iota((rows, wide), 1) % groups)
    member = jnp.where(own_group, dotf(one_hot(named), to_wide, ((0,), (0,))), 0.0)
    rank = dotf(one_hot(prio_row < prio_col), member.astype(BF16))
    kept_s[...] = jnp.where(rank < capacity, member, 0.0).astype(BF16)

    tok_ring.copy(2).wait_recv()
    project(left)
    tok_ring.copy(3).wait_recv()
    project(right)
    for load in loads[7:10]:
        load.wait()
    tok_ring.wait_far()
    wo_ring.start()
    win_ring.start((0, 1))
    project(far)

    prefix = prefix_ref[0]
    block = rows

    def hidden_keys(scores, row0, col0, row_axis):
        if isinstance(row0, int) and col0 + block - 1 <= row0:
            return scores
        line = (block, 1) if row_axis == 0 else (1, block)
        until = iota(line, row_axis) + (row0 + 1 - col0)
        if col0 < PREFIX_MOST:
            until = jnp.maximum(until, prefix - col0)
        seen = iota((block, block), 1 - row_axis) < until
        return jnp.where(seen, scores, NEG)

    def ctx_copy(off):
        to = lax.rem(place + off, TENSOR)
        src = ctx_s.at[block_of(to * rows, rows), :]
        return remote(src, ctx_all.at[place], ctx_sems, off, "tensor", to)

    def attend(row0, seen_rows):
        part_rows = pl.ds(row0, block)
        q = q_s[part_rows, :]
        starts = range(0, seen_rows, block)
        merged = jnp.zeros((block, hcols), F32)
        for head in range(heads):
            q_head = pick_head(q, head)
            scores = []
            for col0 in starts:
                part = dotf(q_head, k_s[col0 : col0 + block, :], ((1,), (1,)))
                scores.append(hidden_keys(part, row0, col0, 0))
            peak = functools.reduce(
                jnp.maximum, [jnp.max(part, axis=1, keepdims=True) for part in scores]
            )
            acc = jnp.zeros((block, hcols), F32)
            for part, col0 in zip(scores, starts):
                soft = jnp.exp(part - peak).astype(BF16)
                acc = acc + dotf(soft, pick_head(v_s[col0 : col0 + block, :], head, 1.0))
            lane = HEAD_DIM if head == 0 else 0
            total = acc[:, lane : lane + 1]
            merged = merged + pick_head(acc * (1.0 / total), head)
            lse = jnp.broadcast_to(peak + jnp.log(total), (block, 128))
            lse_s[8 * head : 8 * head + 8, part_rows] = jnp.transpose(lse)[:8]
        ctx_s[part_rows, :] = merged.astype(BF16)

    def by_length(act, blk):
        short = PREFIX_MOST // block
        pl.when(blk < short)(lambda: act(pl.multiple_of(blk * block, block), PREFIX_MOST))
        for at in range(short, TENSOR):
            pl.when(blk == at)(functools.partial(act, at * block, (at + 1) * block))

    @pl.loop(0, TENSOR)
    def _(turn):
        blk = lax.rem(place + 1 + turn, TENSOR)
        by_length(attend, blk)

        @pl.when(turn < TENSOR - 1)
        def _():
            ctx_copy(turn + 1).start()

        @pl.when(turn == 1)
        def _():
            wo_ring.forward()

    wout_ring.start((0, 1))
    win_ring.forward()
    win_ring.start((2, 3))
    ctx_all[place] = ctx_s[block_of(place * rows, rows), :]
    for load in loads[10:]:
        load.wait()
    wide_router[...] = dotf(to_wide, router_s[...], ((0,), (0,))).astype(BF16)
    pair_s[:, 0:width] = cot_s[...].astype(BF16)
    wo_ring.wait_near()
    wo_ring.wait_far()
    wo_full = wo_s.reshape(TENSOR * hcols, width)
    for off in (2, 1, 3):
        ctx_copy(off).wait_recv()

    step_rows = 128

    @pl.loop(0, rows // step_rows)
    def _(step):
        part = block_of(step * step_rows, step_rows)
        ctx = jnp.concatenate([ctx_all[at, part, :] for at in range(TENSOR)], axis=1)
        residual = tok_s[place, part].astype(F32) + dotf(ctx, wo_full[...])
        res_s[part, :] = residual
        scaled, spread = norm_parts(residual)
        scaled_s[part, :] = scaled
        spread_s[part, :] = jnp.broadcast_to(spread, (step_rows, 128))
        mixer = (scaled * gain_two[...]).astype(BF16)
        pair_s[part, width : 2 * width] = mixer
        logits = dotf(mixer, wide_router[...], ((1,), (1,)))
        kept = kept_s[part, :].astype(F32)
        terms = jnp.where(kept > 0.0, jnp.exp(logits), 0.0)
        total = jnp.sum(terms, axis=0, keepdims=True)
        count = jnp.sum(kept, axis=0, keepdims=True)
        weight = terms / jnp.where(count > 0.0, total, 1.0)
        weight_s[part, :] = weight
        low_s[part, :] = weight.astype(BF16)

    @pl.loop(0, wide // 128)
    def _(blk):
        mixed = dotf(low_s[:, block_of(blk * 128, 128)], pair_s[...], ((0,), (0,))).astype(BF16)
        count = 128 // groups
        out_s[pl.ds(blk * count, count)] = mixed.reshape(count, groups, 2 * width)

    def mix_copy(off):
        to = lax.rem(me + off, peers)
        return fan(out_s.at[to], in_s.at[off], mix_sems, to, off // batch)

    pl.semaphore_wait(plane_sem, peers // ROW - 1)
    each(1, peers, lambda off: mix_copy(off).start())
    in_s[0] = out_s[me]
    wout_ring.start((2, 3))

    def ret_copy(off):
        to = lax.rem(me + peers - off, peers)
        return fan(done_s.at[off], ret_s.at[me], ret_sems, to)

    def expert_part(chunk, slices, start, count=128):
        part = block_of(chunk * count, count)
        sources = count // groups
        rows_in = in_s[pl.ds(chunk * sources, sources)].reshape(count, 2 * width)
        grad = rows_in[:, 0:width]
        mixed = rows_in[:, width : 2 * width]
        for at in slices:
            at = lax.rem(place + at, TENSOR)
            pre = dotf(mixed, win_s[at])
            sigma = 1.0 / (1.0 + jnp.exp(-pre))
            hidden = (pre * sigma).astype(BF16)
            grad_hidden = dotf(grad, wout_s[at], ((1,), (1,)))
            grad_pre = (grad_hidden * (sigma * (1.0 + pre * (1.0 - sigma)))).astype(BF16)
            hidden_s[at, part, :] = hidden
            gpre_s[at, part, :] = grad_pre
            returned = dotf(hidden, wout_s[at])
            grad_mixed = dotf(grad_pre, win_s[at], ((1,), (1,)))
            if start:
                acc_s[0, part, :] = returned
                acc_s[1, part, :] = grad_mixed
                start = False
            else:
                acc_s[0, part, :] += returned
                acc_s[1, part, :] += grad_mixed

    win_ring.wait_near()

    @pl.loop(0, peers // batch)
    def _(chunk):

        @pl.when(chunk == 0)
        def _():
            came = in_s.at[pl.ds(1, batch - 1)]
            fan(came, came, mix_sems, lax.rem(me + 1, peers), 0).wait_recv()

        @pl.when(chunk > 0)
        def _():
            came = in_s.at[pl.ds(chunk * batch, batch)]
            fan(came, came, mix_sems, lax.rem(me + 1, peers), chunk).wait_recv()

        expert_part(chunk, (0,), True)

        @pl.when(chunk == 1)
        def _():
            wout_ring.forward()

    wout_ring.wait_near()

    @pl.loop(0, peers // batch)
    def _(turn):
        expert_part(turn // 2, (3 - 2 * lax.rem(turn, 2),), False, 256)

    win_ring.wait_far()
    wout_ring.wait_far()

    @pl.loop(0, peers // (2 * batch))
    def _(chunk):
        expert_part(chunk, (2,), False, 256)
        part = block_of(chunk * 256, 256)
        begin = chunk * 2 * batch
        done = jnp.concatenate([acc_s[0, part, :], acc_s[1, part, :]], axis=1).astype(BF16)
        done_s[pl.ds(begin, 2 * batch)] = done.reshape(2 * batch, groups, 2 * width)
        each(jnp.maximum(begin, 1), begin + 2 * batch, lambda off: ret_copy(off).start())

    ret_s[me] = done_s[0]

    dwin_ring = Scatter(dwin_s, via_win, land_win, dwin_sems, place)
    dwout_ring = Scatter(dwout_s, via_wout, land_wout, dwout_sems, place)

    def expert_grads(off):
        at = lax.rem(place + off, TENSOR)
        rows_in = in_s[...].reshape(wide, 2 * width)
        dwin_s[at] = dotf(rows_in[:, width : 2 * width], gpre_s[at], ((0,), (0,))).astype(BF16)
        dwout_s[at] = dotf(hidden_s[at], rows_in[:, 0:width], ((0,), (0,))).astype(BF16)

    @pl.loop(0, TENSOR)
    def _(turn):
        expert_grads(lax.rem(turn + 2, TENSOR))

        @pl.when(turn == 0)
        def _():
            dwin_ring.start_far()
            dwout_ring.start_far()

    dwin_ring.start_own()
    dwout_ring.start_own()
    all_of(ret_s, ret_sems).wait_recv()

    dgain_s[...] = jnp.zeros_like(dgain_s)
    from_wide = one_hot(iota((wide, experts), 0) // groups == iota((wide, experts), 1))

    step_rows = 256

    @pl.loop(0, rows // step_rows)
    def _(step):
        part = block_of(step * step_rows, step_rows)
        came = ret_s[...].reshape(wide, 2 * width)
        low = low_s[part, :]
        weight = weight_s[part, :]
        back = dotf(low, came)
        kept_s[part, :] = (res_s[part, :] + back[:, 0:width]).astype(BF16)
        grad_weight = dotf(pair_s[part, :], came, ((1,), (1,)))
        inner = jnp.sum(weight * grad_weight, axis=0, keepdims=True)
        grad_logits = (weight * (grad_weight - inner)).astype(BF16)
        glog_s[part, :] = dotf(grad_logits, from_wide).astype(BF16)
        grad_mixer = back[:, width : 2 * width] + dotf(grad_logits, wide_router[...])
        scaled = scaled_s[part, :]
        dgain_s[...] += jnp.sum(grad_mixer * scaled, axis=0, keepdims=True)
        grad_scaled = grad_mixer * gain_two[...]
        centered = grad_scaled - jnp.mean(grad_scaled, axis=1, keepdims=True)
        along = jnp.mean(grad_scaled * scaled, axis=1, keepdims=True)
        grad_res = cot_s[part, :] + spread_s[part, 0:1] * (centered - scaled * along)
        res_s[part, :] = grad_res
        grad_att = grad_res.astype(BF16)
        gatt_s[part, :] = grad_att
        grad_ctx = dotf(grad_att, wo_full[...], ((1,), (1,))).astype(BF16)
        for at in range(TENSOR):
            gctx_s[at, part, :] = grad_ctx[:, at * hcols : (at + 1) * hcols]

    def back_copy(off):
        to = lax.rem(place + off, TENSOR)
        dst = gctx_all.at[block_of(place * rows, rows), :]
        return remote(gctx_s.at[to], dst, back_sems, off, "tensor", to)

    for off in (3, 2, 1):
        back_copy(off).start()
    dwin_ring.add_far()
    dwin_ring.start_sums()
    out_store = pltpu.make_async_copy(kept_s, out_ref, store_sems.at[0])
    out_store.start()
    gctx_all[block_of(place * rows, rows), :] = gctx_s[place]

    each_rows = width // peers
    for at in range(TENSOR):
        grad_wo = dotf(ctx_all[at], gatt_s[...], ((0,), (0,))).astype(BF16)
        wop_s[:, at, :, 0:width] = grad_wo.reshape(ROW, each_rows, width)
    grad_router = dotf(glog_s[...], pair_s[:, width : 2 * width], ((0,), (0,)))
    blocks = width // hcols
    small_rows = jnp.concatenate(
        [grad_router, dgain_s[...], jnp.zeros((width // blocks - experts - 1, width), F32)], axis=0
    ).astype(BF16)
    for at in range(blocks):
        small = small_rows[:, at * hcols : (at + 1) * hcols]
        wop_s[:, at, :, width : width + hcols] = small.reshape(ROW, each_rows, hcols)

    my_row, my_col = me // ROW, lax.rem(me, ROW)

    def to_row(off, sems, src, dst):
        return fan(src, dst, sems, my_row * ROW + lax.rem(me + off, ROW))

    def wop_copy(off):
        return to_row(off, wop_sems, wop_s.at[lax.rem(me + off, ROW)], wop_row.at[off])

    def col_copy(off):
        to = lax.rem(me + off * ROW, peers)
        return fan(col_s.at[to // ROW], wop_col.at[off], col_sems, to)

    def colb_copy(off):
        to = lax.rem(me + off * ROW, peers)
        return fan(col_all.at[my_row], col_all.at[my_row], colb_sems, to)

    def wopb_copy(off):
        return to_row(off, wopb_sems, col_all, wop_all.at[my_col])

    cols = peers // ROW
    each(1, ROW, lambda off: wop_copy(off).start())
    wop_row[0] = wop_s[my_col]
    dwout_ring.add_far()

    dk_acc[...] = jnp.zeros_like(dk_acc)
    dv_acc[...] = jnp.zeros_like(dv_acc)
    ones = [pick_head(jnp.ones((8, hcols), F32), head) for head in range(heads)]

    def wopz_copy(off):
        to = lax.rem(place + off, TENSOR)
        return remote(wop_sum.at[place], wop_sum.at[place], wopz_sems, off, "tensor", to)

    def attend_back(row0, seen_rows):
        part = pl.ds(row0, block)
        q = q_s[part, :]
        grad = gctx_all[part, :]
        product = grad.astype(F32) * ctx_s[part, :].astype(F32)
        inner = [
            dotf(ones[head], product, ((1,), (1,)), lax.Precision.HIGHEST)[0:1]
            for head in range(heads)
        ]
        lse = [lse_s[8 * head : 8 * head + 1, part] for head in range(heads)]
        q_heads = [pick_head(q, head) for head in range(heads)]
        grad_heads = [pick_head(grad, head) for head in range(heads)]
        dq = [jnp.zeros((HEAD_DIM, block), F32) for head in range(heads)]
        for col0 in range(0, seen_rows, block):
            keys = pl.ds(col0, block)
            dk = dk_acc[keys, :]
            dv = dv_acc[keys, :]
            for head in range(heads):
                scores = dotf(k_s[keys, :], q_heads[head], ((1,), (1,)))
                soft = jnp.exp(hidden_keys(scores, row0, col0, 1) - lse[head])
                grad_soft = dotf(v_s[keys, :], grad_heads[head], ((1,), (1,)))
                grad_scores = (soft * (grad_soft - inner[head])).astype(BF16)
                dv += dotf(soft.astype(BF16), grad_heads[head])
                dk += dotf(grad_scores, q_heads[head])
                lanes = slice(head * HEAD_DIM, (head + 1) * HEAD_DIM)
                dq[head] += dotf(kt_s[lanes, keys], grad_scores)
            dk_acc[keys, :] = dk
            dv_acc[keys, :] = dv
        dq = jnp.transpose(jnp.concatenate(dq, axis=0))
        grads_s[part, 0:hcols] = (dq * SCORE_SCALE).astype(BF16)

    @pl.loop(0, TENSOR)
    def _(turn):
        blk = lax.rem(place + turn, TENSOR)

        @pl.when(turn > 0)
        def _():
            back_copy(TENSOR - turn).wait_recv()

        by_length(attend_back, blk)

        @pl.when(turn == 0)
        def _():
            dwout_ring.start_sums()
            all_of(wop_row, wop_sems).wait_recv()
            total = jnp.zeros(col_s.shape, F32)
            total = lax.fori_loop(0, ROW, lambda off, acc: acc + wop_row[off].astype(F32), total)
            col_s[...] = total.astype(BF16)
            each(1, cols, lambda off: col_copy(off).start())
            wop_col[0] = col_s[my_row]

        @pl.when(turn == 1)
        def _():
            all_of(wop_col, col_sems).wait_recv()
            total = jnp.zeros(wop_sum.shape[1:], F32)
            for at in range(cols):
                total = total + wop_col[at].astype(F32)
            wop_sum[place] = total.astype(BF16)
            for off in (2, 1, 3):
                wopz_copy(off).start()

        @pl.when(turn == 2)
        def _():
            for off in (2, 1, 3):
                wopz_copy(off).wait_recv()
            total = jnp.zeros(wop_sum.shape[1:], F32)
            for at in range(TENSOR):
                total = total + wop_sum[at].astype(F32)
            col_all[my_row] = total.astype(BF16)
            each(1, cols, lambda off: colb_copy(off).start())

        @pl.when(turn == 3)
        def _():
            all_of(col_all, colb_sems).wait_recv()
            each(1, ROW, lambda off: wopb_copy(off).start())
            wop_all[my_col] = col_all[...]

    grads_s[:, hcols : 2 * hcols] = dk_acc[...].astype(BF16)
    grads_s[:, 2 * hcols : 3 * hcols] = dv_acc[...].astype(BF16)

    def partial_rows(owner, part):
        start = owner * rows + part * half
        return dotf(grads_s[block_of(start, half), :], w_s[...], ((1,), (1,)))

    row_ring = Scatter(rows_s, via_rows, land_rows, row_sems, place)
    low, high = row_ring.low, row_ring.high
    rows_s[far, low] = partial_rows(far, 0).astype(BF16)
    rows_s[far, high] = partial_rows(far, 1).astype(BF16)
    row_ring.start_far()

    def piece_copy(off):
        to = lax.rem(me + off, peers)
        return fan(piece_s.at[to], piece_in.at[off], piece_sems, to)

    tall = width // ROW
    count = tall // each_rows

    @pl.loop(0, ROW)
    def _(turn):
        at = lax.rem(me // count + turn, ROW)
        grads = dotf(seqt_s[block_of(at * tall, tall), :], grads_s[...]).astype(BF16)
        for kind in range(3):
            piece = grads[:, kind * hcols : (kind + 1) * hcols].reshape(count, each_rows, hcols)
            piece_s[pl.ds(at * count, count), kind] = piece

        def send(to):
            off = lax.rem(to + peers - me, peers)
            pl.when(off > 0)(lambda: piece_copy(off).start())

        each(at * count, (at + 1) * count, send)

    piece_in[0] = piece_s[me]
    rows_s[right, high] = partial_rows(right, 1).astype(BF16)
    rows_s[left, low] = partial_rows(left, 0).astype(BF16)
    row_ring.start_own()
    rows_s[right, low] = partial_rows(right, 0).astype(BF16)
    rows_s[left, high] = partial_rows(left, 1).astype(BF16)
    row_ring.add_far()
    row_ring.start_sums()
    mine_s[low, :] = partial_rows(place, 0)
    mine_s[high, :] = partial_rows(place, 1)

    for ring in (tok_ring, win_ring, wout_ring, wo_ring, dwin_ring):
        ring.drain()
    for off in (2, 1, 3):
        ctx_copy(off).wait_send()
        back_copy(off).wait_send()
        wopz_copy(off).wait_send()
    all_of(out_s, mix_sems).wait_send()
    all_of(done_s, ret_sems).wait_send()
    all_of(wop_s, wop_sems).wait_send()
    all_of(wop_col, col_sems).wait_send()
    all_of(col_all, colb_sems).wait_send()
    all_of(piece_in, piece_sems).wait_recv()
    total = jnp.zeros(piece_in.shape[1:], F32)
    total = lax.fori_loop(0, peers, lambda off, acc: acc + piece_in[off].astype(F32), total)
    sum_all[me] = total.astype(BF16)

    def sum_copy(off):
        to = lax.rem(me + off, peers)
        return fan(sum_all.at[me], sum_all.at[me], sum_sems, to)

    each(1, peers, lambda off: sum_copy(off).start())

    cols = block_of(me * each_rows, each_rows)
    along = jnp.zeros((each_rows, 1), F32)
    for kind in range(3):
        weight = w_s[cols, kind * hcols : (kind + 1) * hcols].astype(F32)
        along = along + jnp.sum(total[kind] * weight, axis=1, keepdims=True)
    first_s[place] = jnp.broadcast_to(along, (each_rows, 128))

    def first_copy(off):
        to = lax.rem(place + off, TENSOR)
        return remote(first_s.at[place], first_s.at[place], first_sems, off, "tensor", to)

    for off in (2, 1, 3):
        first_copy(off).start()

    def gain_copy(off):
        to = lax.rem(me + off, peers)
        return fan(gain_all.at[me], gain_all.at[me], gain_sems, to)

    dwin_ring.wait()
    dwout_ring.wait()
    for at, (ring, part_s) in enumerate(((dwin_ring, dwin_s), (dwout_ring, dwout_s))):
        for part in (low, high):
            acc_s[at, part, :] = part_s[place, part].astype(F32) + ring.landed(part)
    win_store = pltpu.make_async_copy(acc_s.at[0], dwin_ref, store_sems.at[1])
    wout_store = pltpu.make_async_copy(acc_s.at[1], dwout_ref, store_sems.at[2])
    win_store.start()
    wout_store.start()
    all_of(wop_all, wopb_sems).wait_recv()
    all_of(wop_all, wopb_sems).wait_send()
    go_ref[...] = wop_all[:, place, :, 0:width].reshape(hcols, width).astype(F32)
    kept_rows = (experts + 1 + 15) // 16 * 16
    sums = jnp.concatenate(
        [
            wop_all[:, at, :, width : width + hcols].reshape(ROW * each_rows, hcols)[:kept_rows]
            for at in range(blocks)
        ],
        axis=1,
    ).astype(F32)
    router_ref[...] = sums[0:experts]
    dsecond_ref[...] = sums[experts : experts + 1]

    for off in (2, 1, 3):
        first_copy(off).wait_recv()
    gain_all[me] = first_s[0] + first_s[1] + first_s[2] + first_s[3]
    each(1, peers, lambda off: gain_copy(off).start())

    row_ring.wait()
    for part in (low, high):
        grad_normed = mine_s[part, :] + row_ring.landed(part)
        scaled, spread = norm_parts(tok_s[place, part].astype(F32))
        grad_scaled = grad_normed * gain_one[...]
        centered = grad_scaled - jnp.mean(grad_scaled, axis=1, keepdims=True)
        along = jnp.mean(grad_scaled * scaled, axis=1, keepdims=True)
        scaled_s[part, :] = res_s[part, :] + spread * (centered - scaled * along)
    tok_store = pltpu.make_async_copy(scaled_s, gtok_ref, store_sems.at[3])
    tok_store.start()

    all_of(piece_s, piece_sems).wait_send()
    for off in (2, 1, 3):
        first_copy(off).wait_send()
    dwout_ring.drain()
    row_ring.drain()
    all_of(sum_all, sum_sems).wait_recv()
    for at, grad_ref in enumerate((gq_ref, gk_ref, gv_ref)):
        grad_ref[...] = sum_all[:, at].reshape(width, hcols).astype(F32)
    all_of(gain_all, gain_sems).wait_recv()
    dfirst_ref[...] = jnp.transpose(gain_all[...].reshape(width, 128))[0:1] / gain_one[...]

    all_of(sum_all, sum_sems).wait_send()
    all_of(gain_all, gain_sems).wait_send()
    for store in (out_store, win_store, wout_store, tok_store):
        store.wait()


def layer(prefix, tokens, gain_one, gain_two, wq, wk, wv, wo, router, win, wout, cot, routes, prio):
    rows, width = tokens.shape
    experts = router.shape[0]
    hcols = wq.shape[1]
    fcols = win.shape[1]
    groups = rows // GROUP
    wide = experts * groups
    length = TENSOR * rows
    heads = hcols // HEAD_DIM
    peers = experts
    each_rows = width // peers
    capacity = (5 * GROUP * TOP + 4 * experts - 1) // (4 * experts)

    def dev(shape, kind):
        return jax.ShapeDtypeStruct(shape, kind)

    def low(*shape):
        return pltpu.VMEM(shape, BF16)

    def full(*shape):
        return pltpu.VMEM(shape, F32)

    def sems(count):
        return pltpu.SemaphoreType.DMA((2, count))

    return pl.pallas_call(
        functools.partial(layer_kernel, experts=experts, capacity=float(capacity)),
        out_shape=(
            dev((rows, width), BF16),
            dev((rows, width), F32),
            dev(wq.shape, F32),
            dev(wq.shape, F32),
            dev(wq.shape, F32),
            dev(wo.shape, F32),
            dev((experts, width), F32),
            dev((1, width), F32),
            dev((1, width), F32),
            dev(win.shape, F32),
            dev(wout.shape, F32),
        ),
        in_specs=[SM] + [HB] * 13,
        out_specs=(HB,) * 2 + (VM,) * 7 + (HB,) * 2,
        scratch_shapes=[
            low(TENSOR, rows, width),
            full(1, width),
            full(1, width),
            low(width, 3 * hcols),
            low(TENSOR, hcols, width),
            low(experts, width),
            low(TENSOR, width, fcols),
            low(TENSOR, fcols, width),
            full(rows, width),
            pltpu.VMEM(routes.shape, jnp.int32),
            pltpu.VMEM(prio.shape, jnp.int32),
            low(width, length),
            low(length, hcols),
            low(length, hcols),
            low(hcols, length),
            low(length, hcols),
            low(rows, wide),
            low(length, hcols),
            full(8 * heads, length),
            low(TENSOR, rows, hcols),
            low(wide, width),
            full(rows, width),
            full(rows, width),
            full(rows, 128),
            low(rows, 2 * width),
            full(rows, wide),
            low(rows, wide),
            low(experts, groups, 2 * width),
            low(experts, groups, 2 * width),
            low(experts, groups, 2 * width),
            low(experts, groups, 2 * width),
            full(2, wide, width),
            low(TENSOR, wide, fcols),
            low(TENSOR, wide, fcols),
            low(TENSOR, rows, hcols),
            low(length, hcols),
            low(rows, width),
            low(rows, experts),
            full(1, width),
            low(TENSOR, width, fcols),
            low(TENSOR, fcols, width),
            low(width, fcols),
            low(fcols, width),
            low(2, width, fcols),
            low(2, fcols, width),
            low(ROW, peers // ROW, each_rows, width + hcols),
            low(ROW, peers // ROW, each_rows, width + hcols),
            low(peers // ROW, each_rows, width + hcols),
            low(peers // ROW, each_rows, width + hcols),
            low(TENSOR, each_rows, width + hcols),
            low(peers // ROW, each_rows, width + hcols),
            low(ROW, peers // ROW, each_rows, width + hcols),
            full(length, hcols),
            full(length, hcols),
            low(length, 3 * hcols),
            low(TENSOR, rows, width),
            low(rows, width),
            low(2, rows, width),
            full(rows, width),
            low(peers, 3, each_rows, hcols),
            low(peers, 3, each_rows, hcols),
            low(peers, 3, each_rows, hcols),
            full(TENSOR, each_rows, 128),
            full(peers, each_rows, 128),
            pltpu.SemaphoreType.DMA((13,)),
            pltpu.SemaphoreType.DMA((4,)),
            pltpu.SemaphoreType.REGULAR,
            sems(6),
            sems(6),
            sems(6),
            sems(6),
            sems(TENSOR),
            pltpu.SemaphoreType.DMA((1 + wide // 128,)),
            pltpu.SemaphoreType.DMA((2,)),
            sems(TENSOR),
            sems(6),
            sems(6),
            pltpu.SemaphoreType.DMA((2,)),
            pltpu.SemaphoreType.DMA((2,)),
            pltpu.SemaphoreType.DMA((2,)),
            sems(TENSOR),
            pltpu.SemaphoreType.DMA((2,)),
            sems(6),
            pltpu.SemaphoreType.DMA((2,)),
            pltpu.SemaphoreType.DMA((2,)),
            sems(TENSOR),
            pltpu.SemaphoreType.DMA((2,)),
        ],
        compiler_params=pltpu.CompilerParams(
            collective_id=0, has_side_effects=True, vmem_limit_bytes=VMEM_BYTES
        ),
        name="layer",
    )(prefix, tokens, gain_one, gain_two, wq, wk, wv, wo, router, win, wout, cot, routes, prio)


def write_kernel(*refs):
    count = (len(refs) - 2) // 3
    in_sems, out_sems = refs[-2:]
    loads = [
        pltpu.make_async_copy(refs[at], refs[2 * count + at], in_sems.at[at]) for at in range(count)
    ]
    stores = [
        pltpu.make_async_copy(refs[2 * count + at], refs[count + at], out_sems.at[at])
        for at in range(count)
    ]
    for load in loads:
        load.start()
    for load, store in zip(loads, stores):
        load.wait()
        store.start()
    for store in stores:
        store.wait()


def write_out(results):
    count = len(results)
    return pl.pallas_call(
        write_kernel,
        out_shape=tuple(jax.ShapeDtypeStruct(x.shape, x.dtype) for x in results),
        in_specs=[HB] * count,
        out_specs=(HB,) * count,
        scratch_shapes=[pltpu.VMEM(x.shape, x.dtype) for x in results]
        + [pltpu.SemaphoreType.DMA((count,)), pltpu.SemaphoreType.DMA((count,))],
        compiler_params=pltpu.CompilerParams(vmem_limit_bytes=VMEM_BYTES),
        name="write_out",
    )(*results)


def body(
    tokens,
    first_gain,
    second_gain,
    query_weight,
    key_weight,
    value_weight,
    output_weight,
    router_weight,
    expert_in,
    expert_out,
    cotangent,
    routes,
    priority,
    prefix_len,
):
    width = tokens.shape[1]
    results = layer(
        prefix_len,
        tokens,
        first_gain.reshape(1, width),
        second_gain.reshape(1, width),
        query_weight,
        key_weight,
        value_weight,
        output_weight,
        router_weight.T,
        expert_in[0],
        expert_out[0],
        cotangent,
        routes.T,
        priority,
    )
    out, gtok, gq, gk, gv, go, grouter, dsecond, dfirst, dwin, dwout = write_out(results)
    return (
        out,
        gtok,
        dfirst.reshape(width),
        dsecond.reshape(width),
        gq,
        gk,
        gv,
        go,
        grouter.T,
        dwin[None],
        dwout[None],
    )


def solution(mesh):
    in_specs = (
        P(("expert", "tensor"), None),
        P(),
        P(),
        P(None, "tensor"),
        P(None, "tensor"),
        P(None, "tensor"),
        P("tensor", None),
        P(),
        P("expert", None, "tensor"),
        P("expert", "tensor", None),
        P(("expert", "tensor"), None),
        P(("expert", "tensor"), None),
        P(("expert", "tensor"), None),
        P("expert"),
    )
    out_specs = (
        P(("expert", "tensor"), None),
        P(("expert", "tensor"), None),
        P(),
        P(),
        P(None, "tensor"),
        P(None, "tensor"),
        P(None, "tensor"),
        P("tensor", None),
        P(),
        P("expert", None, "tensor"),
        P("expert", "tensor", None),
    )
    return jax.shard_map(body, mesh=mesh, in_specs=in_specs, out_specs=out_specs, check_vma=False)
```

```python
import functools

import jax
import jax.numpy as jnp
from jax import lax
from jax.experimental import pallas as pl
from jax.experimental.pallas import tpu as pltpu
from jax.sharding import PartitionSpec as P

HEAD_DIM = 64
GROUP = 32
TOP = 4
EPS = 1e-05
NEG = -1e30
SCORE_SCALE = HEAD_DIM**-0.5
PREFIX_MOST = 1024
ROW = 8
MESH = pl.DeviceIdType.MESH
VM = pl.BlockSpec(memory_space=pltpu.VMEM)
SM = pl.BlockSpec(memory_space=pltpu.SMEM)
HB = pl.BlockSpec(memory_space=pltpu.HBM)
TENSOR = 4
VMEM_BYTES = 58 << 20
BF16 = jnp.bfloat16
F32 = jnp.float32


def dotf(left, right, dims=((1,), (0,)), precision=None):
    return lax.dot_general(
        left, right, (dims, ((), ())), preferred_element_type=F32, precision=precision
    )


def iota(shape, axis):
    return lax.broadcasted_iota(jnp.int32, shape, axis)


def one_hot(test):
    return jnp.where(test, 1.0, 0.0).astype(BF16)


def norm_parts(values):
    center = values - jnp.mean(values, axis=1, keepdims=True)
    spread = lax.rsqrt(jnp.mean(center * center, axis=1, keepdims=True) + EPS)
    return center * spread, spread


def remote(src, dst, sems, slot, axis, to):
    return pltpu.make_async_remote_copy(
        src_ref=src,
        dst_ref=dst,
        send_sem=sems.at[0, slot],
        recv_sem=sems.at[1, slot],
        device_id={axis: to},
        device_id_type=MESH,
    )


def fan(src, dst, sems, to, lane=0):
    return pltpu.make_async_remote_copy(
        src_ref=src,
        dst_ref=dst,
        send_sem=sems.at[0],
        recv_sem=sems.at[1 + lane],
        device_id={"expert": to},
        device_id_type=MESH,
    )


def greet(peers):
    barrier = pltpu.get_barrier_semaphore()
    place = lax.axis_index("tensor")
    me = lax.axis_index("expert")

    def signal(axis, to):
        pl.semaphore_signal(barrier, inc=1, device_id={axis: to}, device_id_type=MESH)

    for off in range(1, TENSOR):
        signal("tensor", lax.rem(place + off, TENSOR))
    for off in range(1, ROW):
        signal("expert", me // ROW * ROW + lax.rem(me + off, ROW))
    for off in range(ROW, peers, ROW):
        signal("expert", lax.rem(me + off, peers))
    return TENSOR - 1 + ROW - 1 + peers // ROW - 1


def each(first, last, act):
    def one(at, _):
        act(at)
        return 0

    lax.fori_loop(first, last, one, 0)


def block_of(start, size):
    return pl.ds(pl.multiple_of(start, size), size)


def pick_head(values, head, other=0.0):
    lane = iota(values.shape, 1)
    inside = (lane >= head * HEAD_DIM) & (lane < (head + 1) * HEAD_DIM)
    return jnp.where(inside, values, jnp.full_like(values, other))


class Gather:
    def __init__(self, buf, sems, place, eighths=4):
        self.buf, self.sems, self.place = buf, sems, place
        self.right, self.left = lax.rem(place + 1, TENSOR), lax.rem(place + TENSOR - 1, TENSOR)
        size = buf.shape[1]
        cut = size * eighths // 8
        self.low, self.high = pl.ds(0, cut), pl.ds(cut, size - cut)

    def copy(self, slot):
        owner, part, to = (
            (self.place, self.low, self.right),
            (self.place, self.high, self.left),
            (self.place, self.high, self.right),
            (self.place, self.low, self.left),
            (self.left, self.low, self.right),
            (self.right, self.high, self.left),
        )[slot]
        block = self.buf.at[owner, part]
        return remote(block, block, self.sems, slot, "tensor", to)

    def start(self, slots=range(4)):
        for slot in slots:
            self.copy(slot).start()

    def forward(self):
        self.copy(0).wait_recv()
        self.copy(4).start()
        self.copy(1).wait_recv()
        self.copy(5).start()

    def wait_near(self):
        self.copy(2).wait_recv()
        self.copy(3).wait_recv()

    def wait_far(self):
        self.copy(4).wait_recv()
        self.copy(5).wait_recv()

    def drain(self):
        for slot in range(6):
            self.copy(slot).wait_send()


class Scatter:
    def __init__(self, part, via, land, sems, place):
        self.part, self.via, self.land, self.sems, self.place = part, via, land, sems, place
        self.right, self.left = lax.rem(place + 1, TENSOR), lax.rem(place + TENSOR - 1, TENSOR)
        self.far = lax.rem(place + 2, TENSOR)
        half = part.shape[1] // 2
        self.low, self.high = pl.ds(0, half), pl.ds(half, half)

    def copy(self, slot):
        block, half, to, dst = (
            (self.far, self.low, self.right, self.via),
            (self.far, self.high, self.left, self.via),
            (self.right, self.high, self.right, self.land.at[0]),
            (self.left, self.low, self.left, self.land.at[1]),
            (self.right, self.low, self.right, self.land.at[0]),
            (self.left, self.high, self.left, self.land.at[1]),
        )[slot]
        return remote(self.part.at[block, half], dst.at[half], self.sems, slot, "tensor", to)

    def start_far(self):
        self.copy(0).start()
        self.copy(1).start()

    def start_own(self):
        self.copy(2).start()
        self.copy(3).start()

    def add_far(self):
        self.copy(0).wait_recv()
        self.part[self.right, self.low] = (
            self.part[self.right, self.low].astype(F32) + self.via[self.low].astype(F32)
        ).astype(BF16)
        self.copy(1).wait_recv()
        self.part[self.left, self.high] = (
            self.part[self.left, self.high].astype(F32) + self.via[self.high].astype(F32)
        ).astype(BF16)

    def start_sums(self):
        self.copy(4).start()
        self.copy(5).start()

    def wait(self):
        for slot in range(2, 6):
            self.copy(slot).wait_recv()

    def landed(self, rows):
        return self.land[0, rows].astype(F32) + self.land[1, rows].astype(F32)

    def drain(self):
        for slot in range(6):
            self.copy(slot).wait_send()


def layer_kernel(
    prefix_ref,
    tok_hbm,
    gain_one_hbm,
    gain_two_hbm,
    wq_hbm,
    wk_hbm,
    wv_hbm,
    wo_hbm,
    router_hbm,
    win_hbm,
    wout_hbm,
    cot_hbm,
    routes_hbm,
    prio_hbm,
    out_ref,
    gtok_ref,
    gq_ref,
    gk_ref,
    gv_ref,
    go_ref,
    router_ref,
    dsecond_ref,
    dfirst_ref,
    dwin_ref,
    dwout_ref,
    tok_s,
    gain_one,
    gain_two,
    w_s,
    wo_s,
    router_s,
    win_s,
    wout_s,
    cot_s,
    routes_s,
    prio_s,
    seqt_s,
    q_s,
    k_s,
    kt_s,
    v_s,
    kept_s,
    ctx_s,
    lse_s,
    ctx_all,
    wide_router,
    res_s,
    scaled_s,
    spread_s,
    pair_s,
    weight_s,
    low_s,
    out_s,
    in_s,
    done_s,
    ret_s,
    acc_s,
    hidden_s,
    gpre_s,
    gctx_s,
    gctx_all,
    gatt_s,
    glog_s,
    dgain_s,
    dwin_s,
    dwout_s,
    via_win,
    via_wout,
    land_win,
    land_wout,
    wop_s,
    wop_row,
    col_s,
    wop_col,
    wop_sum,
    col_all,
    wop_all,
    dk_acc,
    dv_acc,
    grads_s,
    rows_s,
    via_rows,
    land_rows,
    mine_s,
    piece_s,
    piece_in,
    sum_all,
    first_s,
    gain_all,
    local_sems,
    store_sems,
    plane_sem,
    tok_sems,
    win_sems,
    wout_sems,
    wo_sems,
    ctx_sems,
    mix_sems,
    ret_sems,
    back_sems,
    dwin_sems,
    dwout_sems,
    wop_sems,
    col_sems,
    colb_sems,
    wopz_sems,
    wopb_sems,
    row_sems,
    piece_sems,
    sum_sems,
    first_sems,
    gain_sems,
    *,
    experts,
    capacity,
):
    place = lax.axis_index("tensor")
    me = lax.axis_index("expert")
    right, left = lax.rem(place + 1, TENSOR), lax.rem(place + TENSOR - 1, TENSOR)
    far = lax.rem(place + 2, TENSOR)
    _, rows, width = tok_s.shape
    length, hcols = q_s.shape
    heads = hcols // HEAD_DIM
    groups = rows // GROUP
    wide = experts * groups
    peers = experts
    greeted = greet(peers)

    loads = [
        (tok_hbm, tok_s.at[place]),
        (gain_one_hbm, gain_one),
        (wq_hbm, w_s.at[:, pl.ds(0, hcols)]),
        (wk_hbm, w_s.at[:, pl.ds(hcols, hcols)]),
        (wv_hbm, w_s.at[:, pl.ds(2 * hcols, hcols)]),
        (routes_hbm, routes_s),
        (prio_hbm, prio_s),
        (wo_hbm, wo_s.at[place]),
        (win_hbm, win_s.at[place]),
        (wout_hbm, wout_s.at[place]),
        (gain_two_hbm, gain_two),
        (router_hbm, router_s),
        (cot_hbm, cot_s),
    ]
    loads = [
        pltpu.make_async_copy(src, dst, local_sems.at[at]) for at, (src, dst) in enumerate(loads)
    ]
    for load in loads:
        load.start()

    def all_of(buf, sems):
        most = buf.at[pl.ds(1, buf.shape[0] - 1)]
        return fan(most, most, sems, lax.rem(me + 1, peers))

    batch = 128 // groups

    tok_ring = Gather(tok_s, tok_sems, place)
    win_ring = Gather(win_s, win_sems, place, 4)
    wout_ring = Gather(wout_s, wout_sems, place, 4)
    wo_ring = Gather(wo_s, wo_sems, place)
    loads[0].wait()
    pl.semaphore_wait(pltpu.get_barrier_semaphore(), greeted)
    tok_ring.start()
    for off in range(ROW, peers, ROW):
        to = lax.rem(me + off, peers)
        pl.semaphore_signal(plane_sem, inc=1, device_id={"expert": to}, device_id_type=MESH)
    for load in loads[1:5]:
        load.wait()

    half = rows // 2

    def project(owner):
        @pl.loop(0, rows // 128)
        def _(at):
            start = at * 128
            scaled, _ = norm_parts(tok_s[owner, block_of(start, 128)].astype(F32))
            normed = (scaled * gain_one[...]).astype(BF16)
            to = block_of(owner * rows + start, 128)
            seqt_s[:, to] = jnp.transpose(normed)
            out = dotf(normed, w_s[...]).astype(BF16)
            q_s[to, :] = out[:, 0:hcols] * SCORE_SCALE
            k_s[to, :] = out[:, hcols : 2 * hcols]
            kt_s[:, to] = jnp.transpose(out[:, hcols : 2 * hcols])
            v_s[to, :] = out[:, 2 * hcols : 3 * hcols]

    project(place)
    tok_ring.forward()

    loads[5].wait()
    loads[6].wait()
    size = GROUP
    to_wide = one_hot(iota((experts, wide), 0) == iota((experts, wide), 1) // groups)
    prio = prio_s[...].astype(F32).astype(BF16)
    spread_rows = dotf(one_hot((iota((rows, groups), 0) // size) == iota((rows, groups), 1)), prio)
    at_col = (iota((rows, size), 0) % size) == iota((rows, size), 1)
    prio_col = jnp.sum(jnp.where(at_col, spread_rows, 0.0), axis=1, keepdims=True)
    group_tok = one_hot((iota((groups, rows), 1) // size) == iota((groups, rows), 0))
    spread_cols = dotf(prio, group_tok, ((0,), (0,)))
    at_row = (iota((size, rows), 1) % size) == iota((size, rows), 0)
    prio_row = jnp.sum(jnp.where(at_row, spread_cols, 0.0), axis=0, keepdims=True)
    named = routes_s[0:1, :] == iota((experts, rows), 0)
    for pick in range(1, TOP):
        named = named | (routes_s[pick : pick + 1, :] == iota((experts, rows), 0))
    own_group = (iota((rows, wide), 0) // size) == (iota((rows, wide), 1) % groups)
    member = jnp.where(own_group, dotf(one_hot(named), to_wide, ((0,), (0,))), 0.0)
    rank = dotf(one_hot(prio_row < prio_col), member.astype(BF16))
    kept_s[...] = jnp.where(rank < capacity, member, 0.0).astype(BF16)

    tok_ring.copy(2).wait_recv()
    project(left)
    tok_ring.copy(3).wait_recv()
    project(right)
    for load in loads[7:10]:
        load.wait()
    tok_ring.wait_far()
    wo_ring.start()
    win_ring.start((0, 1))
    project(far)

    prefix = prefix_ref[0]
    block = rows

    def hidden_keys(scores, row0, col0, row_axis):
        if isinstance(row0, int) and col0 + block - 1 <= row0:
            return scores
        line = (block, 1) if row_axis == 0 else (1, block)
        until = iota(line, row_axis) + (row0 + 1 - col0)
        if col0 < PREFIX_MOST:
            until = jnp.maximum(until, prefix - col0)
        seen = iota((block, block), 1 - row_axis) < until
        return jnp.where(seen, scores, NEG)

    def ctx_copy(off):
        to = lax.rem(place + off, TENSOR)
        src = ctx_s.at[block_of(to * rows, rows), :]
        return remote(src, ctx_all.at[place], ctx_sems, off, "tensor", to)

    def attend(row0, seen_rows):
        part_rows = pl.ds(row0, block)
        q = q_s[part_rows, :]
        starts = range(0, seen_rows, block)
        merged = jnp.zeros((block, hcols), F32)
        for head in range(heads):
            q_head = pick_head(q, head)
            scores = []
            for col0 in starts:
                part = dotf(q_head, k_s[col0 : col0 + block, :], ((1,), (1,)))
                scores.append(hidden_keys(part, row0, col0, 0))
            peak = functools.reduce(
                jnp.maximum, [jnp.max(part, axis=1, keepdims=True) for part in scores]
            )
            acc = jnp.zeros((block, hcols), F32)
            for part, col0 in zip(scores, starts):
                soft = jnp.exp(part - peak).astype(BF16)
                acc = acc + dotf(soft, pick_head(v_s[col0 : col0 + block, :], head, 1.0))
            lane = HEAD_DIM if head == 0 else 0
            total = acc[:, lane : lane + 1]
            merged = merged + pick_head(acc * (1.0 / total), head)
            lse = jnp.broadcast_to(peak + jnp.log(total), (block, 128))
            lse_s[8 * head : 8 * head + 8, part_rows] = jnp.transpose(lse)[:8]
        ctx_s[part_rows, :] = merged.astype(BF16)

    def by_length(act, blk):
        short = PREFIX_MOST // block
        pl.when(blk < short)(lambda: act(pl.multiple_of(blk * block, block), PREFIX_MOST))
        for at in range(short, TENSOR):
            pl.when(blk == at)(functools.partial(act, at * block, (at + 1) * block))

    @pl.loop(0, TENSOR)
    def _(turn):
        blk = lax.rem(place + 1 + turn, TENSOR)
        by_length(attend, blk)

        @pl.when(turn < TENSOR - 1)
        def _():
            ctx_copy(turn + 1).start()

        @pl.when(turn == 1)
        def _():
            wo_ring.forward()

    wout_ring.start((0, 1))
    win_ring.forward()
    win_ring.start((2, 3))
    ctx_all[place] = ctx_s[block_of(place * rows, rows), :]
    for load in loads[10:]:
        load.wait()
    wide_router[...] = dotf(to_wide, router_s[...], ((0,), (0,))).astype(BF16)
    pair_s[:, 0:width] = cot_s[...].astype(BF16)
    wo_ring.wait_near()
    wo_ring.wait_far()
    wo_full = wo_s.reshape(TENSOR * hcols, width)
    for off in (2, 1, 3):
        ctx_copy(off).wait_recv()

    step_rows = 128

    @pl.loop(0, rows // step_rows)
    def _(step):
        part = block_of(step * step_rows, step_rows)
        ctx = jnp.concatenate([ctx_all[at, part, :] for at in range(TENSOR)], axis=1)
        residual = tok_s[place, part].astype(F32) + dotf(ctx, wo_full[...])
        res_s[part, :] = residual
        scaled, spread = norm_parts(residual)
        scaled_s[part, :] = scaled
        spread_s[part, :] = jnp.broadcast_to(spread, (step_rows, 128))
        mixer = (scaled * gain_two[...]).astype(BF16)
        pair_s[part, width : 2 * width] = mixer
        logits = dotf(mixer, wide_router[...], ((1,), (1,)))
        kept = kept_s[part, :].astype(F32)
        terms = jnp.where(kept > 0.0, jnp.exp(logits), 0.0)
        total = jnp.sum(terms, axis=0, keepdims=True)
        count = jnp.sum(kept, axis=0, keepdims=True)
        weight = terms / jnp.where(count > 0.0, total, 1.0)
        weight_s[part, :] = weight
        low_s[part, :] = weight.astype(BF16)

    @pl.loop(0, wide // 128)
    def _(blk):
        mixed = dotf(low_s[:, block_of(blk * 128, 128)], pair_s[...], ((0,), (0,))).astype(BF16)
        count = 128 // groups
        out_s[pl.ds(blk * count, count)] = mixed.reshape(count, groups, 2 * width)

    def mix_copy(off):
        to = lax.rem(me + off, peers)
        return fan(out_s.at[to], in_s.at[off], mix_sems, to, off // batch)

    pl.semaphore_wait(plane_sem, peers // ROW - 1)
    each(1, peers, lambda off: mix_copy(off).start())
    in_s[0] = out_s[me]
    wout_ring.start((2, 3))

    def ret_copy(off):
        to = lax.rem(me + peers - off, peers)
        return fan(done_s.at[off], ret_s.at[me], ret_sems, to)

    def expert_part(chunk, slices, start, count=128):
        part = block_of(chunk * count, count)
        sources = count // groups
        rows_in = in_s[pl.ds(chunk * sources, sources)].reshape(count, 2 * width)
        grad = rows_in[:, 0:width]
        mixed = rows_in[:, width : 2 * width]
        for at in slices:
            at = lax.rem(place + at, TENSOR)
            pre = dotf(mixed, win_s[at])
            sigma = 1.0 / (1.0 + jnp.exp(-pre))
            hidden = (pre * sigma).astype(BF16)
            grad_hidden = dotf(grad, wout_s[at], ((1,), (1,)))
            grad_pre = (grad_hidden * (sigma * (1.0 + pre * (1.0 - sigma)))).astype(BF16)
            hidden_s[at, part, :] = hidden
            gpre_s[at, part, :] = grad_pre
            returned = dotf(hidden, wout_s[at])
            grad_mixed = dotf(grad_pre, win_s[at], ((1,), (1,)))
            if start:
                acc_s[0, part, :] = returned
                acc_s[1, part, :] = grad_mixed
                start = False
            else:
                acc_s[0, part, :] += returned
                acc_s[1, part, :] += grad_mixed

    win_ring.wait_near()

    @pl.loop(0, peers // batch)
    def _(chunk):

        @pl.when(chunk == 0)
        def _():
            came = in_s.at[pl.ds(1, batch - 1)]
            fan(came, came, mix_sems, lax.rem(me + 1, peers), 0).wait_recv()

        @pl.when(chunk > 0)
        def _():
            came = in_s.at[pl.ds(chunk * batch, batch)]
            fan(came, came, mix_sems, lax.rem(me + 1, peers), chunk).wait_recv()

        expert_part(chunk, (0,), True)

        @pl.when(chunk == 0)
        def _():
            wout_ring.forward()

    wout_ring.wait_near()

    @pl.loop(0, peers // batch)
    def _(turn):
        expert_part(turn // 2, (3 - 2 * lax.rem(turn, 2),), False, 256)

    win_ring.wait_far()
    wout_ring.wait_far()

    @pl.loop(0, peers // (2 * batch))
    def _(chunk):
        expert_part(chunk, (2,), False, 256)
        part = block_of(chunk * 256, 256)
        begin = chunk * 2 * batch
        done = jnp.concatenate([acc_s[0, part, :], acc_s[1, part, :]], axis=1).astype(BF16)
        done_s[pl.ds(begin, 2 * batch)] = done.reshape(2 * batch, groups, 2 * width)
        each(jnp.maximum(begin, 1), begin + 2 * batch, lambda off: ret_copy(off).start())

    ret_s[me] = done_s[0]

    dwin_ring = Scatter(dwin_s, via_win, land_win, dwin_sems, place)
    dwout_ring = Scatter(dwout_s, via_wout, land_wout, dwout_sems, place)

    def expert_grads(off):
        at = lax.rem(place + off, TENSOR)
        rows_in = in_s[...].reshape(wide, 2 * width)
        dwin_s[at] = dotf(rows_in[:, width : 2 * width], gpre_s[at], ((0,), (0,))).astype(BF16)
        dwout_s[at] = dotf(hidden_s[at], rows_in[:, 0:width], ((0,), (0,))).astype(BF16)

    @pl.loop(0, TENSOR)
    def _(turn):
        expert_grads(lax.rem(turn + 2, TENSOR))

        @pl.when(turn == 0)
        def _():
            dwin_ring.start_far()
            dwout_ring.start_far()

    dwin_ring.start_own()
    dwout_ring.start_own()
    all_of(ret_s, ret_sems).wait_recv()

    dgain_s[...] = jnp.zeros_like(dgain_s)
    from_wide = one_hot(iota((wide, experts), 0) // groups == iota((wide, experts), 1))

    step_rows = 256

    @pl.loop(0, rows // step_rows)
    def _(step):
        part = block_of(step * step_rows, step_rows)
        came = ret_s[...].reshape(wide, 2 * width)
        low = low_s[part, :]
        weight = weight_s[part, :]
        back = dotf(low, came)
        kept_s[part, :] = (res_s[part, :] + back[:, 0:width]).astype(BF16)
        grad_weight = dotf(pair_s[part, :], came, ((1,), (1,)))
        inner = jnp.sum(weight * grad_weight, axis=0, keepdims=True)
        grad_logits = (weight * (grad_weight - inner)).astype(BF16)
        glog_s[part, :] = dotf(grad_logits, from_wide).astype(BF16)
        grad_mixer = back[:, width : 2 * width] + dotf(grad_logits, wide_router[...])
        scaled = scaled_s[part, :]
        dgain_s[...] += jnp.sum(grad_mixer * scaled, axis=0, keepdims=True)
        grad_scaled = grad_mixer * gain_two[...]
        centered = grad_scaled - jnp.mean(grad_scaled, axis=1, keepdims=True)
        along = jnp.mean(grad_scaled * scaled, axis=1, keepdims=True)
        grad_res = cot_s[part, :] + spread_s[part, 0:1] * (centered - scaled * along)
        res_s[part, :] = grad_res
        grad_att = grad_res.astype(BF16)
        gatt_s[part, :] = grad_att
        grad_ctx = dotf(grad_att, wo_full[...], ((1,), (1,))).astype(BF16)
        for at in range(TENSOR):
            gctx_s[at, part, :] = grad_ctx[:, at * hcols : (at + 1) * hcols]

    def back_copy(off):
        to = lax.rem(place + off, TENSOR)
        dst = gctx_all.at[block_of(place * rows, rows), :]
        return remote(gctx_s.at[to], dst, back_sems, off, "tensor", to)

    for off in (3, 2, 1):
        back_copy(off).start()
    dwin_ring.add_far()
    dwin_ring.start_sums()
    out_store = pltpu.make_async_copy(kept_s, out_ref, store_sems.at[0])
    out_store.start()
    gctx_all[block_of(place * rows, rows), :] = gctx_s[place]

    each_rows = width // peers
    for at in range(TENSOR):
        grad_wo = dotf(ctx_all[at], gatt_s[...], ((0,), (0,))).astype(BF16)
        wop_s[:, at, :, 0:width] = grad_wo.reshape(ROW, each_rows, width)
    grad_router = dotf(glog_s[...], pair_s[:, width : 2 * width], ((0,), (0,)))
    blocks = width // hcols
    small_rows = jnp.concatenate(
        [grad_router, dgain_s[...], jnp.zeros((width // blocks - experts - 1, width), F32)], axis=0
    ).astype(BF16)
    for at in range(blocks):
        small = small_rows[:, at * hcols : (at + 1) * hcols]
        wop_s[:, at, :, width : width + hcols] = small.reshape(ROW, each_rows, hcols)

    my_row, my_col = me // ROW, lax.rem(me, ROW)

    def to_row(off, sems, src, dst):
        return fan(src, dst, sems, my_row * ROW + lax.rem(me + off, ROW))

    def wop_copy(off):
        return to_row(off, wop_sems, wop_s.at[lax.rem(me + off, ROW)], wop_row.at[off])

    def col_copy(off):
        to = lax.rem(me + off * ROW, peers)
        return fan(col_s.at[to // ROW], wop_col.at[off], col_sems, to)

    def colb_copy(off):
        to = lax.rem(me + off * ROW, peers)
        return fan(col_all.at[my_row], col_all.at[my_row], colb_sems, to)

    def wopb_copy(off):
        return to_row(off, wopb_sems, col_all, wop_all.at[my_col])

    cols = peers // ROW
    each(1, ROW, lambda off: wop_copy(off).start())
    wop_row[0] = wop_s[my_col]
    dwout_ring.add_far()

    dk_acc[...] = jnp.zeros_like(dk_acc)
    dv_acc[...] = jnp.zeros_like(dv_acc)
    ones = [pick_head(jnp.ones((8, hcols), F32), head) for head in range(heads)]

    def wopz_copy(off):
        to = lax.rem(place + off, TENSOR)
        return remote(wop_sum.at[place], wop_sum.at[place], wopz_sems, off, "tensor", to)

    def attend_back(row0, seen_rows):
        part = pl.ds(row0, block)
        q = q_s[part, :]
        grad = gctx_all[part, :]
        product = grad.astype(F32) * ctx_s[part, :].astype(F32)
        inner = [
            dotf(ones[head], product, ((1,), (1,)), lax.Precision.HIGHEST)[0:1]
            for head in range(heads)
        ]
        lse = [lse_s[8 * head : 8 * head + 1, part] for head in range(heads)]
        q_heads = [pick_head(q, head) for head in range(heads)]
        grad_heads = [pick_head(grad, head) for head in range(heads)]
        dq = [jnp.zeros((HEAD_DIM, block), F32) for head in range(heads)]
        for col0 in range(0, seen_rows, block):
            keys = pl.ds(col0, block)
            dk = dk_acc[keys, :]
            dv = dv_acc[keys, :]
            for head in range(heads):
                scores = dotf(k_s[keys, :], q_heads[head], ((1,), (1,)))
                soft = jnp.exp(hidden_keys(scores, row0, col0, 1) - lse[head])
                grad_soft = dotf(v_s[keys, :], grad_heads[head], ((1,), (1,)))
                grad_scores = (soft * (grad_soft - inner[head])).astype(BF16)
                dv += dotf(soft.astype(BF16), grad_heads[head])
                dk += dotf(grad_scores, q_heads[head])
                lanes = slice(head * HEAD_DIM, (head + 1) * HEAD_DIM)
                dq[head] += dotf(kt_s[lanes, keys], grad_scores)
            dk_acc[keys, :] = dk
            dv_acc[keys, :] = dv
        dq = jnp.transpose(jnp.concatenate(dq, axis=0))
        grads_s[part, 0:hcols] = (dq * SCORE_SCALE).astype(BF16)

    @pl.loop(0, TENSOR)
    def _(turn):
        blk = lax.rem(place + turn, TENSOR)

        @pl.when(turn > 0)
        def _():
            back_copy(TENSOR - turn).wait_recv()

        by_length(attend_back, blk)

        @pl.when(turn == 0)
        def _():
            dwout_ring.start_sums()
            all_of(wop_row, wop_sems).wait_recv()
            total = jnp.zeros(col_s.shape, F32)
            total = lax.fori_loop(0, ROW, lambda off, acc: acc + wop_row[off].astype(F32), total)
            col_s[...] = total.astype(BF16)
            each(1, cols, lambda off: col_copy(off).start())
            wop_col[0] = col_s[my_row]

        @pl.when(turn == 1)
        def _():
            all_of(wop_col, col_sems).wait_recv()
            total = jnp.zeros(wop_sum.shape[1:], F32)
            for at in range(cols):
                total = total + wop_col[at].astype(F32)
            wop_sum[place] = total.astype(BF16)
            for off in (2, 1, 3):
                wopz_copy(off).start()

        @pl.when(turn == 2)
        def _():
            for off in (2, 1, 3):
                wopz_copy(off).wait_recv()
            total = jnp.zeros(wop_sum.shape[1:], F32)
            for at in range(TENSOR):
                total = total + wop_sum[at].astype(F32)
            col_all[my_row] = total.astype(BF16)
            each(1, cols, lambda off: colb_copy(off).start())

        @pl.when(turn == 3)
        def _():
            all_of(col_all, colb_sems).wait_recv()
            each(1, ROW, lambda off: wopb_copy(off).start())
            wop_all[my_col] = col_all[...]

    grads_s[:, hcols : 2 * hcols] = dk_acc[...].astype(BF16)
    grads_s[:, 2 * hcols : 3 * hcols] = dv_acc[...].astype(BF16)

    def partial_rows(owner, part):
        start = owner * rows + part * half
        return dotf(grads_s[block_of(start, half), :], w_s[...], ((1,), (1,)))

    row_ring = Scatter(rows_s, via_rows, land_rows, row_sems, place)
    low, high = row_ring.low, row_ring.high
    rows_s[far, low] = partial_rows(far, 0).astype(BF16)
    rows_s[far, high] = partial_rows(far, 1).astype(BF16)
    row_ring.start_far()

    def piece_copy(off):
        to = lax.rem(me + off, peers)
        return fan(piece_s.at[to], piece_in.at[off], piece_sems, to)

    tall = width // ROW
    count = tall // each_rows

    @pl.loop(0, ROW)
    def _(turn):
        at = lax.rem(me // count + turn, ROW)
        grads = dotf(seqt_s[block_of(at * tall, tall), :], grads_s[...]).astype(BF16)
        for kind in range(3):
            piece = grads[:, kind * hcols : (kind + 1) * hcols].reshape(count, each_rows, hcols)
            piece_s[pl.ds(at * count, count), kind] = piece

        def send(to):
            off = lax.rem(to + peers - me, peers)
            pl.when(off > 0)(lambda: piece_copy(off).start())

        each(at * count, (at + 1) * count, send)

    piece_in[0] = piece_s[me]
    rows_s[right, high] = partial_rows(right, 1).astype(BF16)
    rows_s[left, low] = partial_rows(left, 0).astype(BF16)
    row_ring.start_own()
    rows_s[right, low] = partial_rows(right, 0).astype(BF16)
    rows_s[left, high] = partial_rows(left, 1).astype(BF16)
    row_ring.add_far()
    row_ring.start_sums()
    mine_s[low, :] = partial_rows(place, 0)
    mine_s[high, :] = partial_rows(place, 1)

    for ring in (tok_ring, win_ring, wout_ring, wo_ring, dwin_ring):
        ring.drain()
    for off in (2, 1, 3):
        ctx_copy(off).wait_send()
        back_copy(off).wait_send()
        wopz_copy(off).wait_send()
    all_of(out_s, mix_sems).wait_send()
    all_of(done_s, ret_sems).wait_send()
    all_of(wop_s, wop_sems).wait_send()
    all_of(wop_col, col_sems).wait_send()
    all_of(col_all, colb_sems).wait_send()
    all_of(piece_in, piece_sems).wait_recv()
    total = jnp.zeros(piece_in.shape[1:], F32)
    total = lax.fori_loop(0, peers, lambda off, acc: acc + piece_in[off].astype(F32), total)
    sum_all[me] = total.astype(BF16)

    def sum_copy(off):
        to = lax.rem(me + off, peers)
        return fan(sum_all.at[me], sum_all.at[me], sum_sems, to)

    each(1, peers, lambda off: sum_copy(off).start())

    cols = block_of(me * each_rows, each_rows)
    along = jnp.zeros((each_rows, 1), F32)
    for kind in range(3):
        weight = w_s[cols, kind * hcols : (kind + 1) * hcols].astype(F32)
        along = along + jnp.sum(total[kind] * weight, axis=1, keepdims=True)
    first_s[place] = jnp.broadcast_to(along, (each_rows, 128))

    def first_copy(off):
        to = lax.rem(place + off, TENSOR)
        return remote(first_s.at[place], first_s.at[place], first_sems, off, "tensor", to)

    for off in (2, 1, 3):
        first_copy(off).start()

    def gain_copy(off):
        to = lax.rem(me + off, peers)
        return fan(gain_all.at[me], gain_all.at[me], gain_sems, to)

    dwin_ring.wait()
    dwout_ring.wait()
    for at, (ring, part_s) in enumerate(((dwin_ring, dwin_s), (dwout_ring, dwout_s))):
        for part in (low, high):
            acc_s[at, part, :] = part_s[place, part].astype(F32) + ring.landed(part)
    win_store = pltpu.make_async_copy(acc_s.at[0], dwin_ref, store_sems.at[1])
    wout_store = pltpu.make_async_copy(acc_s.at[1], dwout_ref, store_sems.at[2])
    win_store.start()
    wout_store.start()
    all_of(wop_all, wopb_sems).wait_recv()
    all_of(wop_all, wopb_sems).wait_send()
    go_ref[...] = wop_all[:, place, :, 0:width].reshape(hcols, width).astype(F32)
    kept_rows = (experts + 1 + 15) // 16 * 16
    sums = jnp.concatenate(
        [
            wop_all[:, at, :, width : width + hcols].reshape(ROW * each_rows, hcols)[:kept_rows]
            for at in range(blocks)
        ],
        axis=1,
    ).astype(F32)
    router_ref[...] = sums[0:experts]
    dsecond_ref[...] = sums[experts : experts + 1]

    for off in (2, 1, 3):
        first_copy(off).wait_recv()
    gain_all[me] = first_s[0] + first_s[1] + first_s[2] + first_s[3]
    each(1, peers, lambda off: gain_copy(off).start())

    row_ring.wait()
    for part in (low, high):
        grad_normed = mine_s[part, :] + row_ring.landed(part)
        scaled, spread = norm_parts(tok_s[place, part].astype(F32))
        grad_scaled = grad_normed * gain_one[...]
        centered = grad_scaled - jnp.mean(grad_scaled, axis=1, keepdims=True)
        along = jnp.mean(grad_scaled * scaled, axis=1, keepdims=True)
        scaled_s[part, :] = res_s[part, :] + spread * (centered - scaled * along)
    tok_store = pltpu.make_async_copy(scaled_s, gtok_ref, store_sems.at[3])
    tok_store.start()

    all_of(piece_s, piece_sems).wait_send()
    for off in (2, 1, 3):
        first_copy(off).wait_send()
    dwout_ring.drain()
    row_ring.drain()
    all_of(sum_all, sum_sems).wait_recv()
    for at, grad_ref in enumerate((gq_ref, gk_ref, gv_ref)):
        grad_ref[...] = sum_all[:, at].reshape(width, hcols).astype(F32)
    all_of(gain_all, gain_sems).wait_recv()
    dfirst_ref[...] = jnp.transpose(gain_all[...].reshape(width, 128))[0:1] / gain_one[...]

    all_of(sum_all, sum_sems).wait_send()
    all_of(gain_all, gain_sems).wait_send()
    for store in (out_store, win_store, wout_store, tok_store):
        store.wait()


def layer(prefix, tokens, gain_one, gain_two, wq, wk, wv, wo, router, win, wout, cot, routes, prio):
    rows, width = tokens.shape
    experts = router.shape[0]
    hcols = wq.shape[1]
    fcols = win.shape[1]
    groups = rows // GROUP
    wide = experts * groups
    length = TENSOR * rows
    heads = hcols // HEAD_DIM
    peers = experts
    each_rows = width // peers
    capacity = (5 * GROUP * TOP + 4 * experts - 1) // (4 * experts)

    def dev(shape, kind):
        return jax.ShapeDtypeStruct(shape, kind)

    def low(*shape):
        return pltpu.VMEM(shape, BF16)

    def full(*shape):
        return pltpu.VMEM(shape, F32)

    def sems(count):
        return pltpu.SemaphoreType.DMA((2, count))

    return pl.pallas_call(
        functools.partial(layer_kernel, experts=experts, capacity=float(capacity)),
        out_shape=(
            dev((rows, width), BF16),
            dev((rows, width), F32),
            dev(wq.shape, F32),
            dev(wq.shape, F32),
            dev(wq.shape, F32),
            dev(wo.shape, F32),
            dev((experts, width), F32),
            dev((1, width), F32),
            dev((1, width), F32),
            dev(win.shape, F32),
            dev(wout.shape, F32),
        ),
        in_specs=[SM] + [HB] * 13,
        out_specs=(HB,) * 2 + (VM,) * 7 + (HB,) * 2,
        scratch_shapes=[
            low(TENSOR, rows, width),
            full(1, width),
            full(1, width),
            low(width, 3 * hcols),
            low(TENSOR, hcols, width),
            low(experts, width),
            low(TENSOR, width, fcols),
            low(TENSOR, fcols, width),
            full(rows, width),
            pltpu.VMEM(routes.shape, jnp.int32),
            pltpu.VMEM(prio.shape, jnp.int32),
            low(width, length),
            low(length, hcols),
            low(length, hcols),
            low(hcols, length),
            low(length, hcols),
            low(rows, wide),
            low(length, hcols),
            full(8 * heads, length),
            low(TENSOR, rows, hcols),
            low(wide, width),
            full(rows, width),
            full(rows, width),
            full(rows, 128),
            low(rows, 2 * width),
            full(rows, wide),
            low(rows, wide),
            low(experts, groups, 2 * width),
            low(experts, groups, 2 * width),
            low(experts, groups, 2 * width),
            low(experts, groups, 2 * width),
            full(2, wide, width),
            low(TENSOR, wide, fcols),
            low(TENSOR, wide, fcols),
            low(TENSOR, rows, hcols),
            low(length, hcols),
            low(rows, width),
            low(rows, experts),
            full(1, width),
            low(TENSOR, width, fcols),
            low(TENSOR, fcols, width),
            low(width, fcols),
            low(fcols, width),
            low(2, width, fcols),
            low(2, fcols, width),
            low(ROW, peers // ROW, each_rows, width + hcols),
            low(ROW, peers // ROW, each_rows, width + hcols),
            low(peers // ROW, each_rows, width + hcols),
            low(peers // ROW, each_rows, width + hcols),
            low(TENSOR, each_rows, width + hcols),
            low(peers // ROW, each_rows, width + hcols),
            low(ROW, peers // ROW, each_rows, width + hcols),
            full(length, hcols),
            full(length, hcols),
            low(length, 3 * hcols),
            low(TENSOR, rows, width),
            low(rows, width),
            low(2, rows, width),
            full(rows, width),
            low(peers, 3, each_rows, hcols),
            low(peers, 3, each_rows, hcols),
            low(peers, 3, each_rows, hcols),
            full(TENSOR, each_rows, 128),
            full(peers, each_rows, 128),
            pltpu.SemaphoreType.DMA((13,)),
            pltpu.SemaphoreType.DMA((4,)),
            pltpu.SemaphoreType.REGULAR,
            sems(6),
            sems(6),
            sems(6),
            sems(6),
            sems(TENSOR),
            pltpu.SemaphoreType.DMA((1 + wide // 128,)),
            pltpu.SemaphoreType.DMA((2,)),
            sems(TENSOR),
            sems(6),
            sems(6),
            pltpu.SemaphoreType.DMA((2,)),
            pltpu.SemaphoreType.DMA((2,)),
            pltpu.SemaphoreType.DMA((2,)),
            sems(TENSOR),
            pltpu.SemaphoreType.DMA((2,)),
            sems(6),
            pltpu.SemaphoreType.DMA((2,)),
            pltpu.SemaphoreType.DMA((2,)),
            sems(TENSOR),
            pltpu.SemaphoreType.DMA((2,)),
        ],
        compiler_params=pltpu.CompilerParams(
            collective_id=0, has_side_effects=True, vmem_limit_bytes=VMEM_BYTES
        ),
        name="layer",
    )(prefix, tokens, gain_one, gain_two, wq, wk, wv, wo, router, win, wout, cot, routes, prio)


def write_kernel(*refs):
    count = (len(refs) - 2) // 3
    in_sems, out_sems = refs[-2:]
    loads = [
        pltpu.make_async_copy(refs[at], refs[2 * count + at], in_sems.at[at]) for at in range(count)
    ]
    stores = [
        pltpu.make_async_copy(refs[2 * count + at], refs[count + at], out_sems.at[at])
        for at in range(count)
    ]
    for load in loads:
        load.start()
    for load, store in zip(loads, stores):
        load.wait()
        store.start()
    for store in stores:
        store.wait()


def write_out(results):
    count = len(results)
    return pl.pallas_call(
        write_kernel,
        out_shape=tuple(jax.ShapeDtypeStruct(x.shape, x.dtype) for x in results),
        in_specs=[HB] * count,
        out_specs=(HB,) * count,
        scratch_shapes=[pltpu.VMEM(x.shape, x.dtype) for x in results]
        + [pltpu.SemaphoreType.DMA((count,)), pltpu.SemaphoreType.DMA((count,))],
        compiler_params=pltpu.CompilerParams(vmem_limit_bytes=VMEM_BYTES),
        name="write_out",
    )(*results)


def body(
    tokens,
    first_gain,
    second_gain,
    query_weight,
    key_weight,
    value_weight,
    output_weight,
    router_weight,
    expert_in,
    expert_out,
    cotangent,
    routes,
    priority,
    prefix_len,
):
    width = tokens.shape[1]
    results = layer(
        prefix_len,
        tokens,
        first_gain.reshape(1, width),
        second_gain.reshape(1, width),
        query_weight,
        key_weight,
        value_weight,
        output_weight,
        router_weight.T,
        expert_in[0],
        expert_out[0],
        cotangent,
        routes.T,
        priority,
    )
    out, gtok, gq, gk, gv, go, grouter, dsecond, dfirst, dwin, dwout = write_out(results)
    return (
        out,
        gtok,
        dfirst.reshape(width),
        dsecond.reshape(width),
        gq,
        gk,
        gv,
        go,
        grouter.T,
        dwin[None],
        dwout[None],
    )


def solution(mesh):
    in_specs = (
        P(("expert", "tensor"), None),
        P(),
        P(),
        P(None, "tensor"),
        P(None, "tensor"),
        P(None, "tensor"),
        P("tensor", None),
        P(),
        P("expert", None, "tensor"),
        P("expert", "tensor", None),
        P(("expert", "tensor"), None),
        P(("expert", "tensor"), None),
        P(("expert", "tensor"), None),
        P("expert"),
    )
    out_specs = (
        P(("expert", "tensor"), None),
        P(("expert", "tensor"), None),
        P(),
        P(),
        P(None, "tensor"),
        P(None, "tensor"),
        P(None, "tensor"),
        P("tensor", None),
        P(),
        P("expert", None, "tensor"),
        P("expert", "tensor", None),
    )
    return jax.shard_map(body, mesh=mesh, in_specs=in_specs, out_specs=out_specs, check_vma=False)
```
